32 devices in a mesh: dp: 2 (over y), psg: 4 (over z), head: 4 (over x, core).
Axes of the slice: x: 2, y: 2, z: 4, core: 2. Of those that a mesh axis runs over, the one named last changes fastest.
Arguments:
- hidden_in: bfloat16 [8, 256, 768], P(('dp', 'psg')), may hold values from -6 to 6
- encodings: bfloat16 [384, 20, 8, 768], P('head', 'psg', 'dp'), may hold values from -6 to 6
- passage_lengths: int32 [20, 8], P('psg', 'dp'), may hold values from 96 to 384
- target_lengths: int32 [8], P(('dp', 'psg')), may hold values from 32 to 256
- rel_buckets: int32 [256, 256], replicated, may hold values from 0 to 31
- gains: bfloat16 [3, 768], replicated, may hold values from 0.5 to 1.5
- rel_table: bfloat16 [32, 12], P(None, 'head'), may hold values from -5 to 5
- self_q: bfloat16 [768, 768], P(('dp', 'psg', 'head')), may hold values from -0.109375 to 0.109375
- self_k: bfloat16 [768, 768], P(('dp', 'psg', 'head')), may hold values from -0.109375 to 0.109375
- self_v: bfloat16 [768, 768], P(('dp', 'psg', 'head')), may hold values from -0.21875 to 0.21875
- self_o: bfloat16 [768, 768], P(('dp', 'psg', 'head')), may hold values from -0.875 to 0.875
- cross_q: bfloat16 [768, 768], P(('dp', 'psg', 'head')), may hold values from -0.109375 to 0.109375
- cross_k: bfloat16 [768, 768], P(('dp', 'psg', 'head')), may hold values from -0.109375 to 0.109375
- cross_v: bfloat16 [768, 768], P(('dp', 'psg', 'head')), may hold values from -0.21875 to 0.21875
- cross_o: bfloat16 [768, 768], P(('dp', 'psg', 'head')), may hold values from -3.5 to 3.5
- ff_gate: bfloat16 [768, 2048], P(('dp', 'psg', 'head')), may hold values from -0.21875 to 0.21875
- ff_up: bfloat16 [768, 2048], P(('dp', 'psg', 'head')), may hold values from -0.21875 to 0.21875
- ff_down: bfloat16 [768, 2048], P(('dp', 'psg', 'head')), may hold values from -0.125 to 0.125
- cotangent: bfloat16 [8, 256, 768], P(('dp', 'psg')), may hold values from -6 to 6
Outputs:
- out_hidden: float32 [8, 256, 768], P(('dp', 'psg'))
- d_hidden: float32 [8, 256, 768], P(('dp', 'psg'))
- d_encodings: float32 [384, 20, 8, 768], P('head', 'psg', 'dp')
- d_gains: float32 [3, 768], replicated
- d_rel_table: float32 [32, 12], P(None, 'head')
- d_self_q: float32 [768, 768], P(('dp', 'psg', 'head'))
- d_self_k: float32 [768, 768], P(('dp', 'psg', 'head'))
- d_self_v: float32 [768, 768], P(('dp', 'psg', 'head'))
- d_self_o: float32 [768, 768], P(('dp', 'psg', 'head'))
- d_cross_q: float32 [768, 768], P(('dp', 'psg', 'head'))
- d_cross_k: float32 [768, 768], P(('dp', 'psg', 'head'))
- d_cross_v: float32 [768, 768], P(('dp', 'psg', 'head'))
- d_cross_o: float32 [768, 768], P(('dp', 'psg', 'head'))
- d_ff_gate: float32 [768, 2048], P(('dp', 'psg', 'head'))
- d_ff_up: float32 [768, 2048], P(('dp', 'psg', 'head'))
- d_ff_down: float32 [768, 2048], P(('dp', 'psg', 'head'))
The draws below stay inside these ranges and needn't reach their ends.
All inputs are finite; a program needn't handle non-finite values.
Results may differ from the reference program's by a relative error of at most 0.024.
The reference program's roundings to bfloat16 on the way count: a program that leaves them out, or rounds other values in their place, can miss the bound.
Values may be sent and summed in bfloat16 or wider, within the bound.
A program may use at most 128 MiB of HBM per device.

```python
import jax
import jax.numpy as jnp
from jax import lax

D = 768
HEADS = 12
HD = 64
FF = 2048
BUCKETS = 32
PASSAGES = 20
PLEN = 384
TLEN = 256
QUERIES = 8


def place_ends(entries, key, least, largest):
    longest = entries.shape.index(max(entries.shape))
    spots = []
    for shift in (0, 1):
        where = [jax.random.randint(jax.random.fold_in(key, axis), (), 0, length) for axis, length in enumerate(entries.shape)]
        where[longest] = (where[longest] + shift) % entries.shape[longest]
        spots.append(tuple(where))
    return entries.at[spots[0]].set(least).at[spots[1]].set(largest)


def levels(rng, dims, cuts, smallest, top_value):
    level, own = 1.0, jax.random.fold_in(rng, 6)
    for axis_at, shards_of in cuts:
        steps = jnp.exp(jax.random.uniform(jax.random.fold_in(own, axis_at), (shards_of,), jnp.float32, smallest / len(cuts), top_value / len(cuts)))
        level = level * jnp.repeat(steps, dims[axis_at] // shards_of).reshape([-1 if axis == axis_at else 1 for axis in range(len(dims))])
    return level


def centred(own_key, shape, width, most, cuts=(), dtype=jnp.bfloat16):
    loudness = levels(own_key, shape, cuts, -0.22, 0.18) if cuts else 1.0
    entries = jax.random.normal(own_key, shape, jnp.float32) * width * loudness
    return jnp.minimum(jnp.maximum(entries, -most), most).astype(dtype)


def setup_inputs(seed: int = 0) -> dict:
    key_of = jax.random.split(jax.random.key(seed), 20)
    return {
        "hidden_in": centred(key_of[0], (QUERIES, TLEN, D), 1.0, 6.0, ((0, 8),)),
        "encodings": centred(key_of[1], (PLEN, PASSAGES, QUERIES, D), 1.0, 6.0, ((0, 4), (1, 4), (2, 2))),
        "passage_lengths": place_ends(jax.random.randint(key_of[2], (PASSAGES, QUERIES), PLEN // 4, PLEN + 1), jax.random.fold_in(key_of[2], 1), PLEN // 4, PLEN).astype(jnp.int32),
        "target_lengths": place_ends(jax.random.randint(key_of[3], (QUERIES,), TLEN // 8, TLEN + 1), jax.random.fold_in(key_of[3], 1), TLEN // 8, TLEN).astype(jnp.int32),
        "rel_buckets": place_ends(jax.random.randint(key_of[4], (TLEN, TLEN), 0, BUCKETS), jax.random.fold_in(key_of[4], 1), 0, BUCKETS - 1).astype(jnp.int32),
        "gains": jnp.clip(1.0 + 0.1 * jax.random.normal(key_of[5], (3, D), jnp.float32), 0.5, 1.5).astype(jnp.bfloat16),
        "rel_table": centred(key_of[6], (BUCKETS, HEADS), 1.0, 5.0, ((1, 4),)),
        "self_q": centred(key_of[7], (D, HEADS * HD), (4 * D) ** -0.5, 0.109375, ((0, 32),)),
        "self_k": centred(key_of[8], (D, HEADS * HD), (4 * D) ** -0.5, 0.109375, ((0, 32),)),
        "self_v": centred(key_of[9], (D, HEADS * HD), D ** -0.5, 0.21875, ((0, 32),)),
        "self_o": centred(key_of[10], (D, HEADS * HD), (HEADS * HD // 16) ** -0.5, 0.875, ((0, 32),)),
        "cross_q": centred(key_of[11], (D, HEADS * HD), (4 * D) ** -0.5, 0.109375, ((0, 32),)),
        "cross_k": centred(key_of[12], (D, HEADS * HD), (4 * D) ** -0.5, 0.109375, ((0, 32),)),
        "cross_v": centred(key_of[13], (D, HEADS * HD), D ** -0.5, 0.21875, ((0, 32),)),
        "cross_o": centred(key_of[14], (D, HEADS * HD), (max(2, HEADS * HD // 256)) ** -0.5, 3.5, ((0, 32),)),
        "ff_gate": centred(key_of[15], (D, FF), D ** -0.5, 0.21875, ((0, 32),)),
        "ff_up": centred(key_of[16], (D, FF), D ** -0.5, 0.21875, ((0, 32),)),
        "ff_down": centred(key_of[17], (D, FF), FF ** -0.5, 0.125, ((0, 32),)),
        "cotangent": centred(key_of[18], (QUERIES, TLEN, D), 1.0, 6.0, ((0, 8),)),
    }


EPSILON = 1e-06
NEGATIVE = -1e+30
PRECISE = lax.Precision.HIGHEST

@jax.custom_vjp
def low(v):
    return lax.optimization_barrier(v.astype(jnp.bfloat16)).astype(jnp.float32)

@jax.custom_vjp
def low_back(v):
    return v

def low_keep(v):
    return (low(v), None)

def low_pass(kept, grad):
    return (grad,)

def back_keep(v):
    return (v, None)

def back_low(kept, grad):
    return (low(grad),)
low.defvjp(low_keep, low_pass)
low_back.defvjp(back_keep, back_low)

def norm_rows(values, gain):
    return values * lax.rsqrt(lax.optimization_barrier(jnp.mean(values * values, axis=-1, keepdims=True)) + EPSILON) * gain

def product(left, right):
    return jnp.dot(left, right, precision=PRECISE, preferred_element_type=jnp.float32)

def one_query(hidden, encoded, passage_len, target_len, buckets, gain_rows, table, self_q, self_k, self_v, self_o, cross_q, cross_k, cross_v, cross_o, ff_gate, ff_up, ff_down):
    positions = jnp.arange(TLEN)
    allowed = (positions[None, :] <= positions[:, None]) & (positions[None, :] < target_len)
    normed_one = low(norm_rows(hidden, gain_rows[0]))
    query_self = low(low_back(product(normed_one, self_q))).reshape(TLEN, HEADS, HD)
    key_self = low(low_back(product(normed_one, self_k))).reshape(TLEN, HEADS, HD)
    value_self = low(low_back(product(normed_one, self_v))).reshape(TLEN, HEADS, HD)
    bias = jnp.transpose(table[buckets], (2, 0, 1))
    raw_self = low_back(jnp.einsum('ihd,jhd->hij', query_self, key_self, precision=PRECISE))
    scores_self = jnp.where(allowed[None], raw_self + bias, NEGATIVE)
    probs_self = low(jax.nn.softmax(scores_self, axis=-1))
    attn_one = jnp.einsum('hij,jhd->ihd', probs_self, value_self, precision=PRECISE)
    attn_one = low(low_back(attn_one.reshape(TLEN, HEADS * HD)))
    first = hidden + low_back(product(attn_one, self_o.T))
    normed_two = low(norm_rows(first, gain_rows[1]))
    query_cross = low(low_back(product(normed_two, cross_q))).reshape(TLEN, HEADS, HD)
    flat = encoded.reshape(PASSAGES * PLEN, D)
    key_cross = low(low_back(product(flat, cross_k))).reshape(PASSAGES * PLEN, HEADS, HD)
    value_cross = low(low_back(product(flat, cross_v))).reshape(PASSAGES * PLEN, HEADS, HD)
    live = (jnp.arange(PLEN)[None, :] < passage_len[:, None]).reshape(PASSAGES * PLEN)
    raw_cross = low_back(jnp.einsum('ihd,jhd->hij', query_cross, key_cross, precision=PRECISE))
    scores_cross = jnp.where(live[None, None, :], raw_cross, NEGATIVE)
    probs_cross = low(jax.nn.softmax(scores_cross, axis=-1))
    attn_two = jnp.einsum('hij,jhd->ihd', probs_cross, value_cross, precision=PRECISE)
    attn_two = low(low_back(attn_two.reshape(TLEN, HEADS * HD)))
    second = first + low_back(product(attn_two, cross_o.T))
    normed_three = low(norm_rows(second, gain_rows[2]))
    gate = low_back(product(normed_three, ff_gate))
    upward = low_back(product(normed_three, ff_up))
    activated = low(jax.nn.gelu(gate, approximate=True) * upward)
    output = second + low_back(product(activated, ff_down.T))
    return jnp.where((positions < target_len)[:, None], output, jnp.zeros_like(output))

def reference(hidden_in, encodings, passage_lengths, target_lengths, rel_buckets, gains, rel_table, self_q, self_k, self_v, self_o, cross_q, cross_k, cross_v, cross_o, ff_gate, ff_up, ff_down, cotangent):
    matrices = tuple((matrix.astype(jnp.float32) for matrix in (self_q, self_k, self_v, self_o, cross_q, cross_k, cross_v, cross_o, ff_gate, ff_up, ff_down)))
    enc_major = jnp.transpose(encodings.astype(jnp.float32), (2, 1, 0, 3))
    lengths_major = jnp.transpose(passage_lengths)
    stepper = jax.checkpoint(one_query)

    def forward(hidden, encoded, gain_rows, table, *weights):

        def single(item):
            return stepper(item[0], item[1], item[2], item[3], rel_buckets, gain_rows, table, *weights)
        return lax.map(single, (hidden, encoded, lengths_major, target_lengths))
    output, pull = jax.vjp(forward, hidden_in.astype(jnp.float32), enc_major, gains.astype(jnp.float32), rel_table.astype(jnp.float32), *matrices)
    grads = pull(cotangent.astype(jnp.float32))
    d_enc = jnp.transpose(grads[1], (2, 1, 0, 3))
    return (output, grads[0], d_enc, grads[2], grads[3], grads[4], grads[5], grads[6], grads[7], grads[8], grads[9], grads[10], grads[11], grads[12], grads[13], grads[14])
```

```python
import functools

import jax
import jax.numpy as jnp
from jax import lax
from jax.experimental import pallas as pl
from jax.experimental.pallas import tpu as pltpu
from jax.sharding import PartitionSpec as P

HD = 64
EPSILON = 1e-06
NEGATIVE = -1e30
AUG = 64
BF = jnp.bfloat16
F32 = jnp.float32
MESH = pl.DeviceIdType.MESH
VMEM = pltpu.VMEM


def nn(a, b):
    return lax.dot_general(a, b, (((1,), (0,)), ((), ())), preferred_element_type=F32)


def nt(a, b):
    return lax.dot_general(a, b, (((1,), (1,)), ((), ())), preferred_element_type=F32)


def tn(a, b):
    return lax.dot_general(a, b, (((0,), (0,)), ((), ())), preferred_element_type=F32)


def rms_scale(v):
    return lax.rsqrt(jnp.mean(v * v, axis=-1, keepdims=True) + EPSILON)


def rms_norm(v, gain):
    return v * rms_scale(v) * gain


def rms_back(dn, v, gain):
    r = rms_scale(v)
    gd = gain * dn
    dv = r * gd - v * (r * r * r * jnp.mean(gd * v, axis=-1, keepdims=True))
    dg = jnp.sum(dn * v * r, axis=0, keepdims=True)
    return dv, dg


def iota(shape, axis):
    return lax.broadcasted_iota(jnp.int32, shape, axis)


class Net:
    def __init__(self, send_sems, recv_sems):
        self.send_sems, self.recv_sems, self.count, self.sent = send_sems, recv_sems, 0, []

    def send(self, src, dst, **device):
        at = self.count
        self.count += 1
        copy = pltpu.make_async_remote_copy(
            src, dst, self.send_sems.at[at], self.recv_sems.at[at],
            device_id=device, device_id_type=MESH,
        )
        copy.start()
        self.sent.append(copy)
        return copy

    def finish(self):
        for copy in self.sent:
            copy.wait_send()


def enter(zs, hs, **_):
    barrier = pltpu.get_barrier_semaphore()
    d, z, h = lax.axis_index("dp"), lax.axis_index("psg"), lax.axis_index("head")
    peers = [dict(head=h ^ m) for m in (1, 2, 3)]
    peers += [dict(psg=lax.rem(z + m, 4)) for m in (1, 2, 3)]
    peers += [dict(dp=1 - d)]
    for peer in peers:
        pl.semaphore_signal(barrier, inc=1, device_id=peer, device_id_type=MESH)
    pl.semaphore_wait(barrier, len(peers))
    return d, z, h


ORDER = (1, 3, 2, 0)


class Gather:
    def __init__(self, net, buf, z, h, rows):
        self.net, self.buf, self.z, self.h, self.rows = net, buf, z, h, rows
        mine = self.at(z, h)
        self.ring = {m: net.send(mine, mine, psg=lax.rem(z + m, 4)) for m in (1, 3, 2)}
        self.hops = {0: self.on(z)}
        self.last = {}

    def at(self, zz, hh):
        return self.buf.at[zz, pl.ds(pl.multiple_of(self.rows * hh, self.rows), self.rows)]

    def on(self, zz):
        block = self.at(zz, self.h)
        return [self.net.send(block, block, head=self.h ^ 2), self.net.send(block, block, head=self.h ^ 1)]

    def source(self, m):
        return lax.rem(self.z - m + 4, 4)

    def relay(self):
        for m in (1, 3, 2):
            self.ring[m].wait_recv()
            self.hops[m] = self.on(self.source(m))
        for m in ORDER:
            self.hops[m][0].wait_recv()
            block = self.at(self.source(m), self.h ^ 2)
            self.last[m] = self.net.send(block, block, head=self.h ^ 1)

    def ready(self, m):
        self.hops[m][1].wait_recv()
        self.last[m].wait_recv()


def kernel_one(
    plen, tlen, table,
    hid, enc, buckets, gains, sq, sk, sv, so, cq, ck, cv, co, fg, fu, fd, cot,
    FB, GQ, QA, KP, VP, KT, PS, QKV, AO, FIRST, ATT, G2, DO, GC, GF, DG3, ET, OUT,
    PF, PQ, PG, AF, AQ, AG, GG, VT, QU, BIAS, AOS, OS, ST, OC, SC, OXS, SXS, OX, SX, OZS, SZS, OZ, SZ,
    OWN, SOWN, ATS, AT, N3, R3S, R3, R1S, R1, OHB,
    ss, rs,
):
    d, z, h = enter(4, 4)
    net = Net(ss, rs)
    T, D = hid.shape
    R = T // 4
    W = 3 * HD
    zp, zm, zo = lax.rem(z + 1, 4), lax.rem(z + 3, 4), lax.rem(z + 2, 4)
    hc, hx = h % 2, h // 2
    b = d * 4 + z

    f = {n: r[...].astype(F32) for n, r in dict(sq=sq, sk=sk, sv=sv, so=so, cq=cq, ck=ck, cv=cv, co=co).items()}
    F = fg.shape[1] // 4
    for g in range(4):
        s = slice(W * g, W * g + W)
        PQ[g] = jnp.concatenate([f[n][:, s] for n in ("sq", "sk", "sv")], axis=1).astype(BF)
        PF[g] = jnp.concatenate([f[n][:, s] for n in ("so", "cq", "ck", "cv", "co")], axis=1).astype(BF)
        for i, ref in enumerate((fg, fu, fd)):
            PG[g, :, F * i : F * i + F] = ref[:, F * g : F * g + F]
    a2a = {}
    for name, src, dst in (("q", PQ, AQ), ("f", PF, AF), ("g", PG, AG)):
        a2a[name] = [net.send(src.at[h ^ m], dst.at[h], head=h ^ m) for m in (1, 2, 3)]
        dst[h] = src[h]

    def assemble(name, src, dst):
        for c in a2a[name]:
            c.wait_recv()
        dst[...] = jnp.concatenate([src[j].astype(F32) for j in range(4)], axis=0).astype(BF)

    half = hid.shape[1] // 16

    class Chan:
        pass

    assemble("q", AQ, GQ.at[b])
    q1 = net.send(GQ.at[b], GQ.at[b], psg=zp)
    q2 = net.send(GQ.at[b], GQ.at[b], psg=zm)
    qy = [net.send(GQ.at[b], GQ.at[b], dp=1 - d)]
    assemble("f", AF, FB.at[h, b])

    def f_head(bb):
        return [net.send(FB.at[h, bb], FB.at[h, bb], head=h ^ 2), net.send(FB.at[h, bb], FB.at[h, bb], head=h ^ 1)]

    f1 = net.send(FB.at[h, b], FB.at[h, b], psg=zp)
    f2 = net.send(FB.at[h, b], FB.at[h, b], psg=zm)
    fy = [net.send(FB.at[h, b], FB.at[h, b], dp=1 - d)]
    fh = {0: f_head(b)}
    assemble("g", AG, GG.at[b])
    gy = net.send(GG.at[b], GG.at[b], dp=1 - d)

    g0 = gains[0:1].astype(F32)
    hidden = hid[...].astype(F32)
    n1 = rms_norm(hidden, g0).astype(BF)
    bk = buckets[...]
    for a in range(3):
        BIAS[a] = jnp.zeros((T, T), F32)

    def bias_step(i, carry):
        hit = bk == i
        for a in range(3):
            BIAS[a] = jnp.where(hit, table[i, a], BIAS[a])
        return carry

    lax.fori_loop(0, table.shape[0], bias_step, 0)

    def flip(q, carry):
        ET[q] = enc[q].astype(F32).T.astype(BF)
        return carry

    lax.fori_loop(0, 4, flip, 0)

    bm, bp, bo = d * 4 + zm, d * 4 + zp, d * 4 + zo
    lo, hi = pl.ds(0, half), pl.ds(half, half)

    q1.wait_recv()
    q3 = net.send(GQ.at[bm, lo], GQ.at[bm, lo], psg=zp)
    qy.append(net.send(GQ.at[bm], GQ.at[bm], dp=1 - d))
    q2.wait_recv()
    q4 = net.send(GQ.at[bp, hi], GQ.at[bp, hi], psg=zm)
    qy.append(net.send(GQ.at[bp], GQ.at[bp], dp=1 - d))
    f1.wait_recv()
    f3 = net.send(FB.at[h, bm, lo], FB.at[h, bm, lo], psg=zp)
    fy.append(net.send(FB.at[h, bm], FB.at[h, bm], dp=1 - d))
    fh[1] = f_head(bm)
    f2.wait_recv()
    f4 = net.send(FB.at[h, bp, hi], FB.at[h, bp, hi], psg=zm)
    fy.append(net.send(FB.at[h, bp], FB.at[h, bp], dp=1 - d))
    fh[2] = f_head(bp)
    q3.wait_recv()
    q4.wait_recv()
    qy.append(net.send(GQ.at[bo], GQ.at[bo], dp=1 - d))
    f3.wait_recv()
    f4.wait_recv()
    fy.append(net.send(FB.at[h, bo], FB.at[h, bo], dp=1 - d))
    fh[3] = f_head(bo)
    gy.wait_recv()
    e = (1 - d) * 4
    gz = []
    for bb in (b, e + z):
        gz.append((net.send(GG.at[bb], GG.at[bb], psg=zp), net.send(GG.at[bb], GG.at[bb], psg=zm)))
    for c in qy:
        c.wait_recv()

    wqkv = GQ[...].reshape(D, 3 * W)
    QKV[...] = nn(n1, wqkv).astype(BF)
    for i, bb in enumerate((e + z, e + zm, e + zp, e + zo)):
        fy[i].wait_recv()
        fh[4 + i] = f_head(bb)
    qs, ks, vs = QKV[:, 0:W], QKV[:, W : 2 * W], QKV[:, 2 * W : 3 * W]
    lane = iota((T, W), 1)
    row, col = iota((T, T), 0), iota((T, T), 1)
    keep = (col <= row) & (col < tlen[0])
    acc = jnp.zeros((T, W), F32)
    zero = jnp.zeros((T, W), BF)
    for a in range(3):
        mine = (lane >= HD * a) & (lane < HD * a + HD)
        s = nt(jnp.where(mine, qs, zero), ks) + BIAS[a]
        s = jnp.where(keep, s, NEGATIVE)
        ex = jnp.exp(s - jnp.max(s, axis=-1, keepdims=True))
        p = ex / jnp.sum(ex, axis=-1, keepdims=True)
        PS[a] = p
        acc += nn(p.astype(BF), jnp.where(mine, vs, zero))
    AOS[...] = acc.astype(BF)
    ao = [net.send(AOS.at[pl.ds(pl.multiple_of(R * (h ^ m), R), R)], AO.at[h], head=h ^ m) for m in (1, 2, 3)]
    AO[h] = AOS[pl.ds(pl.multiple_of(R * h, R), R), :]

    fc = []
    for i, bb in enumerate((b, bm, bp, bo, e + z, e + zm, e + zp, e + zo)):
        fh[i][0].wait_recv()
        fc.append(net.send(FB.at[h ^ 2, bb], FB.at[h ^ 2, bb], head=h ^ 1))
    for i in range(2):
        gz[i][0].wait_recv()
        gz[i][1].wait_recv()
    gz2 = []
    for dd in (d, 1 - d):
        p1, p2 = dd * 4 + zm, dd * 4 + zp
        gz2.append(net.send(GG.at[p1, lo], GG.at[p1, lo], psg=zp))
        gz2.append(net.send(GG.at[p2, hi], GG.at[p2, hi], psg=zm))
    for i in range(8):
        fh[i][1].wait_recv()
        fc[i].wait_recv()
    for c in ao:
        c.wait_recv()

    def whole(g, i, n=1):
        return FB[g, :, :, W * i : W * (i + n)].reshape(D, n * W)

    mine_rows = pl.ds(pl.multiple_of(R * h, R), R)
    first = hid[mine_rows, :].astype(F32)
    for g in range(4):
        first += nt(AO[g], whole(g, 0))
    FIRST[...] = first
    n2 = rms_norm(first, gains[1:2].astype(F32)).astype(BF)
    QA[z, mine_rows, :] = jnp.concatenate([nn(n2, whole(g, 1)) for g in range(4)], axis=1).astype(BF)

    spreadq = Gather(net, QA, z, h, R)

    tok = enc.shape[1]
    krow, klane = iota((tok, AUG), 0), iota((tok, AUG), 1)
    per = 96
    npass = plen.shape[0]
    vaug = jnp.where(klane < 9, -1.0, 0.0).astype(F32)

    def project(q, carry):
        dead = krow >= per * npass
        for p in range(npass):
            inside = (krow >= per * p) & (krow < per * p + per)
            dead = dead | (inside & (krow - per * p + per * h >= plen[p, q]))
        kaug = jnp.where(klane == 9, jnp.where(dead, NEGATIVE, 0.0), vaug)

        def group(g, c2):
            kv = nn(enc[q], FB[g, :, :, 2 * W : 4 * W].reshape(D, 2 * W))
            k, v = kv[:, :W], kv[:, W:]
            KP[q, g] = jnp.concatenate([k, kaug], axis=1).astype(BF)
            VP[q, g] = jnp.concatenate([v, vaug], axis=1).astype(BF)
            KT[q, g] = k.T.astype(BF)
            VT[q, g] = v.T.astype(BF)
            return c2

        return lax.fori_loop(0, 4, group, carry)

    lax.fori_loop(0, 4, project, 0)
    spreadq.relay()

    qaug = jnp.where(iota((T, AUG), 1) == 9, 1.0, 0.0).astype(BF)

    def weights(m1, l1, m2, l2):
        top = jnp.maximum(m1, m2)
        w1, w2 = l1 * jnp.exp(m1 - top), l2 * jnp.exp(m2 - top)
        return top, w1 + w2, w1, w2

    def spread(x):
        return jnp.concatenate([jnp.broadcast_to(x[a : a + 1], (HD, T)) for a in range(3)], axis=0)

    def join(o1, s1, o2, s2):
        top, tot, w1, w2 = weights(s1[0:3], s1[3:6], s2[0:3], s2[3:6])
        o = o1 * spread(w1 / tot) + o2 * spread(w2 / tot)
        return o, jnp.concatenate([top, tot, jnp.zeros((2, T), F32)], axis=0)

    def attend(i, zz):
        for g in range(4):
            QU[g] = QA[zz, :, W * g : W * g + W]

        def group(g, carry):
            qg, kg = QU[g], KP[zz, g]
            outs, tops, tots = [], [], []
            for a in range(3):
                mine = (lane >= HD * a) & (lane < HD * a + HD)
                qm = jnp.concatenate([jnp.where(mine, qg, zero), qaug], axis=1)
                s = nt(kg, qm)
                m = jnp.max(s, axis=0, keepdims=True)
                ex = jnp.exp(s - m)
                l = jnp.sum(ex, axis=0, keepdims=True)
                o = nn(VT[zz, g, HD * a : HD * a + HD, :], ex.astype(BF))
                outs.append(o / l)
                tops.append(m)
                tots.append(l)
            gc, gx = g % 2, g // 2
            OS[i, gc, gx] = jnp.concatenate(outs, axis=0).astype(BF)
            ST[i, gc, gx] = jnp.concatenate(tops + tots + [jnp.zeros((2, T), F32)], axis=0)
            return carry

        lax.fori_loop(0, 4, group, 0)

    to_core, to_x, to_z = {}, {}, {}

    def core_stage(i):
        to_core[i] = (net.send(OS.at[i, 1 - hc], OC.at[i], head=h ^ 1), net.send(ST.at[i, 1 - hc], SC.at[i], head=h ^ 1))

    def x_stage(i):
        for c in to_core[i]:
            c.wait_recv()
        o, s = join(OS[i, hc, 1 - hx].astype(F32), ST[i, hc, 1 - hx], OC[i, 1 - hx].astype(F32), SC[i, 1 - hx])
        OXS[i] = o.astype(BF)
        SXS[i] = s
        to_x[i] = (net.send(OXS.at[i], OX.at[i], head=h ^ 2), net.send(SXS.at[i], SX.at[i], head=h ^ 2))
        o, s = join(OS[i, hc, hx].astype(F32), ST[i, hc, hx], OC[i, hx].astype(F32), SC[i, hx])
        OWN[i] = o
        SOWN[i] = s

    def z_stage(i):
        for c in to_x[i]:
            c.wait_recv()
        o, s = join(OWN[i], SOWN[i], OX[i].astype(F32), SX[i])
        if i < 3:
            m = ORDER[i]
            OZS[i] = o.astype(BF)
            SZS[i] = s
            to = lax.rem(z - m + 4, 4)
            to_z[i] = (net.send(OZS.at[i], OZ.at[i], psg=to), net.send(SZS.at[i], SZ.at[i], psg=to))
        else:
            OWN[i] = o
            SOWN[i] = s

    for i, m in enumerate(ORDER):
        zz = lax.rem(z - m + 4, 4)
        spreadq.ready(m)
        attend(i, zz)
        core_stage(i)
        if i >= 1:
            x_stage(i - 1)
        if i >= 2:
            z_stage(i - 2)
    x_stage(3)
    z_stage(2)
    z_stage(3)
    o, s = OWN[3], SOWN[3]
    for i in range(3):
        for c in to_z[i]:
            c.wait_recv()
        o, s = join(o, s, OZ[i].astype(F32), SZ[i])
    lse = s[0:3] + jnp.log(s[3:6])
    full = jnp.concatenate([o, lse, jnp.zeros((AUG - 3, T), F32)], axis=0)
    ATS[...] = full.T
    at = [net.send(ATS.at[pl.ds(pl.multiple_of(R * (h ^ m), R), R)], AT.at[h], head=h ^ m) for m in (1, 2, 3)]
    AT[h] = ATS[mine_rows, :]
    for c in gz2:
        c.wait_recv()
    for c in at:
        c.wait_recv()
    second = FIRST[...]
    for g in range(4):
        low = AT[g, :, 0:W].astype(BF)
        ATT[g] = low
        second += nt(low, whole(g, 4))
    g2gain = gains[2:3].astype(F32)
    N3[mine_rows, :] = rms_norm(second, g2gain).astype(BF)
    n3c = [net.send(N3.at[mine_rows], N3.at[mine_rows], head=h ^ m) for m in (2, 3, 1)]
    rowid = iota((T, 1), 0)
    go_low = jnp.where(rowid < tlen[0], cot[...], jnp.zeros((T, D), BF))
    wdown = GG[:, :, 2 * F : 3 * F].reshape(D, F)
    wgu = GG[:, :, 0 : 2 * F].reshape(D, 2 * F)
    d_act = nn(go_low, wdown)
    for c in n3c:
        c.wait_recv()
    n3 = N3[...]
    gate_up = nn(n3, wgu)
    gate, up = gate_up[:, :F], gate_up[:, F:]
    c0 = 0.7978845608028654
    inner = c0 * (gate + 0.044715 * gate * gate * gate)
    th = jnp.tanh(inner)
    gel = 0.5 * gate * (1.0 + th)
    act = (gel * up).astype(BF)
    dgel = 0.5 * (1.0 + th) + 0.5 * gate * (1.0 - th * th) * (c0 * (1.0 + 3 * 0.044715 * gate * gate))
    dgu = jnp.concatenate([d_act * up * dgel, d_act * gel], axis=1).astype(BF)
    R3S[...] = nt(dgu, wgu).astype(BF)
    r3 = [net.send(R3S.at[pl.ds(pl.multiple_of(R * (h ^ m), R), R)], R3.at[h], head=h ^ m) for m in (2, 3, 1)]
    R1S[...] = nt(act, wdown).astype(BF)
    r1 = [net.send(R1S.at[pl.ds(pl.multiple_of(R * (h ^ m), R), R)], R1.at[h], head=h ^ m) for m in (2, 3, 1)]
    R3[h] = R3S[mine_rows, :]
    R1[h] = R1S[mine_rows, :]
    GF[:, :, 2 * F : 3 * F] = tn(go_low, act).astype(BF).reshape(8, D // 8, F)
    GF[:, :, 0 : 2 * F] = tn(n3, dgu).astype(BF).reshape(8, D // 8, 2 * F)
    for c in r3:
        c.wait_recv()
    dn3 = R3[0].astype(F32) + R3[1].astype(F32) + R3[2].astype(F32) + R3[3].astype(F32)
    live = (iota((R, 1), 0) + R * h) < tlen[0]
    go = jnp.where(live, cot[mine_rows, :].astype(F32), 0.0)
    dv, dg = rms_back(dn3, second, g2gain)
    DG3[...] = jnp.concatenate([dg, jnp.zeros((7, D), F32)], axis=0)
    g2 = go + dv
    G2[...] = g2
    g2_low = g2.astype(BF)
    alane = iota((R, 2 * AUG), 1)
    wl = iota((R, W), 1)
    aug = jnp.zeros((R, 2 * AUG), F32)
    dos = []

    def parts(x):
        hi_ = x.astype(BF).astype(F32)
        mid = (x - hi_).astype(BF).astype(F32)
        return hi_, mid, x - hi_ - mid

    for g in range(4):
        do = nn(g2_low, whole(g, 4)).astype(BF)
        dos.append(do.astype(F32))
        GC[g % 2, g // 2] = tn(g2_low, ATT[g]).astype(BF)
        prod = do.astype(F32) * AT[g, :, 0:W]
        for a in range(3):
            delta = jnp.sum(jnp.where((wl >= HD * a) & (wl < HD * a + HD), prod, 0.0), axis=1, keepdims=True)
            for off, val in ((0, AT[g, :, W + a : W + a + 1]), (AUG, delta)):
                for j, part in enumerate(parts(val)):
                    aug = jnp.where(alane == off + 9 * g + 3 * a + j, part, aug)
    DO[...] = jnp.concatenate(dos + [aug], axis=1).astype(BF)
    for c in r1:
        c.wait_recv()
    out = second + R1[0].astype(F32) + R1[1].astype(F32) + R1[2].astype(F32) + R1[3].astype(F32)
    OUT[mine_rows, :] = jnp.where(live, out, 0.0)
    oh = [net.send(OUT.at[mine_rows], OUT.at[mine_rows], head=h ^ m) for m in (2, 3, 1)]
    for c in oh:
        c.wait_recv()
    net.finish()


def call_one(plen, tlen, table, hid, enc, buckets, gains, mats, cot):
    T, D = hid.shape
    R = T // 4
    W = 3 * HD
    rows = mats[0].shape[0]
    F = mats[8].shape[1] // 4
    tok = enc.shape[1]
    S = jax.ShapeDtypeStruct
    outs = dict(
        FB=((4, 8, 4 * rows, 5 * W), BF), GQ=((8, 4 * rows, 3 * W), BF), QA=((4, T, D), BF),
        KP=((4, 4, tok, W + AUG), BF), VP=((4, 4, tok, W + AUG), BF), KT=((4, 4, W, tok), BF),
        PS=((3, T, T), F32), QKV=((T, 3 * W), BF), AO=((4, R, W), BF), FIRST=((R, D), F32),
        ATT=((4, R, W), BF), G2=((R, D), F32), DO=((R, D + 2 * AUG), BF), GC=((2, 2, D, W), BF),
        GF=((8, D // 8, 3 * F), BF), DG3=((8, D), F32), ET=((4, D, tok), BF), OUT=((T, D), F32),
    )
    scratch = [
        VMEM((4, rows, 5 * W), BF), VMEM((4, rows, 3 * W), BF), VMEM((4, rows, 3 * F), BF),
        VMEM((4, rows, 5 * W), BF), VMEM((4, rows, 3 * W), BF), VMEM((4, rows, 3 * F), BF),
        VMEM((8, 4 * rows, 3 * F), BF),
        VMEM((4, 4, W, tok), BF), VMEM((4, T, W), BF), VMEM((3, T, T), F32), VMEM((T, W), BF),
        VMEM((4, 2, 2, W, T), BF), VMEM((4, 2, 2, 8, T), F32),
        VMEM((4, 2, W, T), BF), VMEM((4, 2, 8, T), F32),
        VMEM((4, W, T), BF), VMEM((4, 8, T), F32), VMEM((4, W, T), BF), VMEM((4, 8, T), F32),
        VMEM((3, W, T), BF), VMEM((3, 8, T), F32), VMEM((3, W, T), BF), VMEM((3, 8, T), F32),
        VMEM((4, W, T), F32), VMEM((4, 8, T), F32),
        VMEM((T, W + AUG), F32), VMEM((4, R, W + AUG), F32), VMEM((T, D), BF),
        VMEM((T, D), BF), VMEM((4, R, D), BF), VMEM((T, D), BF), VMEM((4, R, D), BF), VMEM((8, 128), F32),
        pltpu.SemaphoreType.DMA((150,)), pltpu.SemaphoreType.DMA((150,)),
    ]
    smem = pl.BlockSpec(memory_space=pltpu.SMEM)
    vm = pl.BlockSpec(memory_space=pltpu.VMEM)
    res = pl.pallas_call(
        kernel_one,
        out_shape=[S(*v) for v in outs.values()],
        in_specs=[smem] * 3 + [vm] * 16,
        out_specs=[vm] * len(outs),
        scratch_shapes=scratch,
        name="forward",
        compiler_params=pltpu.CompilerParams(collective_id=1, has_side_effects=True, vmem_limit_bytes=63 << 20),
    )(plen, tlen, table, hid, enc, buckets, gains, *mats, cot)
    return dict(zip(outs, res))


class Scatter:
    def __init__(self, net, d, z, h, src, own, yr, zr, as_, ar):
        self.__dict__.update(locals())

    def y(self):
        d = self.d
        self.cy = self.net.send(self.src.at[pl.ds((1 - d) * 4, 4)], self.yr, dp=1 - d)

    def ring(self):
        self.cy.wait_recv()
        z = self.z
        self.yr[...] = (self.own().astype(F32) + self.yr[...].astype(F32)).astype(BF)
        self.cz = []
        for m in (1, 3, 2):
            to = lax.rem(z + m, 4)
            self.cz.append(self.net.send(self.yr.at[to], self.zr.at[m - 1], psg=to))

    def heads(self):
        for c in self.cz:
            c.wait_recv()
        total = self.yr[self.z].astype(F32)
        for m in range(3):
            total += self.zr[m].astype(F32)
        self.as_[...] = total
        n = self.ar.shape[1]
        h = self.h
        self.ch = [
            self.net.send(self.as_.at[pl.ds(pl.multiple_of(n * (h ^ m), n), n)], self.ar.at[h], head=h ^ m)
            for m in (2, 3, 1)
        ]
        self.ar[h] = self.as_[pl.ds(pl.multiple_of(n * h, n), n), :]

    def done(self):
        for c in self.ch:
            c.wait_recv()


class Quarter:
    def __init__(self, net, h, far, own, cr, xr):
        self.net, self.h, self.far, self.own, self.cr, self.xr = net, h, far, own, cr, xr
        self.hc, self.hx = h % 2, h // 2

    def core(self):
        self.cc = self.net.send(self.far.at[1 - self.hc], self.cr, head=self.h ^ 1)

    def x(self):
        self.cc.wait_recv()
        out = 1 - self.hx
        self.cr[out] = (self.own(out).astype(F32) + self.cr[out].astype(F32)).astype(BF)
        self.cx = self.net.send(self.cr.at[out], self.xr, head=self.h ^ 2)

    def total(self):
        self.cx.wait_recv()
        hx = self.hx
        return self.own(hx).astype(F32) + self.cr[hx].astype(F32) + self.xr[...].astype(F32)


def kernel_two(
    buckets, gains, hid, ETH, FB, GQ, QA, KPH, VPH, KTH, PS, QKV, AO, FIRST, G2, DO, GC, GF, DG3,
    DENC, DHID, SM, OCO, OF, OM, OL,
    DOB, KP, VP, KT, QAV, ET, QU, DU, QX, DX, DQG, DKV, DQS, DQC, DXR, DOWN, DZS, DZR, DAS, DA, DSF, TBL, NS, NR, DEN,
    GCV, CCR, CXR, CSRC, CYR, CZR, CAS,
    GFV, FYR, FZR, FAS,
    MOWN, MCR, MXR, MSRC, MYR, MZR, MAS,
    LOWN, LCR, LXR, LSRC, LYR, LZR, LAS,
    SMR,
    ss, rs, ls, es,
):
    d, z, h = enter(4, 4)
    net = Net(ss, rs)
    T, D = hid.shape
    R = T // 4
    W = 3 * HD
    hc, hx = h % 2, h // 2
    tok = ETH.shape[2]
    mine_rows = pl.ds(pl.multiple_of(R * h, R), R)

    def source(m):
        return lax.rem(z - m + 4, 4)

    def fetch(i):
        zz, slot = source(ORDER[i]), i % 2
        cs = [pltpu.make_async_copy(a.at[zz], b.at[slot], ls.at[j, slot]) for j, (a, b) in enumerate(((KPH, KP), (VPH, VP), (KTH, KT), (QA, QAV)))]
        for c in cs:
            c.start()
        return cs

    fetched = fetch(0)
    DOB[z, mine_rows, :] = DO[...]
    gather = Gather(net, DOB, z, h, R)
    near = [
        pltpu.make_async_copy(GC.at[hc], GCV, es.at[0]),
        pltpu.make_async_copy(GF.at[pl.ds(d * 4, 4)], GFV, es.at[1]),
    ]
    for c in near:
        c.start()

    def half_of(ref):
        return lambda: ref[pl.ds(d * 4, 4)]

    def part_of(ref):
        return lambda j: ref[hc, j]

    ff = Scatter(net, d, z, h, GF, lambda: GFV[...], FYR, FZR, FAS, OF)
    co = Quarter(net, h, GC, lambda j: GCV[j], CCR, CXR)
    cos = Scatter(net, d, z, h, CSRC, half_of(CSRC), CYR, CZR, CAS, OCO)
    mid = Quarter(net, h, MOWN, part_of(MOWN), MCR, MXR)
    mids = Scatter(net, d, z, h, MSRC, half_of(MSRC), MYR, MZR, MAS, OM)
    lat = Quarter(net, h, LOWN, part_of(LOWN), LCR, LXR)
    lats = Scatter(net, d, z, h, LSRC, half_of(LSRC), LYR, LZR, LAS, OL)
    gather.relay()
    for c in near:
        c.wait()
    co.core()
    ff.y()

    lane = iota((T, W), 1)
    alane = iota((T, AUG), 1)
    zero = jnp.zeros((T, W), BF)
    azero = jnp.zeros((T, AUG), BF)
    one = jnp.ones((T, 1), F32)
    pad = jnp.zeros((T, AUG - 10), F32)

    def mine_of(a):
        return (lane >= HD * a) & (lane < HD * a + HD)

    def whole(g, i, n=1):
        return FB[g, :, :, W * i : W * (i + n)].reshape(D, n * W)

    def attend(i, zz):
        slot = i % 2
        ex = DOB[zz, :, D : D + 2 * AUG].astype(F32)
        for g in range(4):
            QU[g] = QAV[slot, :, W * g : W * g + W]
            DU[g] = DOB[zz, :, W * g : W * g + W]
            QX[g] = jnp.concatenate([ex[:, 9 * g : 9 * g + 9], one, pad], axis=1).astype(BF)
            DX[g] = jnp.concatenate([ex[:, AUG + 9 * g : AUG + 9 * g + 9], one * 0, pad], axis=1).astype(BF)

        def group(g, carry):
            kg, vg = KP[slot, g], VP[slot, g]
            dk = jnp.zeros((tok, W + AUG), F32)
            dv = jnp.zeros((tok, W + AUG), F32)
            dqs = []
            for a in range(3):
                keep = (alane == 9) | ((alane >= 3 * a) & (alane < 3 * a + 3))
                qm = jnp.concatenate([jnp.where(mine_of(a), QU[g], zero), jnp.where(keep, QX[g], azero)], axis=1)
                dm = jnp.concatenate([jnp.where(mine_of(a), DU[g], zero), jnp.where(keep, DX[g], azero)], axis=1)
                p = jnp.exp(nt(kg, qm))
                ds = (p * nt(vg, dm)).astype(BF)
                dqs.append(nn(KT[slot, g, HD * a : HD * a + HD, :], ds))
                dk += nn(ds, qm)
                dv += nn(p.astype(BF), dm)
            DKV[zz, g] = jnp.concatenate([dk[:, :W], dv[:, :W]], axis=1).astype(BF)
            DQG[g] = jnp.concatenate(dqs, axis=0).T.astype(BF)
            return carry

        lax.fori_loop(0, 4, group, 0)
        dq = jnp.concatenate([DQG[g] for g in range(4)], axis=1)
        for j in range(4):
            DQS[i, j % 2, j // 2] = dq[R * j : R * j + R]

    to_core, to_x, to_z = {}, {}, {}

    def core_stage(i):
        to_core[i] = net.send(DQS.at[i, 1 - hc], DQC.at[i], head=h ^ 1)

    def x_stage(i):
        to_core[i].wait_recv()
        DQC[i, 1 - hx] = (DQS[i, hc, 1 - hx].astype(F32) + DQC[i, 1 - hx].astype(F32)).astype(BF)
        to_x[i] = net.send(DQC.at[i, 1 - hx], DXR.at[i], head=h ^ 2)
        DOWN[i] = DQS[i, hc, hx].astype(F32) + DQC[i, hx].astype(F32)

    def z_stage(i):
        to_x[i].wait_recv()
        o = DOWN[i] + DXR[i].astype(F32)
        if i < 3:
            DZS[i] = o.astype(BF)
            to_z[i] = net.send(DZS.at[i], DZR.at[i], psg=source(ORDER[i]))
        else:
            DOWN[i] = o

    for i, m in enumerate(ORDER):
        gather.ready(m)
        for c in fetched:
            c.wait()
        if i < 3:
            fetched = fetch(i + 1)
        attend(i, source(m))
        core_stage(i)
        if i >= 1:
            x_stage(i - 1)
        if i >= 2:
            z_stage(i - 2)
        if i == 0:
            co.x()
            ff.ring()
        if i == 1:
            CSRC[...] = co.total().astype(BF).reshape(CSRC.shape)
            cos.y()
            ff.heads()
        if i == 2:
            cos.ring()
    x_stage(3)
    z_stage(2)
    z_stage(3)
    cos.heads()
    dq = DOWN[3]
    for i in range(3):
        to_z[i].wait_recv()
        dq += DZR[i].astype(F32)
    dq_low = dq.astype(BF)

    def et_copy(n):
        return pltpu.make_async_copy(ETH.at[n % 4], ET.at[n % 2], ls.at[4, n % 2])

    et_copy(0).start()

    first = FIRST[...]
    gain = gains[1:2].astype(F32)
    n2 = rms_norm(first, gain).astype(BF)
    dn2 = jnp.zeros((R, D), F32)
    for g in range(4):
        dqg = dq_low[:, W * g : W * g + W]
        dn2 += nt(dqg, whole(g, 1))
    dv, dg2 = rms_back(dn2, first, gain)
    g1 = G2[...] + dv
    g1_low = g1.astype(BF)
    for g in range(4):
        DAS[g] = nn(g1_low, whole(g, 0)).astype(BF)
    das = [net.send(DAS.at[h ^ m], DA.at[h], head=h ^ m) for m in (2, 3, 1)]
    DA[h] = DAS[h]

    for g in range(4):
        MOWN[g % 2, g // 2, :, 0:W] = tn(n2, dq_low[:, W * g : W * g + W]).astype(BF)
        acc = jnp.zeros((D, 2 * W), F32)
        for q in range(4):
            et_copy(4 * g + q).wait()
            if 4 * g + q < 15:
                et_copy(4 * g + q + 1).start()
            acc += nn(ET[q % 2], DKV[q, g])
        MOWN[g % 2, g // 2, :, W : 3 * W] = acc.astype(BF)
        LOWN[g % 2, g // 2] = tn(g1_low, AO[g]).astype(BF)
    mid.core()
    lat.core()
    for c in das:
        c.wait_recv()

    da = DA[...].reshape(T, W)
    qs, ks, vs = QKV[:, 0:W], QKV[:, W : 2 * W], QKV[:, 2 * W : 3 * W]
    dq1 = jnp.zeros((T, W), F32)
    dk1 = jnp.zeros((T, W), F32)
    dv1 = jnp.zeros((T, W), F32)
    for a in range(3):
        mine = mine_of(a)
        dam = jnp.where(mine, da, zero)
        p = PS[a]
        dp = nt(dam, vs)
        ds = p * (dp - jnp.sum(p * dp, axis=-1, keepdims=True))
        DSF[a] = ds
        dsl = ds.astype(BF)
        dq1 += nn(dsl, jnp.where(mine, ks, zero))
        dk1 += tn(dsl, jnp.where(mine, qs, zero))
        dv1 += tn(p.astype(BF), dam)
    dqkv = jnp.concatenate([dq1, dk1, dv1], axis=1).astype(BF)
    wqkv = GQ[...].reshape(D, 3 * W)
    NS[...] = nt(dqkv, wqkv).astype(BF)
    nr = [net.send(NS.at[pl.ds(pl.multiple_of(R * (h ^ m), R), R)], NR.at[h], head=h ^ m) for m in (2, 3, 1)]
    NR[h] = NS[mine_rows, :]
    mid.x()
    lat.x()
    g0 = gains[0:1].astype(F32)
    n1 = rms_norm(hid[...].astype(F32), g0).astype(BF)
    gqkv = tn(n1, dqkv)
    LSRC[...] = jnp.concatenate([lat.total(), gqkv], axis=1).astype(BF).reshape(LSRC.shape)
    lats.y()
    for c in nr:
        c.wait_recv()
    dn1 = NR[0].astype(F32) + NR[1].astype(F32) + NR[2].astype(F32) + NR[3].astype(F32)
    dv, dg1 = rms_back(dn1, hid[mine_rows, :].astype(F32), g0)
    DHID[mine_rows, :] = g1 + dv
    dh = [net.send(DHID.at[mine_rows], DHID.at[mine_rows], head=h ^ m) for m in (2, 3, 1)]
    MSRC[...] = mid.total().astype(BF).reshape(MSRC.shape)
    mids.y()
    lats.ring()

    bk = buckets[...]

    def table_step(i, carry):
        hit = bk == i
        for a in range(3):
            TBL[a, pl.ds(i, 1), :] = jnp.sum(jnp.where(hit, DSF[a], 0.0), axis=0, keepdims=True)
        return carry

    nb = TBL.shape[1]
    lax.fori_loop(0, nb, table_step, 0)
    tl = iota((nb, 128), 1)
    tab = jnp.zeros((nb, 128), F32)
    for a in range(3):
        tab = jnp.where(tl == a, jnp.sum(TBL[a], axis=1, keepdims=True), tab)
    tab = jnp.concatenate([tab, jnp.zeros((128 - nb, 128), F32)], axis=0).T[0:8]
    tab = jnp.concatenate([tab, jnp.zeros((8, D - 128), F32)], axis=1)
    dgs = jnp.concatenate([dg1, dg2, DG3[0:1], jnp.zeros((5, D), F32)], axis=0)
    SM[0] = jnp.concatenate([dgs, tab], axis=0)
    srow = iota((16, D), 0)

    def small(j, shared, **dev):
        c = net.send(SM.at[j], SMR.at[j], **dev)
        return c, shared

    def small_end(j, cs):
        c, shared = cs
        c.wait_recv()
        got = SMR[j]
        SM[j + 1] = SM[j] + (got if shared else jnp.where(srow < 8, got, 0.0))

    cs = small(0, False, head=h ^ 1)

    step = DEN.shape[1]
    per = tok // step

    def den_copy(n):
        rows = pl.ds(pl.multiple_of(lax.rem(n, per) * step, step), step)
        return pltpu.make_async_copy(DEN.at[lax.rem(n, 2)], DENC.at[n // per, rows], es.at[lax.rem(n, 2)])

    def denc(n, carry):
        rows = pl.ds(pl.multiple_of(lax.rem(n, per) * step, step), step)

        @pl.when(n >= 2)
        def _():
            den_copy(n - 2).wait()

        acc = nt(DKV[n // per, 0, rows, :], whole(0, 2, 2))
        for g in range(1, 4):
            acc += nt(DKV[n // per, g, rows, :], whole(g, 2, 2))
        DEN[lax.rem(n, 2)] = acc
        den_copy(n).start()
        return carry

    lax.fori_loop(0, 2 * per, denc, 0)
    small_end(0, cs)
    cs = small(1, False, head=h ^ 2)
    mids.ring()
    lats.heads()
    lax.fori_loop(2 * per, 4 * per, denc, 0)
    small_end(1, cs)
    cs = small(2, True, dp=1 - d)
    mids.heads()
    small_end(2, cs)
    cs = small(3, True, psg=z ^ 1)
    small_end(3, cs)
    cs = small(4, True, psg=z ^ 2)
    for n in (4 * per - 2, 4 * per - 1):
        den_copy(n).wait()
    small_end(4, cs)
    for s in (ff, cos, mids, lats):
        s.done()
    for c in dh:
        c.wait_recv()
    net.finish()


def call_two(buckets, gains, hid, kept, rows):
    T, D = hid.shape
    R = T // 4
    W = 3 * HD
    k = kept
    tok = k["ET"].shape[2]
    F3 = k["GF"].shape[2]
    S = jax.ShapeDtypeStruct
    blk = D // 8
    outs = dict(
        DENC=((4, tok, D), F32), DHID=((T, D), F32), SM=((6, 16, D), F32),
        OCO=((4, rows, W), F32), OF=((4, rows, F3), F32), OM=((4, rows, 3 * W), F32), OL=((4, rows, 4 * W), F32),
    )

    def quarter(w):
        return [VMEM((2, D, w), BF), VMEM((D, w), BF)]

    def scatter(w):
        return [VMEM((4, blk, w), BF), VMEM((3, blk, w), BF), VMEM((blk, w), F32)]

    scratch = [
        VMEM((4, T, D + 2 * AUG), BF), VMEM((2, 4, tok, W + AUG), BF), VMEM((2, 4, tok, W + AUG), BF), VMEM((2, 4, W, tok), BF), VMEM((2, T, D), BF), VMEM((2, D, tok), BF),
        VMEM((4, T, W), BF), VMEM((4, T, W), BF), VMEM((4, T, AUG), BF), VMEM((4, T, AUG), BF),
        VMEM((4, T, W), BF), VMEM((4, 4, tok, 2 * W), BF),
        VMEM((4, 2, 2, R, D), BF), VMEM((4, 2, R, D), BF), VMEM((4, R, D), BF), VMEM((4, R, D), F32),
        VMEM((3, R, D), BF), VMEM((3, R, D), BF), VMEM((4, R, W), BF), VMEM((4, R, W), BF),
        VMEM((3, T, T), F32), VMEM((3, 32, T), F32), VMEM((T, D), BF), VMEM((4, R, D), BF), VMEM((2, tok // 2, D), F32),
        VMEM((2, D, W), BF), *quarter(W), VMEM((8, blk, W), BF), *scatter(W),
        VMEM((4, blk, F3), BF), *scatter(F3),
        VMEM((2, 2, D, 3 * W), BF), *quarter(3 * W), VMEM((8, blk, 3 * W), BF), *scatter(3 * W),
        VMEM((2, 2, D, W), BF), *quarter(W), VMEM((8, blk, 4 * W), BF), *scatter(4 * W),
        VMEM((5, 16, D), F32),
        pltpu.SemaphoreType.DMA((120,)), pltpu.SemaphoreType.DMA((120,)), pltpu.SemaphoreType.DMA((5, 2)), pltpu.SemaphoreType.DMA((2,)),
    ]
    vm = pl.BlockSpec(memory_space=pltpu.VMEM)
    anym = pl.BlockSpec(memory_space=pl.ANY)
    names = ("ET", "FB", "GQ", "QA", "KP", "VP", "KT", "PS", "QKV", "AO", "FIRST", "G2", "DO", "GC", "GF", "DG3")
    res = pl.pallas_call(
        kernel_two,
        out_shape=[S(*v) for v in outs.values()],
        in_specs=[vm] * 3 + [anym if n in ("ET", "KP", "VP", "KT", "QA", "GC", "GF") else vm for n in names],
        out_specs=[anym] + [vm] * (len(outs) - 1),
        scratch_shapes=scratch,
        name="backward",
        compiler_params=pltpu.CompilerParams(collective_id=2, has_side_effects=True, vmem_limit_bytes=63 << 20),
    )(buckets, gains, hid, *[k[n] for n in names])
    return dict(zip(outs, res))


def local_fast(
    hidden_in, encodings, passage_lengths, target_lengths, rel_buckets, gains, rel_table, *rest
):
    mats, cot = rest[:11], rest[11]
    span, passages, group, D = encodings.shape
    rows = mats[0].shape[0]
    W = 3 * HD
    F = mats[8].shape[1] // 4
    count = span * passages
    padded = -(-count // 128) * 128
    enc = jnp.transpose(encodings, (2, 1, 0, 3)).reshape(group, count, D)
    enc = jnp.pad(enc, ((0, 0), (0, padded - count), (0, 0)))
    hid = hidden_in[0]
    kept = call_one(
        passage_lengths, target_lengths, rel_table.astype(F32), hid, enc, rel_buckets, gains, mats, cot[0]
    )
    r = call_two(rel_buckets, gains, hid, kept, rows)
    d_enc = jnp.transpose(r["DENC"][:, :count].reshape(group, passages, span, D), (2, 1, 0, 3))

    def columns(a, at, w):
        return jnp.transpose(a[:, :, at : at + w], (1, 0, 2)).reshape(rows, 4 * w)

    small = r["SM"][5]
    OM, OL, OF = r["OM"], r["OL"], r["OF"]
    return (
        kept["OUT"][None], r["DHID"][None], d_enc, small[0:3],
        jnp.transpose(small[8:11, : rel_table.shape[0]]),
        columns(OL, W, W), columns(OL, 2 * W, W), columns(OL, 3 * W, W), columns(OL, 0, W),
        columns(OM, 0, W), columns(OM, W, W), columns(OM, 2 * W, W), columns(r["OCO"], 0, W),
        columns(OF, 0, F), columns(OF, F, F), columns(OF, 2 * F, F),
    )


def merged(part, axis, combine):
    gathered = jax.tree.map(lambda a: lax.all_gather(a, axis), part)

    def take(source):
        return jax.tree.map(lambda a: lax.dynamic_index_in_dim(a, source, 0, False), gathered)

    return lax.fori_loop(
        1, lax.axis_size(axis), lambda source, state: combine(state, take(source)), take(0)
    )


def rms_plain(values, gain):
    return values * lax.rsqrt(jnp.mean(values * values, axis=-1, keepdims=True) + EPSILON) * gain


def gated(gate_in, up_in):
    return jax.nn.gelu(gate_in, approximate=True) * up_in


def over_heads(partial_value):
    return lax.psum(partial_value, "head")


def own_columns(matrix, index, width):
    return lax.dynamic_slice_in_dim(matrix, index * width, width, 1)


def left_mul(left, matrix):
    return jnp.einsum("qtd,dc->qtc", left, matrix, preferred_element_type=jnp.float32)


def right_mul(left, matrix):
    return jnp.einsum("qtc,dc->qtd", left, matrix, preferred_element_type=jnp.float32)


def row_outer(left, right):
    return jnp.einsum("qtd,qtc->dc", left, right, preferred_element_type=jnp.float32)


def local_plain(
    hidden_in,
    encodings,
    passage_lengths,
    target_lengths,
    rel_buckets,
    gains,
    rel_table,
    self_q,
    self_k,
    self_v,
    self_o,
    cross_q,
    cross_k,
    cross_v,
    cross_o,
    ff_gate,
    ff_up,
    ff_down,
    cotangent,
):
    gathered = (
        lax.all_gather(self_q, ("dp", "psg", "head"), axis=0, tiled=True),
        lax.all_gather(self_k, ("dp", "psg", "head"), axis=0, tiled=True),
        lax.all_gather(self_v, ("dp", "psg", "head"), axis=0, tiled=True),
        lax.all_gather(self_o, ("dp", "psg", "head"), axis=0, tiled=True),
        lax.all_gather(cross_q, ("dp", "psg", "head"), axis=0, tiled=True),
        lax.all_gather(cross_k, ("dp", "psg", "head"), axis=0, tiled=True),
        lax.all_gather(cross_v, ("dp", "psg", "head"), axis=0, tiled=True),
        lax.all_gather(cross_o, ("dp", "psg", "head"), axis=0, tiled=True),
        lax.all_gather(ff_gate, ("dp", "psg", "head"), axis=0, tiled=True),
        lax.all_gather(ff_up, ("dp", "psg", "head"), axis=0, tiled=True),
        lax.all_gather(ff_down, ("dp", "psg", "head"), axis=0, tiled=True),
    )
    (
        self_query,
        self_key,
        self_value,
        self_out,
        cross_query,
        cross_key,
        cross_value,
        cross_out,
        gate_full,
        up_full,
        down_full,
    ) = gathered
    head_index = lax.axis_index("head")
    heads_local = rel_table.shape[1]
    width = heads_local * HD
    total_width = self_query.shape[1]
    ff_total = gate_full.shape[1]
    ff_local = ff_total // lax.axis_size("head")
    query_rows = hidden_in.shape[0]
    target_span = hidden_in.shape[1]
    hidden = hidden_in.astype(jnp.float32)
    gain_all = gains.astype(jnp.float32)
    qkv_weight = jnp.concatenate(
        [
            own_columns(self_query, head_index, width),
            own_columns(self_key, head_index, width),
            own_columns(self_value, head_index, width),
        ],
        axis=1,
    )
    normed_one = rms_plain(hidden, gain_all[0]).astype(jnp.bfloat16)
    qkv_self = left_mul(normed_one, qkv_weight).astype(jnp.bfloat16)
    queries_self = qkv_self[..., :width].reshape(query_rows, target_span, heads_local, HD)
    keys_self = qkv_self[..., width : 2 * width].reshape(query_rows, target_span, heads_local, HD)
    values_self = qkv_self[..., 2 * width :].reshape(query_rows, target_span, heads_local, HD)
    positions = jnp.arange(target_span)
    causal = (positions[None, None, :] <= positions[None, :, None]) & (
        positions[None, None, :] < target_lengths[:, None, None]
    )
    buckets_hot = (rel_buckets[:, :, None] == jnp.arange(rel_table.shape[0])[None, None, :]).astype(
        jnp.float32
    )
    bias = jnp.einsum(
        "ijb,bh->hij", buckets_hot, rel_table.astype(jnp.float32), precision=lax.Precision.HIGHEST
    )
    scores_self = jnp.einsum(
        "qihd,qjhd->qhij", queries_self, keys_self, preferred_element_type=jnp.float32
    )
    scores_self = jnp.where(causal[:, None], scores_self + bias[None], NEGATIVE)
    probs_self = jax.nn.softmax(scores_self, axis=-1)
    probs_self_low = probs_self.astype(jnp.bfloat16)
    attn_one = jnp.einsum(
        "qhij,qjhd->qihd", probs_self_low, values_self, preferred_element_type=jnp.float32
    )
    attn_one = attn_one.reshape(query_rows, target_span, width).astype(jnp.bfloat16)
    self_out_own = own_columns(self_out, head_index, width)
    first = hidden + over_heads(right_mul(attn_one, self_out_own))
    normed_two = rms_plain(first, gain_all[1]).astype(jnp.bfloat16)
    cross_query_own = own_columns(cross_query, head_index, width)
    query_cross = left_mul(normed_two, cross_query_own).astype(jnp.bfloat16)
    query_group = lax.all_gather(query_cross, "psg", axis=0, tiled=True)
    group_count = query_group.shape[0]
    head_parts = lax.axis_size("head")
    kv_split = jnp.concatenate(
        [
            cross_key.reshape(cross_key.shape[0], head_parts, width),
            cross_value.reshape(cross_value.shape[0], head_parts, width),
        ],
        axis=2,
    )
    local_kv = jnp.einsum(
        "tpqd,dgc->qptgc", encodings, kv_split, preferred_element_type=jnp.float32
    ).astype(jnp.bfloat16)
    moved_kv = lax.all_to_all(local_kv, "head", split_axis=3, concat_axis=2, tiled=True)
    key_value = moved_kv.reshape(moved_kv.shape[0], moved_kv.shape[1], moved_kv.shape[2], 2 * width)
    passages_local = key_value.shape[1]
    passage_span = key_value.shape[2]
    key_count = passages_local * passage_span
    kv_flat = key_value.reshape(group_count, key_count, 2 * width)
    span = jnp.arange(passage_span)
    key_valid = (span[None, None, :] < jnp.transpose(passage_lengths)[:, :, None]).reshape(
        group_count, key_count
    )

    def masked_scores(query_block, kv_block, valid_block):
        query_heads = query_block.reshape(target_span, heads_local, HD)
        keys_part = kv_block[:, :width].reshape(key_count, heads_local, HD)
        raw = jnp.einsum("ihd,jhd->hij", query_heads, keys_part, preferred_element_type=jnp.float32)
        return jnp.where(valid_block[None, None, :], raw, NEGATIVE)

    def stats_one(item):
        masked = masked_scores(item[0], item[1], item[2])
        largest = jnp.max(masked, axis=-1)
        total = jnp.sum(jnp.exp(masked - largest[..., None]), axis=-1)
        return (largest, total)

    tops, totals = lax.map(stats_one, (query_group, kv_flat, key_valid))

    def combine(pair_one, pair_two):
        larger = jnp.maximum(pair_one[0], pair_two[0])
        return (
            larger,
            pair_one[1] * jnp.exp(pair_one[0] - larger)
            + pair_two[1] * jnp.exp(pair_two[0] - larger),
        )

    tops, totals = merged((tops, totals), "psg", combine)
    log_total = tops + jnp.log(totals)

    def values_one(item):
        masked = masked_scores(item[0], item[1], item[2])
        probs_low = jnp.exp(masked - item[3][..., None]).astype(jnp.bfloat16)
        values_part = item[1][:, width:].reshape(key_count, heads_local, HD)
        weighted = jnp.einsum(
            "hij,jhd->ihd", probs_low, values_part, preferred_element_type=jnp.float32
        )
        return weighted.reshape(target_span, width)

    partial_out = lax.map(values_one, (query_group, kv_flat, key_valid, log_total))
    attn_two = lax.psum_scatter(partial_out, "psg", scatter_dimension=0, tiled=True).astype(
        jnp.bfloat16
    )
    cross_out_own = own_columns(cross_out, head_index, width)
    second = first + over_heads(right_mul(attn_two, cross_out_own))
    normed_three = rms_plain(second, gain_all[2]).astype(jnp.bfloat16)
    ff_weight = jnp.concatenate(
        [own_columns(gate_full, head_index, ff_local), own_columns(up_full, head_index, ff_local)],
        axis=1,
    )
    gate_up = left_mul(normed_three, ff_weight)
    gate_part = gate_up[..., :ff_local]
    up_part = gate_up[..., ff_local:]
    activated = gated(gate_part, up_part).astype(jnp.bfloat16)
    down_own = own_columns(down_full, head_index, ff_local)
    output = second + over_heads(right_mul(activated, down_own))
    row_valid = (positions[None, :] < target_lengths[:, None])[:, :, None]
    out_hidden = jnp.where(row_valid, output, 0.0)
    grad_out = jnp.where(row_valid, cotangent.astype(jnp.float32), 0.0)
    grad_out_low = grad_out.astype(jnp.bfloat16)
    grad_down = row_outer(grad_out_low, activated)
    grad_act = left_mul(grad_out_low, down_own)
    gate_value, pull_gate = jax.vjp(gated, gate_part, up_part)
    grad_gate, grad_up = pull_gate(grad_act)
    grad_gate_up = jnp.concatenate([grad_gate, grad_up], axis=-1).astype(jnp.bfloat16)
    grad_ff_weight = row_outer(normed_three, grad_gate_up)
    grad_normed_three = over_heads(right_mul(grad_gate_up, ff_weight))
    norm_value, pull_three = jax.vjp(rms_plain, second, gain_all[2])
    grad_second_norm, grad_gain_three = pull_three(grad_normed_three)
    grad_two = grad_out + grad_second_norm
    grad_two_low = grad_two.astype(jnp.bfloat16)
    grad_cross_out = row_outer(grad_two_low, attn_two)
    grad_attn_two = left_mul(grad_two_low, cross_out_own).astype(jnp.bfloat16)
    grad_attn_group = lax.all_gather(grad_attn_two, "psg", axis=0, tiled=True)

    def prob_pieces(item):
        masked = masked_scores(item[0], item[1], item[2])
        probs = jnp.exp(masked - item[3][..., None])
        values_part = item[1][:, width:].reshape(key_count, heads_local, HD)
        grad_rows = item[4].reshape(target_span, heads_local, HD)
        grad_probs = jnp.einsum(
            "ihd,jhd->hij", grad_rows, values_part, preferred_element_type=jnp.float32
        )
        return (probs, grad_probs)

    def delta_one(item):
        probs, grad_probs = prob_pieces(item)
        return jnp.sum(probs * grad_probs, axis=-1)

    delta_part = lax.map(delta_one, (query_group, kv_flat, key_valid, log_total, grad_attn_group))
    delta = lax.psum(delta_part, "psg")

    def grads_one(item):
        probs, grad_probs = prob_pieces(item[:5])
        grad_scores = (probs * (grad_probs - item[5][..., None])).astype(jnp.bfloat16)
        probs_low = probs.astype(jnp.bfloat16)
        query_heads = item[0].reshape(target_span, heads_local, HD)
        keys_part = item[1][:, :width].reshape(key_count, heads_local, HD)
        grad_rows = item[4].reshape(target_span, heads_local, HD)
        grad_query = jnp.einsum(
            "hij,jhd->ihd", grad_scores, keys_part, preferred_element_type=jnp.float32
        )
        grad_keys = jnp.einsum(
            "hij,ihd->jhd", grad_scores, query_heads, preferred_element_type=jnp.float32
        )
        grad_values = jnp.einsum(
            "hij,ihd->jhd", probs_low, grad_rows, preferred_element_type=jnp.float32
        )
        grad_kv = jnp.concatenate(
            [grad_keys.reshape(key_count, width), grad_values.reshape(key_count, width)], axis=-1
        ).astype(jnp.bfloat16)
        return (grad_query.reshape(target_span, width), grad_kv)

    grad_query_group, grad_kv_flat = lax.map(
        grads_one, (query_group, kv_flat, key_valid, log_total, grad_attn_group, delta)
    )
    grad_query_cross = lax.psum_scatter(
        grad_query_group, "psg", scatter_dimension=0, tiled=True
    ).astype(jnp.bfloat16)
    grad_cross_query = row_outer(normed_two, grad_query_cross)
    grad_normed_two = over_heads(right_mul(grad_query_cross, cross_query_own))
    norm_value_two, pull_two = jax.vjp(rms_plain, first, gain_all[1])
    grad_first_norm, grad_gain_two = pull_two(grad_normed_two)
    grad_one = grad_two + grad_first_norm
    grad_kv = grad_kv_flat.reshape(group_count, passages_local, passage_span, 2 * width)
    grad_back = lax.all_to_all(
        grad_kv.reshape(group_count, passages_local, passage_span, 1, 2 * width),
        "head",
        split_axis=2,
        concat_axis=3,
        tiled=True,
    )
    d_encodings = jnp.einsum(
        "qptgc,dgc->tpqd", grad_back, kv_split, preferred_element_type=jnp.float32
    )
    grad_split = jnp.einsum(
        "tpqd,qptgc->dgc", encodings, grad_back, preferred_element_type=jnp.float32
    )
    grad_cross_key = grad_split[:, :, :width].reshape(grad_split.shape[0], total_width)
    grad_cross_value = grad_split[:, :, width:].reshape(grad_split.shape[0], total_width)
    grad_one_low = grad_one.astype(jnp.bfloat16)
    grad_self_out = row_outer(grad_one_low, attn_one)
    grad_attn_one = left_mul(grad_one_low, self_out_own).astype(jnp.bfloat16)
    grad_attn_one = grad_attn_one.reshape(query_rows, target_span, heads_local, HD)
    grad_probs_self = jnp.einsum(
        "qihd,qjhd->qhij", grad_attn_one, values_self, preferred_element_type=jnp.float32
    )
    grad_scores_self = probs_self * (
        grad_probs_self - jnp.sum(probs_self * grad_probs_self, axis=-1, keepdims=True)
    )
    grad_table = jnp.einsum(
        "ijb,hij->bh",
        buckets_hot,
        jnp.sum(grad_scores_self, axis=0),
        precision=lax.Precision.HIGHEST,
    )
    grad_scores_low = grad_scores_self.astype(jnp.bfloat16)
    grad_query_self = jnp.einsum(
        "qhij,qjhd->qihd", grad_scores_low, keys_self, preferred_element_type=jnp.float32
    )
    grad_key_self = jnp.einsum(
        "qhij,qihd->qjhd", grad_scores_low, queries_self, preferred_element_type=jnp.float32
    )
    grad_value_self = jnp.einsum(
        "qhij,qihd->qjhd", probs_self_low, grad_attn_one, preferred_element_type=jnp.float32
    )
    grad_qkv = jnp.concatenate(
        [
            grad_query_self.reshape(query_rows, target_span, width),
            grad_key_self.reshape(query_rows, target_span, width),
            grad_value_self.reshape(query_rows, target_span, width),
        ],
        axis=-1,
    ).astype(jnp.bfloat16)
    grad_qkv_weight = row_outer(normed_one, grad_qkv)
    grad_normed_one = over_heads(right_mul(grad_qkv, qkv_weight))
    norm_value_one, pull_one = jax.vjp(rms_plain, hidden, gain_all[0])
    grad_hidden_norm, grad_gain_one = pull_one(grad_normed_one)
    d_hidden = grad_one + grad_hidden_norm
    grad_gains = jnp.stack([grad_gain_one, grad_gain_two, grad_gain_three])
    d_gains, d_rel_table = lax.psum((grad_gains, grad_table), ("dp", "psg"))
    own_grads = [
        grad_qkv_weight[:, :width],
        grad_qkv_weight[:, width : 2 * width],
        grad_qkv_weight[:, 2 * width :],
        grad_self_out,
        grad_cross_query,
        grad_cross_out,
        grad_ff_weight[:, :ff_local],
        grad_ff_weight[:, ff_local:],
        grad_down,
    ]
    row_sums = lax.psum_scatter(tuple(own_grads), ("dp", "psg"), scatter_dimension=0, tiled=True)
    owned = (
        lax.all_to_all(row_sums[0], "head", split_axis=0, concat_axis=1, tiled=True),
        lax.all_to_all(row_sums[1], "head", split_axis=0, concat_axis=1, tiled=True),
        lax.all_to_all(row_sums[2], "head", split_axis=0, concat_axis=1, tiled=True),
        lax.all_to_all(row_sums[3], "head", split_axis=0, concat_axis=1, tiled=True),
        lax.all_to_all(row_sums[4], "head", split_axis=0, concat_axis=1, tiled=True),
        lax.all_to_all(row_sums[5], "head", split_axis=0, concat_axis=1, tiled=True),
        lax.all_to_all(row_sums[6], "head", split_axis=0, concat_axis=1, tiled=True),
        lax.all_to_all(row_sums[7], "head", split_axis=0, concat_axis=1, tiled=True),
        lax.all_to_all(row_sums[8], "head", split_axis=0, concat_axis=1, tiled=True),
    )
    key_done, value_done = (
        lax.psum_scatter(grad_cross_key, ("dp", "psg", "head"), scatter_dimension=0, tiled=True),
        lax.psum_scatter(grad_cross_value, ("dp", "psg", "head"), scatter_dimension=0, tiled=True),
    )
    return (
        out_hidden,
        d_hidden,
        d_encodings,
        d_gains,
        d_rel_table,
        owned[0],
        owned[1],
        owned[2],
        owned[3],
        owned[4],
        key_done,
        value_done,
        owned[5],
        owned[6],
        owned[7],
        owned[8],
    )


PLACED = (
    P(("dp", "psg"), None, None),
    P("head", "psg", "dp", None),
    P("psg", "dp"),
    P(("dp", "psg")),
    P(),
    P(),
    P(None, "head"),
    P(("dp", "psg", "head"), None),
    P(("dp", "psg", "head"), None),
    P(("dp", "psg", "head"), None),
    P(("dp", "psg", "head"), None),
    P(("dp", "psg", "head"), None),
    P(("dp", "psg", "head"), None),
    P(("dp", "psg", "head"), None),
    P(("dp", "psg", "head"), None),
    P(("dp", "psg", "head"), None),
    P(("dp", "psg", "head"), None),
    P(("dp", "psg", "head"), None),
    P(("dp", "psg"), None, None),
)

OUTS = (
    P(("dp", "psg"), None, None),
    P(("dp", "psg"), None, None),
    P("head", "psg", "dp", None),
    P(),
    P(None, "head"),
    P(("dp", "psg", "head"), None),
    P(("dp", "psg", "head"), None),
    P(("dp", "psg", "head"), None),
    P(("dp", "psg", "head"), None),
    P(("dp", "psg", "head"), None),
    P(("dp", "psg", "head"), None),
    P(("dp", "psg", "head"), None),
    P(("dp", "psg", "head"), None),
    P(("dp", "psg", "head"), None),
    P(("dp", "psg", "head"), None),
    P(("dp", "psg", "head"), None),
)


def solution(mesh):
    def local(*args):
        rows, span, heads = args[7].shape[0], args[1].shape[0], args[6].shape[1]
        fits = (mesh.shape["dp"], mesh.shape["psg"], mesh.shape["head"], heads) == (2, 4, 4, 3)
        fits = fits and (4 * rows) % 16 == 0 and rows % 8 == 0
        return (local_fast if fits else local_plain)(*args)

    placed = PLACED
    return jax.shard_map(local, mesh=mesh, in_specs=placed, out_specs=OUTS, check_vma=False)
```

```python
import functools

import jax
import jax.numpy as jnp
from jax import lax
from jax.experimental import pallas as pl
from jax.experimental.pallas import tpu as pltpu
from jax.sharding import PartitionSpec as P

HD = 64
EPSILON = 1e-06
NEGATIVE = -1e30
AUG = 64
BF = jnp.bfloat16
F32 = jnp.float32
MESH = pl.DeviceIdType.MESH
VMEM = pltpu.VMEM


def nn(a, b):
    return lax.dot_general(a, b, (((1,), (0,)), ((), ())), preferred_element_type=F32)


def nt(a, b):
    return lax.dot_general(a, b, (((1,), (1,)), ((), ())), preferred_element_type=F32)


def tn(a, b):
    return lax.dot_general(a, b, (((0,), (0,)), ((), ())), preferred_element_type=F32)


def rms_scale(v):
    return lax.rsqrt(jnp.mean(v * v, axis=-1, keepdims=True) + EPSILON)


def rms_norm(v, gain):
    return v * rms_scale(v) * gain


def rms_back(dn, v, gain):
    r = rms_scale(v)
    gd = gain * dn
    dv = r * gd - v * (r * r * r * jnp.mean(gd * v, axis=-1, keepdims=True))
    dg = jnp.sum(dn * v * r, axis=0, keepdims=True)
    return dv, dg


def iota(shape, axis):
    return lax.broadcasted_iota(jnp.int32, shape, axis)


class Net:
    def __init__(self, send_sems, recv_sems):
        self.send_sems, self.recv_sems, self.count, self.sent = send_sems, recv_sems, 0, []

    def send(self, src, dst, **device):
        at = self.count
        self.count += 1
        copy = pltpu.make_async_remote_copy(
            src, dst, self.send_sems.at[at], self.recv_sems.at[at],
            device_id=device, device_id_type=MESH,
        )
        copy.start()
        self.sent.append(copy)
        return copy

    def finish(self):
        for copy in self.sent:
            copy.wait_send()


def places():
    d, z, h = lax.axis_index("dp"), lax.axis_index("psg"), lax.axis_index("head")
    return dict(
        c=(h % 2, dict(head=h ^ 1)), x=(h // 2, dict(head=h ^ 2)), y=(d, dict(dp=1 - d)),
        a=(z // 2, dict(psg=z ^ 3)), b=(z % 2, dict(psg=z ^ 1)),
    )


class Doubling:
    def __init__(self, net, ref, names, order, late=()):
        self.net, self.ref, self.names, self.order, self.at = net, ref, names, order, places()
        self.late = [order.index(n) + 1 for n in late]
        self.sent = {s: [] if s in self.late else [self.go(0, s)] for s in range(1, len(order) + 1)}

    def region(self, j):
        idx = []
        for n in self.names:
            p, mine = self.order.index(n) + 1, self.at[n][0]
            idx.append(mine if p > j else (1 - mine if p == j else slice(None)))
        return self.ref.at[tuple(idx)]

    def go(self, j, s):
        block = self.region(j)
        return self.net.send(block, block, **self.at[self.order[s - 1]][1])

    def open(self, name, have):
        s = self.order.index(name) + 1
        self.late.remove(s)
        self.sent[s] = [self.go(i, s) for i in range(have + 1)]

    def step(self, name):
        j = self.order.index(name) + 1
        for c in self.sent[j]:
            c.wait_recv()
        for s in range(j + 1, len(self.order) + 1):
            if s not in self.late:
                self.sent[s].append(self.go(j, s))
            elif s == j + 1:
                self.sent[s] = [self.go(i, s) for i in range(s)]


class Halving:
    def __init__(self, net, src, names, order, bufs, total, shard):
        self.net, self.src, self.names, self.order, self.bufs = net, src, names, order, bufs
        self.total, self.shard, self.at, self.stage = total, shard, places(), 0

    def index(self, stage, last, free):
        idx, free = [], list(free)
        for n in self.names:
            p, mine = self.order.index(n), self.at[n][0]
            idx.append(mine if p < stage else (last(mine) if p == stage else free.pop(0)))
        return tuple(idx)

    def push(self):
        n = len(self.order) - self.stage - 1
        far = self.src.at[self.index(self.stage, lambda m: 1 - m, [slice(None)] * n)]
        self.copy = self.net.send(far, self.bufs[self.stage], **self.at[self.order[self.stage]][1])

    def pull(self):
        self.copy.wait_recv()
        n = len(self.order) - self.stage - 1
        buf = self.bufs[self.stage]
        if n == 0:
            idx = self.index(self.stage, lambda m: m, [])
            self.total[...] = self.src[idx].astype(F32) + buf[...].astype(F32)
        else:
            def add(i, carry):
                bits = [(i // 2**k) % 2 for k in range(n)]
                idx = self.index(self.stage, lambda m: m, bits)
                self.src[idx] = (self.src[idx].astype(F32) + buf[tuple(bits)].astype(F32)).astype(BF)
                return carry

            lax.fori_loop(0, 2**n, add, 0)
        self.stage += 1
        if n:
            self.push()
        else:
            self.trade()

    def trade(self):
        n, h = self.shard.shape[1], lax.axis_index("head")

        def rows(hh):
            return pl.ds(pl.multiple_of(n * hh, n), n)

        self.last = [self.net.send(self.total.at[rows(h ^ m)], self.shard.at[h], head=h ^ m) for m in (2, 3, 1)]
        self.shard[h] = self.total[rows(h), :]

    def done(self):
        for c in self.last:
            c.wait_recv()


def enter():
    barrier = pltpu.get_barrier_semaphore()
    d, z, h = lax.axis_index("dp"), lax.axis_index("psg"), lax.axis_index("head")
    peers = [dict(head=h ^ m) for m in (1, 2, 3)]
    peers += [dict(psg=lax.rem(z + m, 4)) for m in (1, 2, 3)]
    peers += [dict(dp=1 - d)]
    for peer in peers:
        pl.semaphore_signal(barrier, inc=1, device_id=peer, device_id_type=MESH)
    pl.semaphore_wait(barrier, len(peers))
    return d, z, h


ORDER = (1, 3, 2, 0)


class Gather:
    def __init__(self, net, buf, z, h, rows):
        self.net, self.buf, self.z, self.h, self.rows = net, buf, z, h, rows
        mine = self.at(z, h)
        self.ring = {m: net.send(mine, mine, psg=lax.rem(z + m, 4)) for m in (1, 3, 2)}
        self.hops = {0: self.on(z)}
        self.last = {}

    def at(self, zz, hh):
        return self.buf.at[zz, pl.ds(pl.multiple_of(self.rows * hh, self.rows), self.rows)]

    def on(self, zz):
        block = self.at(zz, self.h)
        return [self.net.send(block, block, head=self.h ^ 2), self.net.send(block, block, head=self.h ^ 1)]

    def source(self, m):
        return lax.rem(self.z - m + 4, 4)

    def relay(self):
        for m in (1, 3, 2):
            self.ring[m].wait_recv()
            self.hops[m] = self.on(self.source(m))
        for m in ORDER:
            self.hops[m][0].wait_recv()
            block = self.at(self.source(m), self.h ^ 2)
            self.last[m] = self.net.send(block, block, head=self.h ^ 1)

    def ready(self, m):
        self.hops[m][1].wait_recv()
        self.last[m].wait_recv()


def kernel_one(
    plen, tlen,
    table, hid, ench, buckets, gains, sq, sk, sv, so, cq, ck, cv, co, fg, fu, fd, cot,
    FAH, FKH, GQH, KPH, VPH, KTH, ETH, PSH, QA, QKV, AO, FIRST, G2, DO, GCH, GFH, DG3, OUT,
    PQ, PA, PK, PC, PG, AQ, AA, AK, AC, AG,
    FA, FK, FC, GQ, GG, KP, VP, KT, VT, ET, PS, ATT, GC, GF,
    enc, QU, BIAS, AOS, OS, ST, OC, SC, OXS, SXS, OX, SX, OZS, SZS, OZ, SZ,
    OWN, SOWN, ATS, AT, N3, R3S, R3, R1S, R1, QM,
    ss, rs, ls,
):
    d, z, h = enter()
    net = Net(ss, rs)
    T, D = hid.shape
    R = T // 4
    W = 3 * HD
    hc, hx = h % 2, h // 2
    e = 1 - d
    zp, zm, zo = lax.rem(z + 1, 4), lax.rem(z + 3, 4), lax.rem(z + 2, 4)
    kept = []

    def keep_out(src, dst):
        c = pltpu.make_async_copy(src, dst, ls.at[len(kept)])
        c.start()
        kept.append(c)

    e_load = pltpu.make_async_copy(ench, enc, ls.at[11])
    e_load.start()

    mats = {n: r[...].astype(F32) for n, r in dict(sq=sq, sk=sk, sv=sv, so=so, cq=cq, ck=ck, cv=cv, co=co).items()}
    F = fg.shape[1] // 4

    def pack(dst, names):
        for g in range(4):
            s = slice(W * g, W * g + W)
            parts = [mats[n][:, s] for n in names]
            dst[g] = (jnp.concatenate(parts, axis=1) if len(parts) > 1 else parts[0]).astype(BF)

    def trade(src, dst):
        cs = [net.send(src.at[h ^ m], dst.at[h], head=h ^ m) for m in (2, 3, 1)]
        dst[h] = src[h]
        return cs

    pack(PQ, ("sq", "sk", "sv"))
    tq = trade(PQ, AQ)
    pack(PA, ("so", "cq"))
    ta = trade(PA, AA)
    pack(PK, ("ck", "cv"))
    tk = trade(PK, AK)
    pack(PC, ("co",))
    for g in range(4):
        for i, ref in enumerate((fg, fu, fd)):
            PG[g, :, F * i : F * i + F] = ref[:, F * g : F * g + F]
    tc = trade(PC, AC)
    tg = trade(PG, AG)

    def assemble(cs, src, dst):
        for c in cs:
            c.wait_recv()
        dst[...] = jnp.concatenate([src[j].astype(F32) for j in range(4)], axis=0).astype(BF)

    full, own = ("c", "x", "y", "a", "b"), ("y", "a", "b")
    za, zb = z // 2, z % 2
    assemble(tq, AQ, GQ.at[d, za, zb])
    wq = Doubling(net, GQ, own, ("b", "a", "y"))
    assemble(ta, AA, FA.at[hc, hx, d, za, zb])
    wa = Doubling(net, FA, full, ("b", "a", "x", "y", "c"))
    assemble(tk, AK, FK.at[hc, hx, d, za, zb])
    wk = Doubling(net, FK, full, ("b", "a", "y", "x", "c"))
    g0 = gains[0:1].astype(F32)
    hidden = hid[...].astype(F32)
    n1 = rms_norm(hidden, g0).astype(BF)

    def flip(q, carry):
        ET[q] = enc[q].astype(F32).T.astype(BF)
        return carry

    assemble(tc, AC, FC.at[hc, hx, d, za, zb])
    assemble(tg, AG, GG.at[d, za, zb])
    for w in (wq, wk, wa):
        w.step("b")
    e_load.wait()
    lax.fori_loop(0, 2, flip, 0)
    for w in (wq, wa, wk):
        w.step("a")
    wc = Doubling(net, FC, full, ("b", "a", "y", "x", "c"), ("x", "c"))
    wg = Doubling(net, GG, own, ("b", "a", "y"), ("y",))
    lax.fori_loop(2, 4, flip, 0)
    bk = buckets[...]
    tab = table[...].astype(F32)
    for a in range(3):
        acc = jnp.zeros((T, T), F32)
        for i in range(tab.shape[1]):
            acc = jnp.where(bk == i, tab[a : a + 1, i : i + 1], acc)
        BIAS[a] = acc
    wa.step("x")
    wk.step("y")
    wg.open("y", 0)
    wq.step("y")

    wqkv = GQ[...].reshape(D, 3 * W)
    QKV[...] = nn(n1, wqkv).astype(BF)
    keep_out(GQ, GQH)
    wk.step("x")
    wc.step("b")
    wg.step("b")
    qs, ks, vs = QKV[:, 0:W], QKV[:, W : 2 * W], QKV[:, 2 * W : 3 * W]
    lane = iota((T, W), 1)
    row, col = iota((T, T), 0), iota((T, T), 1)
    keep = (col <= row) & (col < tlen[0])
    acc = jnp.zeros((T, W), F32)
    zero = jnp.zeros((T, W), BF)
    for a in range(3):
        mine = (lane >= HD * a) & (lane < HD * a + HD)
        s = nt(jnp.where(mine, qs, zero), ks) + BIAS[a]
        s = jnp.where(keep, s, NEGATIVE)
        ex = jnp.exp(s - jnp.max(s, axis=-1, keepdims=True))
        p = ex / jnp.sum(ex, axis=-1, keepdims=True)
        PS[a] = p
        acc += nn(p.astype(BF), jnp.where(mine, vs, zero))
    AOS[...] = acc.astype(BF)
    ao = [net.send(AOS.at[pl.ds(pl.multiple_of(R * (h ^ m), R), R)], AO.at[h], head=h ^ m) for m in (2, 3, 1)]
    AO[h] = AOS[pl.ds(pl.multiple_of(R * h, R), R), :]
    keep_out(PS, PSH)
    wa.step("y")
    wa.step("c")
    for c in ao:
        c.wait_recv()

    def part(ref, g, i=None):
        blk = ref[g % 2, g // 2] if i is None else ref[g % 2, g // 2, :, :, :, :, W * i : W * i + W]
        return blk.reshape(D, blk.shape[-1])

    mine_rows = pl.ds(pl.multiple_of(R * h, R), R)
    first = hid[mine_rows, :].astype(F32)
    for g in range(4):
        first += nt(AO[g], part(FA, g, 0))
    FIRST[...] = first
    n2 = rms_norm(first, gains[1:2].astype(F32)).astype(BF)
    QA[z, mine_rows, :] = jnp.concatenate([nn(n2, part(FA, g, 1)) for g in range(4)], axis=1).astype(BF)
    spreadq = Gather(net, QA, z, h, R)
    keep_out(FA, FAH)
    wk.step("c")
    keep_out(FK, FKH)

    tok = enc.shape[1]
    krow, klane = iota((tok, AUG), 0), iota((tok, AUG), 1)
    per = 96
    npass = plen.shape[1]
    vaug = jnp.where(klane < 9, -1.0, 0.0).astype(F32)

    def project(q, carry):
        dead = krow >= per * npass
        for p in range(npass):
            inside = (krow >= per * p) & (krow < per * p + per)
            dead = dead | (inside & (krow - per * p + per * h >= plen[q, p]))
        kaug = jnp.where(klane == 9, jnp.where(dead, NEGATIVE, 0.0), vaug)

        def group(g, c2):
            kv = nn(enc[q], FK[g % 2, g // 2].reshape(D, 2 * W))
            k, v = kv[:, :W], kv[:, W:]
            KP[q, g] = jnp.concatenate([k, kaug], axis=1).astype(BF)
            VP[q, g] = jnp.concatenate([v, vaug], axis=1).astype(BF)
            KT[q, g] = k.T.astype(BF)
            VT[q, g] = v.T.astype(BF)
            return c2

        lax.fori_loop(0, 4, group, 0)
        return carry

    lax.fori_loop(0, 2, project, 0)
    spreadq.relay()
    wc.step("a")
    wg.step("a")
    lax.fori_loop(2, 4, project, 0)
    for src, dst in ((KP, KPH), (VP, VPH), (KT, KTH), (ET, ETH)):
        keep_out(src, dst)

    qaug = jnp.where(iota((T, AUG), 1) == 9, 1.0, 0.0).astype(BF)

    def weights(m1, l1, m2, l2):
        top = jnp.maximum(m1, m2)
        w1, w2 = l1 * jnp.exp(m1 - top), l2 * jnp.exp(m2 - top)
        return top, w1 + w2, w1, w2

    def spread(x):
        return jnp.concatenate([jnp.broadcast_to(x[a : a + 1], (HD, T)) for a in range(3)], axis=0)

    def join(o1, s1, o2, s2):
        top, tot, w1, w2 = weights(s1[0:3], s1[3:6], s2[0:3], s2[3:6])
        o = o1 * spread(w1 / tot) + o2 * spread(w2 / tot)
        return o, jnp.concatenate([top, tot, jnp.zeros((2, T), F32)], axis=0)

    def attend(i, zz):
        for g in range(4):
            QU[g] = QA[zz, :, W * g : W * g + W]

        def group(g, carry):
            qg, kg = QU[g], KP[zz, g]
            outs, tops, tots = [], [], []
            for a in range(3):
                mine = (lane >= HD * a) & (lane < HD * a + HD)
                qm = jnp.concatenate([jnp.where(mine, qg, zero), qaug], axis=1)
                s = nt(kg, qm)
                m = jnp.max(s, axis=0, keepdims=True)
                ex = jnp.exp(s - m)
                l = jnp.sum(ex, axis=0, keepdims=True)
                o = nn(VT[zz, g, HD * a : HD * a + HD, :], ex.astype(BF))
                outs.append(o / l)
                tops.append(m)
                tots.append(l)
            gc, gx = g % 2, g // 2
            OS[i, gc, gx] = jnp.concatenate(outs, axis=0).astype(BF)
            ST[i, gc, gx] = jnp.concatenate(tops + tots + [jnp.zeros((2, T), F32)], axis=0)
            return carry

        lax.fori_loop(0, 4, group, 0)

    q_core, q_x, q_z = {}, {}, {}

    def core_stage(i):
        q_core[i] = (net.send(OS.at[i, 1 - hc], OC.at[i], head=h ^ 1), net.send(ST.at[i, 1 - hc], SC.at[i], head=h ^ 1))

    def x_stage(i):
        for c in q_core[i]:
            c.wait_recv()
        o, s = join(OS[i, hc, 1 - hx].astype(F32), ST[i, hc, 1 - hx], OC[i, 1 - hx].astype(F32), SC[i, 1 - hx])
        OXS[i] = o.astype(BF)
        SXS[i] = s
        q_x[i] = (net.send(OXS.at[i], OX.at[i], head=h ^ 2), net.send(SXS.at[i], SX.at[i], head=h ^ 2))
        o, s = join(OS[i, hc, hx].astype(F32), ST[i, hc, hx], OC[i, hx].astype(F32), SC[i, hx])
        OWN[i] = o
        SOWN[i] = s

    def z_stage(i):
        for c in q_x[i]:
            c.wait_recv()
        o, s = join(OWN[i], SOWN[i], OX[i].astype(F32), SX[i])
        if i < 3:
            m = ORDER[i]
            OZS[i] = o.astype(BF)
            SZS[i] = s
            to = lax.rem(z - m + 4, 4)
            q_z[i] = (net.send(OZS.at[i], OZ.at[i], psg=to), net.send(SZS.at[i], SZ.at[i], psg=to))
        else:
            OWN[i] = o
            SOWN[i] = s

    for i, m in enumerate(ORDER):
        zz = lax.rem(z - m + 4, 4)
        spreadq.ready(m)
        attend(i, zz)
        if i < 2:
            wc.step(("y", "x")[i])
        core_stage(i)
        if i >= 1:
            x_stage(i - 1)
        if i >= 2:
            z_stage(i - 2)
    x_stage(3)
    z_stage(2)
    z_stage(3)
    o, s = OWN[3], SOWN[3]
    for i in range(3):
        for c in q_z[i]:
            c.wait_recv()
        o, s = join(o, s, OZ[i].astype(F32), SZ[i])
    lse = s[0:3] + jnp.log(s[3:6])
    full = jnp.concatenate([o, lse, jnp.zeros((AUG - 3, T), F32)], axis=0)
    ATS[...] = full.T
    at = [net.send(ATS.at[pl.ds(pl.multiple_of(R * (h ^ m), R), R)], AT.at[h], head=h ^ m) for m in (1, 2, 3)]
    AT[h] = ATS[mine_rows, :]
    wc.step("c")
    for c in at:
        c.wait_recv()
    second = FIRST[...]
    for g in range(4):
        low = AT[g, :, 0:W].astype(BF)
        ATT[g] = low
        second += nt(low, part(FC, g))
    g2gain = gains[2:3].astype(F32)
    N3[mine_rows, :] = rms_norm(second, g2gain).astype(BF)
    n3c = [net.send(N3.at[mine_rows], N3.at[mine_rows], head=h ^ m) for m in (2, 3, 1)]
    rowid = iota((T, 1), 0)
    go_low = jnp.where(rowid < tlen[0], cot[...], jnp.zeros((T, D), BF))
    wg.step("y")
    for c in n3c:
        c.wait_recv()
    wdown = GG[:, :, :, :, 2 * F : 3 * F].reshape(D, F)
    wgu = GG[:, :, :, :, 0 : 2 * F].reshape(D, 2 * F)
    d_act = nn(go_low, wdown)
    n3 = N3[...]
    gate_up = nn(n3, wgu)
    gate, up = gate_up[:, :F], gate_up[:, F:]
    c0 = 0.7978845608028654
    inner = c0 * (gate + 0.044715 * gate * gate * gate)
    th = jnp.tanh(inner)
    gel = 0.5 * gate * (1.0 + th)
    act = (gel * up).astype(BF)
    dgel = 0.5 * (1.0 + th) + 0.5 * gate * (1.0 - th * th) * (c0 * (1.0 + 3 * 0.044715 * gate * gate))
    dgu = jnp.concatenate([d_act * up * dgel, d_act * gel], axis=1).astype(BF)
    R3S[...] = nt(dgu, wgu).astype(BF)
    r3 = [net.send(R3S.at[pl.ds(pl.multiple_of(R * (h ^ m), R), R)], R3.at[h], head=h ^ m) for m in (2, 3, 1)]
    R1S[...] = nt(act, wdown).astype(BF)
    r1 = [net.send(R1S.at[pl.ds(pl.multiple_of(R * (h ^ m), R), R)], R1.at[h], head=h ^ m) for m in (2, 3, 1)]
    R3[h] = R3S[mine_rows, :]
    R1[h] = R1S[mine_rows, :]
    GF[:, :, :, :, 2 * F : 3 * F] = tn(go_low, act).astype(BF).reshape(2, 2, 2, D // 8, F)
    GF[:, :, :, :, 0 : 2 * F] = tn(n3, dgu).astype(BF).reshape(2, 2, 2, D // 8, 2 * F)
    keep_out(GF, GFH)
    for c in r3:
        c.wait_recv()
    dn3 = R3[0].astype(F32) + R3[1].astype(F32) + R3[2].astype(F32) + R3[3].astype(F32)
    live = (iota((R, 1), 0) + R * h) < tlen[0]
    go = jnp.where(live, cot[mine_rows, :].astype(F32), 0.0)
    dv, dg = rms_back(dn3, second, g2gain)
    DG3[...] = jnp.concatenate([dg, jnp.zeros((7, D), F32)], axis=0)
    g2 = go + dv
    G2[...] = g2
    g2_low = g2.astype(BF)
    alane = iota((R, 2 * AUG), 1)
    wl = iota((R, W), 1)
    aug = jnp.zeros((R, 2 * AUG), F32)
    dos = []

    def parts(x):
        hi_ = x.astype(BF).astype(F32)
        mid = (x - hi_).astype(BF).astype(F32)
        return hi_, mid, x - hi_ - mid

    for g in range(4):
        do = nn(g2_low, part(FC, g)).astype(BF)
        dos.append(do.astype(F32))
        GC[g % 2, g // 2] = tn(g2_low, ATT[g]).astype(BF).reshape(2, 2, 2, D // 8, W)
        prod = do.astype(F32) * AT[g, :, 0:W]
        for a in range(3):
            delta = jnp.sum(jnp.where((wl >= HD * a) & (wl < HD * a + HD), prod, 0.0), axis=1, keepdims=True)
            for off, val in ((0, AT[g, :, W + a : W + a + 1]), (AUG, delta)):
                for j, piece in enumerate(parts(val)):
                    aug = jnp.where(alane == off + 9 * g + 3 * a + j, piece, aug)
    DO[...] = jnp.concatenate(dos + [aug], axis=1).astype(BF)
    keep_out(GC, GCH)
    for c in r1:
        c.wait_recv()
    out = second + R1[0].astype(F32) + R1[1].astype(F32) + R1[2].astype(F32) + R1[3].astype(F32)
    OUT[...] = jnp.where(live, out, 0.0)
    for c in kept:
        c.wait()
    net.finish()


def call_one(plen, tlen, table, hid, enc, buckets, gains, mats, cot):
    T, D = hid.shape
    R = T // 4
    W = 3 * HD
    rows = mats[0].shape[0]
    F = mats[8].shape[1] // 4
    tok = enc.shape[1]
    S = jax.ShapeDtypeStruct
    blk = 4 * rows
    big = dict(
        FA=((2, 2, 2, 2, 2, blk, 2 * W), BF), FK=((2, 2, 2, 2, 2, blk, 2 * W), BF), FC=((2, 2, 2, 2, 2, blk, W), BF),
        GQ=((2, 2, 2, blk, 3 * W), BF),
        KP=((4, 4, tok, W + AUG), BF), VP=((4, 4, tok, W + AUG), BF), KT=((4, 4, W, tok), BF),
        ET=((4, D, tok), BF), PS=((3, T, T), F32),
        GC=((2, 2, 2, 2, 2, blk, W), BF), GF=((2, 2, 2, blk, 3 * F), BF),
    )
    outs = {n: big[n] for n in ("FA", "FK", "GQ", "KP", "VP", "KT", "ET", "PS")}
    outs.update(
        QA=((4, T, D), BF), QKV=((T, 3 * W), BF), AO=((4, R, W), BF), FIRST=((R, D), F32),
        G2=((R, D), F32), DO=((R, D + 2 * AUG), BF), GC=big["GC"],
        GF=big["GF"], DG3=((8, D), F32), OUT=((R, D), F32),
    )
    pack = [VMEM((4, rows, w), BF) for w in (3 * W, 2 * W, 2 * W, W, 3 * F)]
    scratch = pack + pack + [
        *[VMEM(*big[n]) for n in ("FA", "FK", "FC", "GQ")], VMEM((2, 2, 2, blk, 3 * F), BF),
        *[VMEM(*big[n]) for n in ("KP", "VP", "KT")], VMEM((4, 4, W, tok), BF),
        *[VMEM(*big[n]) for n in ("ET", "PS")], VMEM((4, R, W), BF), VMEM(*big["GC"]), VMEM(*big["GF"]),
        VMEM(enc.shape, BF), VMEM((4, T, W), BF), VMEM((3, T, T), F32), VMEM((T, W), BF),
        VMEM((4, 2, 2, W, T), BF), VMEM((4, 2, 2, 8, T), F32),
        VMEM((4, 2, W, T), BF), VMEM((4, 2, 8, T), F32),
        VMEM((4, W, T), BF), VMEM((4, 8, T), F32), VMEM((4, W, T), BF), VMEM((4, 8, T), F32),
        VMEM((3, W, T), BF), VMEM((3, 8, T), F32), VMEM((3, W, T), BF), VMEM((3, 8, T), F32),
        VMEM((4, W, T), F32), VMEM((4, 8, T), F32),
        VMEM((T, W + AUG), F32), VMEM((4, R, W + AUG), F32), VMEM((T, D), BF),
        VMEM((T, D), BF), VMEM((4, R, D), BF), VMEM((T, D), BF), VMEM((4, R, D), BF),
        VMEM((3 * T, W + AUG), BF),
        pltpu.SemaphoreType.DMA((160,)), pltpu.SemaphoreType.DMA((160,)), pltpu.SemaphoreType.DMA((12,)),
    ]
    smem = pl.BlockSpec(memory_space=pltpu.SMEM)
    vm = pl.BlockSpec(memory_space=pltpu.VMEM)
    anym = pl.BlockSpec(memory_space=pl.ANY)
    res = pl.pallas_call(
        kernel_one,
        out_shape=[S(*v) for v in outs.values()],
        in_specs=[smem] * 2 + [vm] * 2 + [anym] + [vm] * 14,
        out_specs=[anym if n in big else vm for n in outs],
        scratch_shapes=scratch,
        name="forward",
        compiler_params=pltpu.CompilerParams(collective_id=1, has_side_effects=True, vmem_limit_bytes=63 << 20),
    )(plen, tlen, table, hid, enc, buckets, gains, *mats, cot)
    return dict(zip(outs, res))


def kernel_two(
    buckets, gains, hid, ETH, FAH, FKH, GQH, QA, KPH, VPH, KTH, PSH, QKV, AO, FIRST, G2, DO, GCH, GFH, DG3, OUTR,
    DENC, DHID, OUT, SM, OF, OC, OK, OA, OL,
    DOB, KP, VP, KT, QAV, ET, FA, FK, GQ, PS,
    QU, DU, QX, DX, QM, DM, DS, PB, DQG, DKV, DQS, DQC, DXR, DOWN, DZS, DZR, DAS, DA, DSF, TBL, NS, NR, DEN,
    FSRC, F1, F2, F3, FTOT, CSRC, C1, C2, C3, C4, C5, CTOT,
    KSRC, K1, K2, K3, K4, K5, KTOT, ASRC, A1, A2, A3, A4, A5, ATOT,
    LSRC, L1, L2, L3, LTOT,
    SMR, DQL, N2, G1L,
    ss, rs, ls, es,
):
    d, z, h = enter()
    net = Net(ss, rs)
    T, D = hid.shape
    R = T // 4
    W = 3 * HD
    hc, hx = h % 2, h // 2
    tok = ETH.shape[2]
    mine_rows = pl.ds(pl.multiple_of(R * h, R), R)

    def source(m):
        return lax.rem(z - m + 4, 4)

    def load(pairs, sem):
        cs = [pltpu.make_async_copy(a, b, sem(j)) for j, (a, b) in enumerate(pairs)]
        for c in cs:
            c.start()
        return cs

    def fetch(i):
        zz, slot = source(ORDER[i]), i % 2
        return load(
            [(a.at[zz], b.at[slot]) for a, b in ((KPH, KP), (VPH, VP), (KTH, KT), (QA, QAV))],
            lambda j: ls.at[j, slot],
        )

    DOB[z, mine_rows, :] = DO[...]
    gather = Gather(net, DOB, z, h, R)
    fetched = fetch(0)
    near = load([(GCH, CSRC), (GFH, FSRC)], lambda j: es.at[j])
    full, own = ("c", "x", "y", "a", "b"), ("y", "a", "b")
    sf = Halving(net, FSRC, own, ("y", "a", "b"), (F1, F2, F3), FTOT, OF)
    sc = Halving(net, CSRC, full, ("c", "y", "x", "a", "b"), (C1, C2, C3, C4, C5), CTOT, OC)
    sk = Halving(net, KSRC, full, ("c", "x", "y", "a", "b"), (K1, K2, K3, K4, K5), KTOT, OK)
    sa = Halving(net, ASRC, full, ("c", "y", "x", "a", "b"), (A1, A2, A3, A4, A5), ATOT, OA)
    sl = Halving(net, LSRC, own, ("a", "b", "y"), (L1, L2, L3), LTOT, OL)
    weights = load([(FAH, FA), (FKH, FK), (GQH, GQ), (PSH, PS)], lambda j: es.at[2 + j])
    gather.relay()
    OUT[mine_rows, :] = OUTR[...]
    for c in near:
        c.wait()
    sf.push()
    sc.push()

    lane = iota((T, W), 1)
    alane = iota((T, AUG), 1)
    zero = jnp.zeros((T, W), BF)
    azero = jnp.zeros((T, AUG), BF)
    one = jnp.ones((T, 1), F32)
    pad = jnp.zeros((T, AUG - 10), F32)

    def mine_of(a):
        return (lane >= HD * a) & (lane < HD * a + HD)

    def part(ref, g, i=None):
        blk = ref[g % 2, g // 2] if i is None else ref[g % 2, g // 2, :, :, :, :, W * i : W * i + W]
        return blk.reshape(D, blk.shape[-1])

    half = tok // 2

    def attend(i, zz):
        slot = i % 2
        ex = DOB[zz, :, D : D + 2 * AUG].astype(F32)
        for g in range(4):
            QU[g] = QAV[slot, :, W * g : W * g + W]
            DU[g] = DOB[zz, :, W * g : W * g + W]
            QX[g] = jnp.concatenate([ex[:, 9 * g : 9 * g + 9], one, pad], axis=1).astype(BF)
            DX[g] = jnp.concatenate([ex[:, AUG + 9 * g : AUG + 9 * g + 9], one * 0, pad], axis=1).astype(BF)

        def group(g, carry):
            for a in range(3):
                keep = (alane == 9) | ((alane >= 3 * a) & (alane < 3 * a + 3))
                QM[T * a : T * a + T] = jnp.concatenate([jnp.where(mine_of(a), QU[g], zero), jnp.where(keep, QX[g], azero)], axis=1)
                DM[T * a : T * a + T] = jnp.concatenate([jnp.where(mine_of(a), DU[g], zero), jnp.where(keep, DX[g], azero)], axis=1)
            for t in range(0, tok, half):
                kg, vg = KP[slot, g, t : t + half], VP[slot, g, t : t + half]
                for a in range(3):
                    p = jnp.exp(nt(kg, QM[T * a : T * a + T]))
                    ds = p * nt(vg, DM[T * a : T * a + T])
                    DS[t : t + half, T * a : T * a + T] = ds.astype(BF)
                    PB[t : t + half, T * a : T * a + T] = p.astype(BF)
            dk = nn(DS[...], QM[...])
            dv = nn(PB[...], DM[...])
            DKV[zz, g] = jnp.concatenate([dk[:, :W], dv[:, :W]], axis=1).astype(BF)
            dqs = [nn(KT[slot, g, HD * a : HD * a + HD, :], DS[:, T * a : T * a + T]) for a in range(3)]
            DQG[g] = jnp.concatenate(dqs, axis=0).T.astype(BF)
            return carry

        lax.fori_loop(0, 4, group, 0)
        dq = jnp.concatenate([DQG[g] for g in range(4)], axis=1)
        for j in range(4):
            DQS[i, j % 2, j // 2] = dq[R * j : R * j + R]

    q_core, q_x, q_z = {}, {}, {}

    def core_stage(i):
        q_core[i] = net.send(DQS.at[i, 1 - hc], DQC.at[i], head=h ^ 1)

    def x_stage(i):
        q_core[i].wait_recv()
        DQC[i, 1 - hx] = (DQS[i, hc, 1 - hx].astype(F32) + DQC[i, 1 - hx].astype(F32)).astype(BF)
        q_x[i] = net.send(DQC.at[i, 1 - hx], DXR.at[i], head=h ^ 2)
        DOWN[i] = DQS[i, hc, hx].astype(F32) + DQC[i, hx].astype(F32)

    def z_stage(i):
        q_x[i].wait_recv()
        o = DOWN[i] + DXR[i].astype(F32)
        if i < 3:
            DZS[i] = o.astype(BF)
            q_z[i] = net.send(DZS.at[i], DZR.at[i], psg=source(ORDER[i]))
        else:
            DOWN[i] = o

    for i, m in enumerate(ORDER):
        gather.ready(m)
        for c in fetched:
            c.wait()
        if i < 3:
            fetched = fetch(i + 1)
        attend(i, source(m))
        core_stage(i)
        if i >= 1:
            x_stage(i - 1)
        if i >= 2:
            z_stage(i - 2)
        if i == 0:
            sc.pull()
    x_stage(3)
    z_stage(2)
    z_stage(3)

    def et_copy(n):
        return pltpu.make_async_copy(ETH.at[n % 4], ET.at[n % 2], ls.at[4, n % 2])

    et_copy(0).start()
    for c in weights:
        c.wait()
    dq = DOWN[3]
    for i in range(3):
        q_z[i].wait_recv()
        dq += DZR[i].astype(F32)
    dq_low = dq.astype(BF)

    first = FIRST[...]
    gain = gains[1:2].astype(F32)
    n2 = rms_norm(first, gain).astype(BF)
    dn2 = jnp.zeros((R, D), F32)
    for g in range(4):
        dn2 += nt(dq_low[:, W * g : W * g + W], part(FA, g, 1))
    dv, dg2 = rms_back(dn2, first, gain)
    g1 = G2[...] + dv
    g1_low = g1.astype(BF)
    N2[...] = n2
    G1L[...] = g1_low
    for g in range(4):
        DAS[g] = nn(g1_low, part(FA, g, 0)).astype(BF)
    das = [net.send(DAS.at[h ^ m], DA.at[h], head=h ^ m) for m in (2, 3, 1)]
    DA[h] = DAS[h]
    sf.pull()
    sc.pull()

    for g in range(4):
        DQL[g] = dq_low[:, W * g : W * g + W]

    def whole_grads(g, carry):
        acc = jnp.zeros((D, 2 * W), F32)
        for q in range(4):
            et_copy(4 * g + q).wait()

            @pl.when(4 * g + q < 15)
            def _():
                et_copy(4 * g + q + 1).start()

            acc += nn(ET[q % 2], DKV[q, g])
        gc, gx = g % 2, g // 2
        KSRC[gc, gx] = acc.astype(BF).reshape(2, 2, 2, D // 8, 2 * W)
        rest = jnp.concatenate([tn(N2[...], DQL[g]), tn(G1L[...], AO[g])], axis=1)
        ASRC[gc, gx] = rest.astype(BF).reshape(2, 2, 2, D // 8, 2 * W)
        return carry

    lax.fori_loop(0, 4, whole_grads, 0)
    sk.push()
    sa.push()
    for c in das:
        c.wait_recv()

    da = DA[...].reshape(T, W)
    qs, ks, vs = QKV[:, 0:W], QKV[:, W : 2 * W], QKV[:, 2 * W : 3 * W]
    dq1 = jnp.zeros((T, W), F32)
    dk1 = jnp.zeros((T, W), F32)
    dv1 = jnp.zeros((T, W), F32)
    for a in range(3):
        mine = mine_of(a)
        dam = jnp.where(mine, da, zero)
        p = PS[a]
        dp = nt(dam, vs)
        ds = p * (dp - jnp.sum(p * dp, axis=-1, keepdims=True))
        DSF[a] = ds
        dsl = ds.astype(BF)
        dq1 += nn(dsl, jnp.where(mine, ks, zero))
        dk1 += tn(dsl, jnp.where(mine, qs, zero))
        dv1 += tn(p.astype(BF), dam)
    dqkv = jnp.concatenate([dq1, dk1, dv1], axis=1).astype(BF)
    wqkv = GQ[...].reshape(D, 3 * W)
    NS[...] = nt(dqkv, wqkv).astype(BF)
    nr = [net.send(NS.at[pl.ds(pl.multiple_of(R * (h ^ m), R), R)], NR.at[h], head=h ^ m) for m in (2, 3, 1)]
    NR[h] = NS[mine_rows, :]
    sk.pull()
    sa.pull()
    sf.pull()
    sc.pull()
    g0 = gains[0:1].astype(F32)
    n1 = rms_norm(hid[...].astype(F32), g0).astype(BF)
    LSRC[...] = tn(n1, dqkv).astype(BF).reshape(LSRC.shape)
    sl.push()

    step = DEN.shape[1]
    per = tok // step

    def den_copy(n):
        rows = pl.ds(pl.multiple_of(lax.rem(n, per) * step, step), step)
        return pltpu.make_async_copy(DEN.at[lax.rem(n, 2)], DENC.at[n // per, rows], es.at[lax.rem(n, 2)])

    def denc(n, carry):
        rows = pl.ds(pl.multiple_of(lax.rem(n, per) * step, step), step)

        @pl.when(n >= 2)
        def _():
            den_copy(n - 2).wait()

        acc = nt(DKV[n // per, 0, rows, :], part(FK, 0))
        for g in range(1, 4):
            acc += nt(DKV[n // per, g, rows, :], part(FK, g))
        DEN[lax.rem(n, 2)] = acc
        den_copy(n).start()
        return carry

    def dencs(a, b):
        lax.fori_loop(a, b, denc, 0)

    dencs(0, 1)
    sl.pull()
    sk.pull()
    sa.pull()
    sf.pull()
    sc.pull()
    dencs(1, 2)
    for c in nr:
        c.wait_recv()
    dn1 = NR[0].astype(F32) + NR[1].astype(F32) + NR[2].astype(F32) + NR[3].astype(F32)
    dv, dg1 = rms_back(dn1, hid[mine_rows, :].astype(F32), g0)
    DHID[mine_rows, :] = g1 + dv
    dh = [net.send(DHID.at[mine_rows], DHID.at[mine_rows], head=h ^ m) for m in (2, 3, 1)]
    dh += [net.send(OUT.at[mine_rows], OUT.at[mine_rows], head=h ^ m) for m in (2, 3, 1)]
    sc.pull()

    bk = buckets[...]

    def table_step(i, carry):
        hit = bk == i
        for a in range(3):
            TBL[a, pl.ds(i, 1), :] = jnp.sum(jnp.where(hit, DSF[a], 0.0), axis=0, keepdims=True)
        return carry

    nb = TBL.shape[1]
    lax.fori_loop(0, nb, table_step, 0)
    tl = iota((nb, 128), 1)
    tab = jnp.zeros((nb, 128), F32)
    for a in range(3):
        tab = jnp.where(tl == a, jnp.sum(TBL[a], axis=1, keepdims=True), tab)
    tab = jnp.concatenate([tab, jnp.zeros((128 - nb, 128), F32)], axis=0).T[0:8]
    tab = jnp.concatenate([tab, jnp.zeros((8, D - 128), F32)], axis=1)
    dgs = jnp.concatenate([dg1, dg2, DG3[0:1], jnp.zeros((5, D), F32)], axis=0)
    SM[0] = jnp.concatenate([dgs, tab], axis=0)
    srow = iota((16, D), 0)

    def small(j, **dev):
        return net.send(SM.at[j], SMR.at[j], **dev)

    def small_end(j, c, shared):
        c.wait_recv()
        got = SMR[j]
        SM[j + 1] = SM[j] + (got if shared else jnp.where(srow < 8, got, 0.0))

    c = small(0, head=h ^ 1)
    sl.pull()
    sk.pull()
    sa.pull()
    small_end(0, c, False)
    c = small(1, head=h ^ 2)
    dencs(2, 4)
    sl.pull()
    sk.pull()
    sa.pull()
    small_end(1, c, False)
    c = small(2, dp=1 - d)
    dencs(4, 5)
    sk.pull()
    sa.pull()
    small_end(2, c, True)
    c = small(3, psg=z ^ 1)
    dencs(5, 6)
    small_end(3, c, True)
    c = small(4, psg=z ^ 2)
    dencs(6, 4 * per)
    small_end(4, c, True)
    for n in (4 * per - 2, 4 * per - 1):
        den_copy(n).wait()
    for s in (sf, sc, sk, sa, sl):
        s.done()
    for c in dh:
        c.wait_recv()
    net.finish()


def call_two(buckets, gains, hid, kept, rows):
    T, D = hid.shape
    R = T // 4
    W = 3 * HD
    k = kept
    tok = k["ET"].shape[2]
    F3 = k["GF"].shape[4]
    S = jax.ShapeDtypeStruct
    blk = D // 8
    outs = dict(
        DENC=((4, tok, D), F32), DHID=((T, D), F32), OUT=((T, D), F32), SM=((6, 16, D), F32),
        OF=((4, rows, F3), F32), OC=((4, rows, W), F32), OK=((4, rows, 2 * W), F32), OA=((4, rows, 2 * W), F32),
        OL=((4, rows, 3 * W), F32),
    )

    def halving(n, w):
        return [VMEM((2,) * k + (blk, w), BF) for k in (n, *range(n - 1, -1, -1))] + [VMEM((blk, w), F32)]

    def like(n, *lead):
        return VMEM((*lead, *k[n].shape[1:]) if lead else k[n].shape, k[n].dtype)

    scratch = [
        VMEM((4, T, D + 2 * AUG), BF), like("KP", 2), like("VP", 2), like("KT", 2), like("QA", 2), like("ET", 2),
        like("FA"), like("FK"), like("GQ"), like("PS"),
        VMEM((4, T, W), BF), VMEM((4, T, W), BF), VMEM((4, T, AUG), BF), VMEM((4, T, AUG), BF),
        VMEM((3 * T, W + AUG), BF), VMEM((3 * T, W + AUG), BF), VMEM((tok, 3 * T), BF), VMEM((tok, 3 * T), BF),
        VMEM((4, T, W), BF), VMEM((4, 4, tok, 2 * W), BF),
        VMEM((4, 2, 2, R, D), BF), VMEM((4, 2, R, D), BF), VMEM((4, R, D), BF), VMEM((4, R, D), F32),
        VMEM((3, R, D), BF), VMEM((3, R, D), BF), VMEM((4, R, W), BF), VMEM((4, R, W), BF),
        VMEM((3, T, T), F32), VMEM((3, 32, T), F32), VMEM((T, D), BF), VMEM((4, R, D), BF), VMEM((2, tok // 2, D), F32),
        *halving(3, F3), *halving(5, W), *halving(5, 2 * W), *halving(5, 2 * W), *halving(3, 3 * W),
        VMEM((5, 16, D), F32), VMEM((4, R, W), BF), VMEM((R, D), BF), VMEM((R, D), BF),
        pltpu.SemaphoreType.DMA((120,)), pltpu.SemaphoreType.DMA((120,)), pltpu.SemaphoreType.DMA((5, 2)), pltpu.SemaphoreType.DMA((6,)),
    ]
    vm = pl.BlockSpec(memory_space=pltpu.VMEM)
    anym = pl.BlockSpec(memory_space=pl.ANY)
    names = ("ET", "FA", "FK", "GQ", "QA", "KP", "VP", "KT", "PS", "QKV", "AO", "FIRST", "G2", "DO", "GC", "GF", "DG3", "OUT")
    far = ("ET", "FA", "FK", "GQ", "QA", "KP", "VP", "KT", "PS", "GC", "GF")
    res = pl.pallas_call(
        kernel_two,
        out_shape=[S(*v) for v in outs.values()],
        in_specs=[vm] * 3 + [anym if n in far else vm for n in names],
        out_specs=[anym] + [vm] * (len(outs) - 1),
        scratch_shapes=scratch,
        name="backward",
        compiler_params=pltpu.CompilerParams(collective_id=2, has_side_effects=True, vmem_limit_bytes=63 << 20),
    )(buckets, gains, hid, *[k[n] for n in names])
    return dict(zip(outs, res))


def local_fast(
    hidden_in, encodings, passage_lengths, target_lengths, rel_buckets, gains, rel_table, *rest
):
    mats, cot = rest[:11], rest[11]
    span, passages, group, D = encodings.shape
    rows = mats[0].shape[0]
    W = 3 * HD
    F = mats[8].shape[1] // 4
    count = span * passages
    padded = -(-count // 128) * 128
    enc = jnp.transpose(encodings, (2, 1, 0, 3)).reshape(group, count, D)
    enc = jnp.pad(enc, ((0, 0), (0, padded - count), (0, 0)))
    hid = hidden_in[0]
    kept = call_one(
        passage_lengths.T, target_lengths, rel_table.T, hid, enc, rel_buckets, gains, mats, cot[0]
    )
    r = call_two(rel_buckets, gains, hid, kept, rows)
    d_enc = jnp.transpose(r["DENC"][:, :count].reshape(group, passages, span, D), (2, 1, 0, 3))

    def columns(a, at, w):
        return jnp.transpose(a[:, :, at : at + w], (1, 0, 2)).reshape(rows, 4 * w)

    small = r["SM"][5]
    OF, OC, OK, OA, OL = (r[n] for n in ("OF", "OC", "OK", "OA", "OL"))
    return (
        r["OUT"][None], r["DHID"][None], d_enc, small[0:3],
        jnp.transpose(small[8:11, : rel_table.shape[0]]),
        columns(OL, 0, W), columns(OL, W, W), columns(OL, 2 * W, W), columns(OA, W, W),
        columns(OA, 0, W), columns(OK, 0, W), columns(OK, W, W), columns(OC, 0, W),
        columns(OF, 0, F), columns(OF, F, F), columns(OF, 2 * F, F),
    )


def merged(part, axis, combine):
    gathered = jax.tree.map(lambda a: lax.all_gather(a, axis), part)

    def take(source):
        return jax.tree.map(lambda a: lax.dynamic_index_in_dim(a, source, 0, False), gathered)

    return lax.fori_loop(
        1, lax.axis_size(axis), lambda source, state: combine(state, take(source)), take(0)
    )


def rms_plain(values, gain):
    return values * lax.rsqrt(jnp.mean(values * values, axis=-1, keepdims=True) + EPSILON) * gain


def gated(gate_in, up_in):
    return jax.nn.gelu(gate_in, approximate=True) * up_in


def over_heads(partial_value):
    return lax.psum(partial_value, "head")


def own_columns(matrix, index, width):
    return lax.dynamic_slice_in_dim(matrix, index * width, width, 1)


def left_mul(left, matrix):
    return jnp.einsum("qtd,dc->qtc", left, matrix, preferred_element_type=jnp.float32)


def right_mul(left, matrix):
    return jnp.einsum("qtc,dc->qtd", left, matrix, preferred_element_type=jnp.float32)


def row_outer(left, right):
    return jnp.einsum("qtd,qtc->dc", left, right, preferred_element_type=jnp.float32)


def local_plain(
    hidden_in,
    encodings,
    passage_lengths,
    target_lengths,
    rel_buckets,
    gains,
    rel_table,
    self_q,
    self_k,
    self_v,
    self_o,
    cross_q,
    cross_k,
    cross_v,
    cross_o,
    ff_gate,
    ff_up,
    ff_down,
    cotangent,
):
    gathered = (
        lax.all_gather(self_q, ("dp", "psg", "head"), axis=0, tiled=True),
        lax.all_gather(self_k, ("dp", "psg", "head"), axis=0, tiled=True),
        lax.all_gather(self_v, ("dp", "psg", "head"), axis=0, tiled=True),
        lax.all_gather(self_o, ("dp", "psg", "head"), axis=0, tiled=True),
        lax.all_gather(cross_q, ("dp", "psg", "head"), axis=0, tiled=True),
        lax.all_gather(cross_k, ("dp", "psg", "head"), axis=0, tiled=True),
        lax.all_gather(cross_v, ("dp", "psg", "head"), axis=0, tiled=True),
        lax.all_gather(cross_o, ("dp", "psg", "head"), axis=0, tiled=True),
        lax.all_gather(ff_gate, ("dp", "psg", "head"), axis=0, tiled=True),
        lax.all_gather(ff_up, ("dp", "psg", "head"), axis=0, tiled=True),
        lax.all_gather(ff_down, ("dp", "psg", "head"), axis=0, tiled=True),
    )
    (
        self_query,
        self_key,
        self_value,
        self_out,
        cross_query,
        cross_key,
        cross_value,
        cross_out,
        gate_full,
        up_full,
        down_full,
    ) = gathered
    head_index = lax.axis_index("head")
    heads_local = rel_table.shape[1]
    width = heads_local * HD
    total_width = self_query.shape[1]
    ff_total = gate_full.shape[1]
    ff_local = ff_total // lax.axis_size("head")
    query_rows = hidden_in.shape[0]
    target_span = hidden_in.shape[1]
    hidden = hidden_in.astype(jnp.float32)
    gain_all = gains.astype(jnp.float32)
    qkv_weight = jnp.concatenate(
        [
            own_columns(self_query, head_index, width),
            own_columns(self_key, head_index, width),
            own_columns(self_value, head_index, width),
        ],
        axis=1,
    )
    normed_one = rms_plain(hidden, gain_all[0]).astype(jnp.bfloat16)
    qkv_self = left_mul(normed_one, qkv_weight).astype(jnp.bfloat16)
    queries_self = qkv_self[..., :width].reshape(query_rows, target_span, heads_local, HD)
    keys_self = qkv_self[..., width : 2 * width].reshape(query_rows, target_span, heads_local, HD)
    values_self = qkv_self[..., 2 * width :].reshape(query_rows, target_span, heads_local, HD)
    positions = jnp.arange(target_span)
    causal = (positions[None, None, :] <= positions[None, :, None]) & (
        positions[None, None, :] < target_lengths[:, None, None]
    )
    buckets_hot = (rel_buckets[:, :, None] == jnp.arange(rel_table.shape[0])[None, None, :]).astype(
        jnp.float32
    )
    bias = jnp.einsum(
        "ijb,bh->hij", buckets_hot, rel_table.astype(jnp.float32), precision=lax.Precision.HIGHEST
    )
    scores_self = jnp.einsum(
        "qihd,qjhd->qhij", queries_self, keys_self, preferred_element_type=jnp.float32
    )
    scores_self = jnp.where(causal[:, None], scores_self + bias[None], NEGATIVE)
    probs_self = jax.nn.softmax(scores_self, axis=-1)
    probs_self_low = probs_self.astype(jnp.bfloat16)
    attn_one = jnp.einsum(
        "qhij,qjhd->qihd", probs_self_low, values_self, preferred_element_type=jnp.float32
    )
    attn_one = attn_one.reshape(query_rows, target_span, width).astype(jnp.bfloat16)
    self_out_own = own_columns(self_out, head_index, width)
    first = hidden + over_heads(right_mul(attn_one, self_out_own))
    normed_two = rms_plain(first, gain_all[1]).astype(jnp.bfloat16)
    cross_query_own = own_columns(cross_query, head_index, width)
    query_cross = left_mul(normed_two, cross_query_own).astype(jnp.bfloat16)
    query_group = lax.all_gather(query_cross, "psg", axis=0, tiled=True)
    group_count = query_group.shape[0]
    head_parts = lax.axis_size("head")
    kv_split = jnp.concatenate(
        [
            cross_key.reshape(cross_key.shape[0], head_parts, width),
            cross_value.reshape(cross_value.shape[0], head_parts, width),
        ],
        axis=2,
    )
    local_kv = jnp.einsum(
        "tpqd,dgc->qptgc", encodings, kv_split, preferred_element_type=jnp.float32
    ).astype(jnp.bfloat16)
    moved_kv = lax.all_to_all(local_kv, "head", split_axis=3, concat_axis=2, tiled=True)
    key_value = moved_kv.reshape(moved_kv.shape[0], moved_kv.shape[1], moved_kv.shape[2], 2 * width)
    passages_local = key_value.shape[1]
    passage_span = key_value.shape[2]
    key_count = passages_local * passage_span
    kv_flat = key_value.reshape(group_count, key_count, 2 * width)
    span = jnp.arange(passage_span)
    key_valid = (span[None, None, :] < jnp.transpose(passage_lengths)[:, :, None]).reshape(
        group_count, key_count
    )

    def masked_scores(query_block, kv_block, valid_block):
        query_heads = query_block.reshape(target_span, heads_local, HD)
        keys_part = kv_block[:, :width].reshape(key_count, heads_local, HD)
        raw = jnp.einsum("ihd,jhd->hij", query_heads, keys_part, preferred_element_type=jnp.float32)
        return jnp.where(valid_block[None, None, :], raw, NEGATIVE)

    def stats_one(item):
        masked = masked_scores(item[0], item[1], item[2])
        largest = jnp.max(masked, axis=-1)
        total = jnp.sum(jnp.exp(masked - largest[..., None]), axis=-1)
        return (largest, total)

    tops, totals = lax.map(stats_one, (query_group, kv_flat, key_valid))

    def combine(pair_one, pair_two):
        larger = jnp.maximum(pair_one[0], pair_two[0])
        return (
            larger,
            pair_one[1] * jnp.exp(pair_one[0] - larger)
            + pair_two[1] * jnp.exp(pair_two[0] - larger),
        )

    tops, totals = merged((tops, totals), "psg", combine)
    log_total = tops + jnp.log(totals)

    def values_one(item):
        masked = masked_scores(item[0], item[1], item[2])
        probs_low = jnp.exp(masked - item[3][..., None]).astype(jnp.bfloat16)
        values_part = item[1][:, width:].reshape(key_count, heads_local, HD)
        weighted = jnp.einsum(
            "hij,jhd->ihd", probs_low, values_part, preferred_element_type=jnp.float32
        )
        return weighted.reshape(target_span, width)

    partial_out = lax.map(values_one, (query_group, kv_flat, key_valid, log_total))
    attn_two = lax.psum_scatter(partial_out, "psg", scatter_dimension=0, tiled=True).astype(
        jnp.bfloat16
    )
    cross_out_own = own_columns(cross_out, head_index, width)
    second = first + over_heads(right_mul(attn_two, cross_out_own))
    normed_three = rms_plain(second, gain_all[2]).astype(jnp.bfloat16)
    ff_weight = jnp.concatenate(
        [own_columns(gate_full, head_index, ff_local), own_columns(up_full, head_index, ff_local)],
        axis=1,
    )
    gate_up = left_mul(normed_three, ff_weight)
    gate_part = gate_up[..., :ff_local]
    up_part = gate_up[..., ff_local:]
    activated = gated(gate_part, up_part).astype(jnp.bfloat16)
    down_own = own_columns(down_full, head_index, ff_local)
    output = second + over_heads(right_mul(activated, down_own))
    row_valid = (positions[None, :] < target_lengths[:, None])[:, :, None]
    out_hidden = jnp.where(row_valid, output, 0.0)
    grad_out = jnp.where(row_valid, cotangent.astype(jnp.float32), 0.0)
    grad_out_low = grad_out.astype(jnp.bfloat16)
    grad_down = row_outer(grad_out_low, activated)
    grad_act = left_mul(grad_out_low, down_own)
    gate_value, pull_gate = jax.vjp(gated, gate_part, up_part)
    grad_gate, grad_up = pull_gate(grad_act)
    grad_gate_up = jnp.concatenate([grad_gate, grad_up], axis=-1).astype(jnp.bfloat16)
    grad_ff_weight = row_outer(normed_three, grad_gate_up)
    grad_normed_three = over_heads(right_mul(grad_gate_up, ff_weight))
    norm_value, pull_three = jax.vjp(rms_plain, second, gain_all[2])
    grad_second_norm, grad_gain_three = pull_three(grad_normed_three)
    grad_two = grad_out + grad_second_norm
    grad_two_low = grad_two.astype(jnp.bfloat16)
    grad_cross_out = row_outer(grad_two_low, attn_two)
    grad_attn_two = left_mul(grad_two_low, cross_out_own).astype(jnp.bfloat16)
    grad_attn_group = lax.all_gather(grad_attn_two, "psg", axis=0, tiled=True)

    def prob_pieces(item):
        masked = masked_scores(item[0], item[1], item[2])
        probs = jnp.exp(masked - item[3][..., None])
        values_part = item[1][:, width:].reshape(key_count, heads_local, HD)
        grad_rows = item[4].reshape(target_span, heads_local, HD)
        grad_probs = jnp.einsum(
            "ihd,jhd->hij", grad_rows, values_part, preferred_element_type=jnp.float32
        )
        return (probs, grad_probs)

    def delta_one(item):
        probs, grad_probs = prob_pieces(item)
        return jnp.sum(probs * grad_probs, axis=-1)

    delta_part = lax.map(delta_one, (query_group, kv_flat, key_valid, log_total, grad_attn_group))
    delta = lax.psum(delta_part, "psg")

    def grads_one(item):
        probs, grad_probs = prob_pieces(item[:5])
        grad_scores = (probs * (grad_probs - item[5][..., None])).astype(jnp.bfloat16)
        probs_low = probs.astype(jnp.bfloat16)
        query_heads = item[0].reshape(target_span, heads_local, HD)
        keys_part = item[1][:, :width].reshape(key_count, heads_local, HD)
        grad_rows = item[4].reshape(target_span, heads_local, HD)
        grad_query = jnp.einsum(
            "hij,jhd->ihd", grad_scores, keys_part, preferred_element_type=jnp.float32
        )
        grad_keys = jnp.einsum(
            "hij,ihd->jhd", grad_scores, query_heads, preferred_element_type=jnp.float32
        )
        grad_values = jnp.einsum(
            "hij,ihd->jhd", probs_low, grad_rows, preferred_element_type=jnp.float32
        )
        grad_kv = jnp.concatenate(
            [grad_keys.reshape(key_count, width), grad_values.reshape(key_count, width)], axis=-1
        ).astype(jnp.bfloat16)
        return (grad_query.reshape(target_span, width), grad_kv)

    grad_query_group, grad_kv_flat = lax.map(
        grads_one, (query_group, kv_flat, key_valid, log_total, grad_attn_group, delta)
    )
    grad_query_cross = lax.psum_scatter(
        grad_query_group, "psg", scatter_dimension=0, tiled=True
    ).astype(jnp.bfloat16)
    grad_cross_query = row_outer(normed_two, grad_query_cross)
    grad_normed_two = over_heads(right_mul(grad_query_cross, cross_query_own))
    norm_value_two, pull_two = jax.vjp(rms_plain, first, gain_all[1])
    grad_first_norm, grad_gain_two = pull_two(grad_normed_two)
    grad_one = grad_two + grad_first_norm
    grad_kv = grad_kv_flat.reshape(group_count, passages_local, passage_span, 2 * width)
    grad_back = lax.all_to_all(
        grad_kv.reshape(group_count, passages_local, passage_span, 1, 2 * width),
        "head",
        split_axis=2,
        concat_axis=3,
        tiled=True,
    )
    d_encodings = jnp.einsum(
        "qptgc,dgc->tpqd", grad_back, kv_split, preferred_element_type=jnp.float32
    )
    grad_split = jnp.einsum(
        "tpqd,qptgc->dgc", encodings, grad_back, preferred_element_type=jnp.float32
    )
    grad_cross_key = grad_split[:, :, :width].reshape(grad_split.shape[0], total_width)
    grad_cross_value = grad_split[:, :, width:].reshape(grad_split.shape[0], total_width)
    grad_one_low = grad_one.astype(jnp.bfloat16)
    grad_self_out = row_outer(grad_one_low, attn_one)
    grad_attn_one = left_mul(grad_one_low, self_out_own).astype(jnp.bfloat16)
    grad_attn_one = grad_attn_one.reshape(query_rows, target_span, heads_local, HD)
    grad_probs_self = jnp.einsum(
        "qihd,qjhd->qhij", grad_attn_one, values_self, preferred_element_type=jnp.float32
    )
    grad_scores_self = probs_self * (
        grad_probs_self - jnp.sum(probs_self * grad_probs_self, axis=-1, keepdims=True)
    )
    grad_table = jnp.einsum(
        "ijb,hij->bh",
        buckets_hot,
        jnp.sum(grad_scores_self, axis=0),
        precision=lax.Precision.HIGHEST,
    )
    grad_scores_low = grad_scores_self.astype(jnp.bfloat16)
    grad_query_self = jnp.einsum(
        "qhij,qjhd->qihd", grad_scores_low, keys_self, preferred_element_type=jnp.float32
    )
    grad_key_self = jnp.einsum(
        "qhij,qihd->qjhd", grad_scores_low, queries_self, preferred_element_type=jnp.float32
    )
    grad_value_self = jnp.einsum(
        "qhij,qihd->qjhd", probs_self_low, grad_attn_one, preferred_element_type=jnp.float32
    )
    grad_qkv = jnp.concatenate(
        [
            grad_query_self.reshape(query_rows, target_span, width),
            grad_key_self.reshape(query_rows, target_span, width),
            grad_value_self.reshape(query_rows, target_span, width),
        ],
        axis=-1,
    ).astype(jnp.bfloat16)
    grad_qkv_weight = row_outer(normed_one, grad_qkv)
    grad_normed_one = over_heads(right_mul(grad_qkv, qkv_weight))
    norm_value_one, pull_one = jax.vjp(rms_plain, hidden, gain_all[0])
    grad_hidden_norm, grad_gain_one = pull_one(grad_normed_one)
    d_hidden = grad_one + grad_hidden_norm
    grad_gains = jnp.stack([grad_gain_one, grad_gain_two, grad_gain_three])
    d_gains, d_rel_table = lax.psum((grad_gains, grad_table), ("dp", "psg"))
    own_grads = [
        grad_qkv_weight[:, :width],
        grad_qkv_weight[:, width : 2 * width],
        grad_qkv_weight[:, 2 * width :],
        grad_self_out,
        grad_cross_query,
        grad_cross_out,
        grad_ff_weight[:, :ff_local],
        grad_ff_weight[:, ff_local:],
        grad_down,
    ]
    row_sums = lax.psum_scatter(tuple(own_grads), ("dp", "psg"), scatter_dimension=0, tiled=True)
    owned = (
        lax.all_to_all(row_sums[0], "head", split_axis=0, concat_axis=1, tiled=True),
        lax.all_to_all(row_sums[1], "head", split_axis=0, concat_axis=1, tiled=True),
        lax.all_to_all(row_sums[2], "head", split_axis=0, concat_axis=1, tiled=True),
        lax.all_to_all(row_sums[3], "head", split_axis=0, concat_axis=1, tiled=True),
        lax.all_to_all(row_sums[4], "head", split_axis=0, concat_axis=1, tiled=True),
        lax.all_to_all(row_sums[5], "head", split_axis=0, concat_axis=1, tiled=True),
        lax.all_to_all(row_sums[6], "head", split_axis=0, concat_axis=1, tiled=True),
        lax.all_to_all(row_sums[7], "head", split_axis=0, concat_axis=1, tiled=True),
        lax.all_to_all(row_sums[8], "head", split_axis=0, concat_axis=1, tiled=True),
    )
    key_done, value_done = (
        lax.psum_scatter(grad_cross_key, ("dp", "psg", "head"), scatter_dimension=0, tiled=True),
        lax.psum_scatter(grad_cross_value, ("dp", "psg", "head"), scatter_dimension=0, tiled=True),
    )
    return (
        out_hidden,
        d_hidden,
        d_encodings,
        d_gains,
        d_rel_table,
        owned[0],
        owned[1],
        owned[2],
        owned[3],
        owned[4],
        key_done,
        value_done,
        owned[5],
        owned[6],
        owned[7],
        owned[8],
    )


PLACED = (
    P(("dp", "psg"), None, None),
    P("head", "psg", "dp", None),
    P("psg", "dp"),
    P(("dp", "psg")),
    P(),
    P(),
    P(None, "head"),
    P(("dp", "psg", "head"), None),
    P(("dp", "psg", "head"), None),
    P(("dp", "psg", "head"), None),
    P(("dp", "psg", "head"), None),
    P(("dp", "psg", "head"), None),
    P(("dp", "psg", "head"), None),
    P(("dp", "psg", "head"), None),
    P(("dp", "psg", "head"), None),
    P(("dp", "psg", "head"), None),
    P(("dp", "psg", "head"), None),
    P(("dp", "psg", "head"), None),
    P(("dp", "psg"), None, None),
)

OUTS = (
    P(("dp", "psg"), None, None),
    P(("dp", "psg"), None, None),
    P("head", "psg", "dp", None),
    P(),
    P(None, "head"),
    P(("dp", "psg", "head"), None),
    P(("dp", "psg", "head"), None),
    P(("dp", "psg", "head"), None),
    P(("dp", "psg", "head"), None),
    P(("dp", "psg", "head"), None),
    P(("dp", "psg", "head"), None),
    P(("dp", "psg", "head"), None),
    P(("dp", "psg", "head"), None),
    P(("dp", "psg", "head"), None),
    P(("dp", "psg", "head"), None),
    P(("dp", "psg", "head"), None),
)


def solution(mesh):
    def local(*args):
        rows, span, heads = args[7].shape[0], args[1].shape[0], args[6].shape[1]
        fits = (mesh.shape["dp"], mesh.shape["psg"], mesh.shape["head"], heads) == (2, 4, 4, 3)
        fits = fits and (4 * rows) % 16 == 0 and rows % 8 == 0
        return (local_fast if fits else local_plain)(*args)

    placed = PLACED
    return jax.shard_map(local, mesh=mesh, in_specs=placed, out_specs=OUTS, check_vma=False)
```

```python
import functools

import jax
import jax.numpy as jnp
from jax import lax
from jax.experimental import pallas as pl
from jax.experimental.pallas import tpu as pltpu
from jax.sharding import PartitionSpec as P

HD = 64
EPSILON = 1e-06
NEGATIVE = -1e30
AUG = 64
BF = jnp.bfloat16
F32 = jnp.float32
MESH = pl.DeviceIdType.MESH
VMEM = pltpu.VMEM


def nn(a, b):
    return lax.dot_general(a, b, (((1,), (0,)), ((), ())), preferred_element_type=F32)


def nt(a, b):
    return lax.dot_general(a, b, (((1,), (1,)), ((), ())), preferred_element_type=F32)


def tn(a, b):
    return lax.dot_general(a, b, (((0,), (0,)), ((), ())), preferred_element_type=F32)


def rms_scale(v):
    return lax.rsqrt(jnp.mean(v * v, axis=-1, keepdims=True) + EPSILON)


def rms_norm(v, gain):
    return v * rms_scale(v) * gain


def rms_back(dn, v, gain):
    r = rms_scale(v)
    gd = gain * dn
    dv = r * gd - v * (r * r * r * jnp.mean(gd * v, axis=-1, keepdims=True))
    dg = jnp.sum(dn * v * r, axis=0, keepdims=True)
    return dv, dg


def iota(shape, axis):
    return lax.broadcasted_iota(jnp.int32, shape, axis)


class Net:
    def __init__(self, send_sems, recv_sems):
        self.send_sems, self.recv_sems, self.count, self.sent = send_sems, recv_sems, 0, []

    def send(self, src, dst, **device):
        at = self.count
        self.count += 1
        copy = pltpu.make_async_remote_copy(
            src, dst, self.send_sems.at[at], self.recv_sems.at[at],
            device_id=device, device_id_type=MESH,
        )
        copy.start()
        self.sent.append(copy)
        return copy

    def finish(self):
        for copy in self.sent:
            copy.wait_send()


def places():
    d, z, h = lax.axis_index("dp"), lax.axis_index("psg"), lax.axis_index("head")
    return dict(
        c=(h % 2, dict(head=h ^ 1)), x=(h // 2, dict(head=h ^ 2)), y=(d, dict(dp=1 - d)),
        a=(z // 2, dict(psg=z ^ 3)), b=(z % 2, dict(psg=z ^ 1)),
    )


class Doubling:
    def __init__(self, net, ref, names, order, late=()):
        self.net, self.ref, self.names, self.order, self.at = net, ref, names, order, places()
        self.late = [order.index(n) + 1 for n in late]
        self.sent = {s: [] if s in self.late else [self.go(0, s)] for s in range(1, len(order) + 1)}

    def region(self, j):
        idx = []
        for n in self.names:
            p, mine = self.order.index(n) + 1, self.at[n][0]
            idx.append(mine if p > j else (1 - mine if p == j else slice(None)))
        return self.ref.at[tuple(idx)]

    def go(self, j, s):
        block = self.region(j)
        return self.net.send(block, block, **self.at[self.order[s - 1]][1])

    def open(self, name, have):
        s = self.order.index(name) + 1
        self.late.remove(s)
        self.sent[s] = [self.go(i, s) for i in range(have + 1)]

    def step(self, name):
        j = self.order.index(name) + 1
        for c in self.sent[j]:
            c.wait_recv()
        for s in range(j + 1, len(self.order) + 1):
            if s not in self.late:
                self.sent[s].append(self.go(j, s))
            elif s == j + 1:
                self.sent[s] = [self.go(i, s) for i in range(s)]


class Halving:
    def __init__(self, net, src, names, order, bufs, total, shard):
        self.net, self.src, self.names, self.order, self.bufs = net, src, names, order, bufs
        self.total, self.shard, self.at, self.stage = total, shard, places(), 0

    def index(self, stage, last, free):
        idx, free = [], list(free)
        for n in self.names:
            p, mine = self.order.index(n), self.at[n][0]
            idx.append(mine if p < stage else (last(mine) if p == stage else free.pop(0)))
        return tuple(idx)

    def push(self):
        n = len(self.order) - self.stage - 1
        far = self.src.at[self.index(self.stage, lambda m: 1 - m, [slice(None)] * n)]
        self.copy = self.net.send(far, self.bufs[self.stage], **self.at[self.order[self.stage]][1])

    def pull(self):
        self.copy.wait_recv()
        n = len(self.order) - self.stage - 1
        buf = self.bufs[self.stage]
        if n == 0:
            idx = self.index(self.stage, lambda m: m, [])
            self.total[...] = self.src[idx].astype(F32) + buf[...].astype(F32)
        else:
            def add(i, carry):
                bits = [(i // 2**k) % 2 for k in range(n)]
                idx = self.index(self.stage, lambda m: m, bits)
                self.src[idx] = (self.src[idx].astype(F32) + buf[tuple(bits)].astype(F32)).astype(BF)
                return carry

            lax.fori_loop(0, 2**n, add, 0)
        self.stage += 1
        if n:
            self.push()
        else:
            self.trade()

    def trade(self):
        n, h = self.shard.shape[1], lax.axis_index("head")

        def rows(hh):
            return pl.ds(pl.multiple_of(n * hh, n), n)

        self.last = [self.net.send(self.total.at[rows(h ^ m)], self.shard.at[h], head=h ^ m) for m in (2, 3, 1)]
        self.shard[h] = self.total[rows(h), :]

    def done(self):
        for c in self.last:
            c.wait_recv()


def enter():
    barrier = pltpu.get_barrier_semaphore()
    d, z, h = lax.axis_index("dp"), lax.axis_index("psg"), lax.axis_index("head")
    peers = [dict(head=h ^ m) for m in (1, 2, 3)]
    peers += [dict(psg=lax.rem(z + m, 4)) for m in (1, 2, 3)]
    peers += [dict(dp=1 - d)]
    for peer in peers:
        pl.semaphore_signal(barrier, inc=1, device_id=peer, device_id_type=MESH)
    pl.semaphore_wait(barrier, len(peers))
    return d, z, h


ORDER = (1, 3, 2, 0)


class Gather:
    def __init__(self, net, buf, z, h, rows):
        self.net, self.buf, self.z, self.h, self.rows = net, buf, z, h, rows
        mine = self.at(z, h)
        self.ring = {m: net.send(mine, mine, psg=lax.rem(z + m, 4)) for m in (1, 3, 2)}
        self.hops = {0: self.on(z)}
        self.last = {}

    def at(self, zz, hh):
        return self.buf.at[zz, pl.ds(pl.multiple_of(self.rows * hh, self.rows), self.rows)]

    def on(self, zz):
        block = self.at(zz, self.h)
        return [self.net.send(block, block, head=self.h ^ 2), self.net.send(block, block, head=self.h ^ 1)]

    def source(self, m):
        return lax.rem(self.z - m + 4, 4)

    def relay(self):
        for m in (1, 3, 2):
            self.ring[m].wait_recv()
            self.hops[m] = self.on(self.source(m))
        for m in ORDER:
            self.hops[m][0].wait_recv()
            block = self.at(self.source(m), self.h ^ 2)
            self.last[m] = self.net.send(block, block, head=self.h ^ 1)

    def ready(self, m):
        self.hops[m][1].wait_recv()
        self.last[m].wait_recv()


def kernel_one(
    plen, tlen,
    table, hid, ench, buckets, gains, sq, sk, sv, so, cq, ck, cv, co, fg, fu, fd, cot,
    FAH, FKH, GQH, KPH, VPH, KTH, ETH, PSH, QA, QKV, AOS, FIRST, G2, DO, GFH, DG3, OUT, N2, ATO,
    PQ, PA, PK, PC, PG, AQ, AA, AK, AC, AG,
    FA, FK, FC, GQ, GG, KP, VP, KT, VT, ET, PS, AO, GF,
    enc, QU, BIAS, OS, ST, OC, SC, OXS, SXS, OX, SX, OZS, SZS, OZ, SZ,
    OWN, SOWN, ATS, AT, N3, R3S, R3, R1S, R1, QM,
    ss, rs, ls,
):
    d, z, h = enter()
    net = Net(ss, rs)
    T, D = hid.shape
    R = T // 4
    W = 3 * HD
    hc, hx = h % 2, h // 2
    e = 1 - d
    zp, zm, zo = lax.rem(z + 1, 4), lax.rem(z + 3, 4), lax.rem(z + 2, 4)
    kept = []

    def keep_out(src, dst):
        c = pltpu.make_async_copy(src, dst, ls.at[len(kept)])
        c.start()
        kept.append(c)

    count = ench.shape[1]
    e_load = pltpu.make_async_copy(ench, enc.at[:, pl.ds(0, count)], ls.at[11])
    e_load.start()

    mats = {n: r[...].astype(F32) for n, r in dict(sq=sq, sk=sk, sv=sv, so=so, cq=cq, ck=ck, cv=cv, co=co).items()}
    F = fg.shape[1] // 4

    def pack(dst, names):
        for g in range(4):
            s = slice(W * g, W * g + W)
            parts = [mats[n][:, s] for n in names]
            dst[g] = (jnp.concatenate(parts, axis=1) if len(parts) > 1 else parts[0]).astype(BF)

    def trade(src, dst):
        cs = [net.send(src.at[h ^ m], dst.at[h], head=h ^ m) for m in (2, 3, 1)]
        dst[h] = src[h]
        return cs

    pack(PQ, ("sq", "sk", "sv"))
    tq = trade(PQ, AQ)
    pack(PA, ("so", "cq"))
    ta = trade(PA, AA)
    pack(PK, ("ck", "cv"))
    tk = trade(PK, AK)
    pack(PC, ("co",))
    for g in range(4):
        for i, ref in enumerate((fg, fu, fd)):
            PG[g, :, F * i : F * i + F] = ref[:, F * g : F * g + F]
    tc = trade(PC, AC)
    tg = trade(PG, AG)

    def assemble(cs, src, dst):
        for c in cs:
            c.wait_recv()
        dst[...] = jnp.concatenate([src[j].astype(F32) for j in range(4)], axis=0).astype(BF)

    full, own = ("c", "x", "y", "a", "b"), ("y", "a", "b")
    za, zb = z // 2, z % 2
    assemble(tq, AQ, GQ.at[d, za, zb])
    wq = Doubling(net, GQ, own, ("b", "a", "y"))
    assemble(ta, AA, FA.at[hc, hx, d, za, zb])
    wa = Doubling(net, FA, full, ("b", "a", "x", "y", "c"))
    assemble(tk, AK, FK.at[hc, hx, d, za, zb])
    wk = Doubling(net, FK, full, ("b", "a", "y", "x", "c"))
    g0 = gains[0:1].astype(F32)
    hidden = hid[...].astype(F32)
    n1 = rms_norm(hidden, g0).astype(BF)

    def flip(q, carry):
        ET[q] = enc[q].astype(F32).T.astype(BF)
        return carry

    assemble(tc, AC, FC.at[hc, hx, d, za, zb])
    assemble(tg, AG, GG.at[d, za, zb])
    for w in (wq, wk, wa):
        w.step("b")
    e_load.wait()
    enc[:, count:, :] = jnp.zeros((enc.shape[0], enc.shape[1] - count, D), BF)
    lax.fori_loop(0, 2, flip, 0)
    for w in (wq, wa, wk):
        w.step("a")
    wc = Doubling(net, FC, full, ("b", "a", "y", "x", "c"), ("x", "c"))
    wg = Doubling(net, GG, own, ("b", "a", "y"), ("y",))
    lax.fori_loop(2, 4, flip, 0)
    bk = buckets[...]
    tab = table[...].astype(F32)
    for a in range(3):
        acc = jnp.zeros((T, T), F32)
        for i in range(tab.shape[1]):
            acc = jnp.where(bk == i, tab[a : a + 1, i : i + 1], acc)
        BIAS[a] = acc
    wa.step("x")
    wk.step("y")
    wg.open("y", 0)
    wq.step("y")

    wqkv = GQ[...].reshape(D, 3 * W)
    QKV[...] = nn(n1, wqkv).astype(BF)
    keep_out(GQ, GQH)
    wk.step("x")
    wc.step("b")
    wg.step("b")
    qs, ks, vs = QKV[:, 0:W], QKV[:, W : 2 * W], QKV[:, 2 * W : 3 * W]
    lane = iota((T, W), 1)
    row, col = iota((T, T), 0), iota((T, T), 1)
    keep = (col <= row) & (col < tlen[0])
    acc = jnp.zeros((T, W), F32)
    zero = jnp.zeros((T, W), BF)
    for a in range(3):
        mine = (lane >= HD * a) & (lane < HD * a + HD)
        s = nt(jnp.where(mine, qs, zero), ks) + BIAS[a]
        s = jnp.where(keep, s, NEGATIVE)
        ex = jnp.exp(s - jnp.max(s, axis=-1, keepdims=True))
        p = ex / jnp.sum(ex, axis=-1, keepdims=True)
        PS[a] = p
        acc += nn(p.astype(BF), jnp.where(mine, vs, zero))
    AOS[...] = acc.astype(BF)
    ao = [net.send(AOS.at[pl.ds(pl.multiple_of(R * (h ^ m), R), R)], AO.at[h], head=h ^ m) for m in (2, 3, 1)]
    AO[h] = AOS[pl.ds(pl.multiple_of(R * h, R), R), :]
    keep_out(PS, PSH)
    wa.step("y")
    wa.step("c")
    for c in ao:
        c.wait_recv()

    def part(ref, g, i=None):
        blk = ref[g % 2, g // 2] if i is None else ref[g % 2, g // 2, :, :, :, :, W * i : W * i + W]
        return blk.reshape(D, blk.shape[-1])

    mine_rows = pl.ds(pl.multiple_of(R * h, R), R)
    first = hid[mine_rows, :].astype(F32)
    for g in range(4):
        first += nt(AO[g], part(FA, g, 0))
    FIRST[...] = first
    n2 = rms_norm(first, gains[1:2].astype(F32)).astype(BF)
    N2[mine_rows, :] = n2
    QA[z, mine_rows, :] = jnp.concatenate([nn(n2, part(FA, g, 1)) for g in range(4)], axis=1).astype(BF)
    spreadq = Gather(net, QA, z, h, R)
    n2c = [net.send(N2.at[mine_rows], N2.at[mine_rows], head=h ^ m) for m in (2, 3, 1)]
    keep_out(FA, FAH)
    wk.step("c")
    keep_out(FK, FKH)

    tok = enc.shape[1]
    krow, klane = iota((tok, AUG), 0), iota((tok, AUG), 1)
    per = 96
    npass = plen.shape[1]
    vaug = jnp.where(klane < 9, -1.0, 0.0).astype(F32)

    def project(q, carry):
        dead = krow >= per * npass
        for p in range(npass):
            inside = (krow >= per * p) & (krow < per * p + per)
            dead = dead | (inside & (krow - per * p + per * h >= plen[q, p]))
        kaug = jnp.where(klane == 9, jnp.where(dead, NEGATIVE, 0.0), vaug)

        def group(g, c2):
            kv = nn(enc[q], FK[g % 2, g // 2].reshape(D, 2 * W))
            k, v = kv[:, :W], kv[:, W:]
            KP[q, g] = jnp.concatenate([k, kaug], axis=1).astype(BF)
            VP[q, g] = jnp.concatenate([v, vaug], axis=1).astype(BF)
            KT[q, g] = k.T.astype(BF)
            VT[q, g] = v.T.astype(BF)
            return c2

        lax.fori_loop(0, 4, group, 0)
        return carry

    lax.fori_loop(0, 2, project, 0)
    spreadq.relay()
    wc.step("a")
    wg.step("a")
    lax.fori_loop(2, 4, project, 0)
    for src, dst in ((KP, KPH), (VP, VPH), (KT, KTH), (ET, ETH)):
        keep_out(src, dst)

    qaug = jnp.where(iota((T, AUG), 1) == 9, 1.0, 0.0).astype(BF)

    def weights(m1, l1, m2, l2):
        top = jnp.maximum(m1, m2)
        w1, w2 = l1 * jnp.exp(m1 - top), l2 * jnp.exp(m2 - top)
        return top, w1 + w2, w1, w2

    def spread(x):
        return jnp.concatenate([jnp.broadcast_to(x[a : a + 1], (HD, T)) for a in range(3)], axis=0)

    def join(o1, s1, o2, s2):
        top, tot, w1, w2 = weights(s1[0:3], s1[3:6], s2[0:3], s2[3:6])
        o = o1 * spread(w1 / tot) + o2 * spread(w2 / tot)
        return o, jnp.concatenate([top, tot, jnp.zeros((2, T), F32)], axis=0)

    def attend(i, zz):
        for g in range(4):
            QU[g] = QA[zz, :, W * g : W * g + W]

        def group(g, carry):
            qg, kg = QU[g], KP[zz, g]
            outs, tops, tots = [], [], []
            for a in range(3):
                mine = (lane >= HD * a) & (lane < HD * a + HD)
                qm = jnp.concatenate([jnp.where(mine, qg, zero), qaug], axis=1)
                s = nt(kg, qm)
                m = jnp.max(s, axis=0, keepdims=True)
                ex = jnp.exp(s - m)
                l = jnp.sum(ex, axis=0, keepdims=True)
                o = nn(VT[zz, g, HD * a : HD * a + HD, :], ex.astype(BF))
                outs.append(o / l)
                tops.append(m)
                tots.append(l)
            gc, gx = g % 2, g // 2
            OS[i, gc, gx] = jnp.concatenate(outs, axis=0).astype(BF)
            ST[i, gc, gx] = jnp.concatenate(tops + tots + [jnp.zeros((2, T), F32)], axis=0)
            return carry

        lax.fori_loop(0, 4, group, 0)

    q_core, q_x, q_z = {}, {}, {}

    def core_stage(i):
        q_core[i] = (net.send(OS.at[i, 1 - hc], OC.at[i], head=h ^ 1), net.send(ST.at[i, 1 - hc], SC.at[i], head=h ^ 1))

    def x_stage(i):
        for c in q_core[i]:
            c.wait_recv()
        o, s = join(OS[i, hc, 1 - hx].astype(F32), ST[i, hc, 1 - hx], OC[i, 1 - hx].astype(F32), SC[i, 1 - hx])
        OXS[i] = o.astype(BF)
        SXS[i] = s
        q_x[i] = (net.send(OXS.at[i], OX.at[i], head=h ^ 2), net.send(SXS.at[i], SX.at[i], head=h ^ 2))
        o, s = join(OS[i, hc, hx].astype(F32), ST[i, hc, hx], OC[i, hx].astype(F32), SC[i, hx])
        OWN[i] = o
        SOWN[i] = s

    def z_stage(i):
        for c in q_x[i]:
            c.wait_recv()
        o, s = join(OWN[i], SOWN[i], OX[i].astype(F32), SX[i])
        if i < 3:
            m = ORDER[i]
            OZS[i] = o.astype(BF)
            SZS[i] = s
            to = lax.rem(z - m + 4, 4)
            q_z[i] = (net.send(OZS.at[i], OZ.at[i], psg=to), net.send(SZS.at[i], SZ.at[i], psg=to))
        else:
            OWN[i] = o
            SOWN[i] = s

    for i, m in enumerate(ORDER):
        zz = lax.rem(z - m + 4, 4)
        spreadq.ready(m)
        attend(i, zz)
        if i < 2:
            wc.step(("y", "x")[i])
        core_stage(i)
        if i >= 1:
            x_stage(i - 1)
        if i >= 2:
            z_stage(i - 2)
    x_stage(3)
    z_stage(2)
    z_stage(3)
    o, s = OWN[3], SOWN[3]
    for i in range(3):
        for c in q_z[i]:
            c.wait_recv()
        o, s = join(o, s, OZ[i].astype(F32), SZ[i])
    lse = s[0:3] + jnp.log(s[3:6])
    full = jnp.concatenate([o, lse, jnp.zeros((AUG - 3, T), F32)], axis=0)
    ATS[...] = full.T
    ATO[...] = ATS[:, 0:W].astype(BF)
    for c in n2c:
        c.wait_recv()
    at = [net.send(ATS.at[pl.ds(pl.multiple_of(R * (h ^ m), R), R)], AT.at[h], head=h ^ m) for m in (1, 2, 3)]
    AT[h] = ATS[mine_rows, :]
    wc.step("c")
    for c in at:
        c.wait_recv()
    second = FIRST[...]
    for g in range(4):
        low = AT[g, :, 0:W].astype(BF)
        second += nt(low, part(FC, g))
    g2gain = gains[2:3].astype(F32)
    N3[mine_rows, :] = rms_norm(second, g2gain).astype(BF)
    n3c = [net.send(N3.at[mine_rows], N3.at[mine_rows], head=h ^ m) for m in (2, 3, 1)]
    rowid = iota((T, 1), 0)
    go_low = jnp.where(rowid < tlen[0], cot[...], jnp.zeros((T, D), BF))
    wg.step("y")
    for c in n3c:
        c.wait_recv()
    wdown = GG[:, :, :, :, 2 * F : 3 * F].reshape(D, F)
    wgu = GG[:, :, :, :, 0 : 2 * F].reshape(D, 2 * F)
    d_act = nn(go_low, wdown)
    n3 = N3[...]
    gate_up = nn(n3, wgu)
    gate, up = gate_up[:, :F], gate_up[:, F:]
    c0 = 0.7978845608028654
    inner = c0 * (gate + 0.044715 * gate * gate * gate)
    th = jnp.tanh(inner)
    gel = 0.5 * gate * (1.0 + th)
    act = (gel * up).astype(BF)
    dgel = 0.5 * (1.0 + th) + 0.5 * gate * (1.0 - th * th) * (c0 * (1.0 + 3 * 0.044715 * gate * gate))
    dgu = jnp.concatenate([d_act * up * dgel, d_act * gel], axis=1).astype(BF)
    R3S[...] = nt(dgu, wgu).astype(BF)
    r3 = [net.send(R3S.at[pl.ds(pl.multiple_of(R * (h ^ m), R), R)], R3.at[h], head=h ^ m) for m in (2, 3, 1)]
    R1S[...] = nt(act, wdown).astype(BF)
    r1 = [net.send(R1S.at[pl.ds(pl.multiple_of(R * (h ^ m), R), R)], R1.at[h], head=h ^ m) for m in (2, 3, 1)]
    R3[h] = R3S[mine_rows, :]
    R1[h] = R1S[mine_rows, :]
    GF[:, :, :, :, 2 * F : 3 * F] = tn(go_low, act).astype(BF).reshape(2, 2, 2, D // 8, F)
    GF[:, :, :, :, 0 : 2 * F] = tn(n3, dgu).astype(BF).reshape(2, 2, 2, D // 8, 2 * F)
    keep_out(GF, GFH)
    for c in r3:
        c.wait_recv()
    dn3 = R3[0].astype(F32) + R3[1].astype(F32) + R3[2].astype(F32) + R3[3].astype(F32)
    live = (iota((R, 1), 0) + R * h) < tlen[0]
    go = jnp.where(live, cot[mine_rows, :].astype(F32), 0.0)
    dv, dg = rms_back(dn3, second, g2gain)
    DG3[...] = jnp.concatenate([dg, jnp.zeros((7, D), F32)], axis=0)
    g2 = go + dv
    G2[...] = g2
    g2_low = g2.astype(BF)
    alane = iota((R, 2 * AUG), 1)
    wl = iota((R, W), 1)
    aug = jnp.zeros((R, 2 * AUG), F32)
    dos = []

    def parts(x):
        hi_ = x.astype(BF).astype(F32)
        mid = (x - hi_).astype(BF).astype(F32)
        return hi_, mid, x - hi_ - mid

    for g in range(4):
        do = nn(g2_low, part(FC, g)).astype(BF)
        dos.append(do.astype(F32))
        prod = do.astype(F32) * AT[g, :, 0:W]
        for a in range(3):
            delta = jnp.sum(jnp.where((wl >= HD * a) & (wl < HD * a + HD), prod, 0.0), axis=1, keepdims=True)
            for off, val in ((0, AT[g, :, W + a : W + a + 1]), (AUG, delta)):
                for j, piece in enumerate(parts(val)):
                    aug = jnp.where(alane == off + 9 * g + 3 * a + j, piece, aug)
    DO[...] = jnp.concatenate(dos + [aug], axis=1).astype(BF)
    for c in r1:
        c.wait_recv()
    out = second + R1[0].astype(F32) + R1[1].astype(F32) + R1[2].astype(F32) + R1[3].astype(F32)
    OUT[...] = jnp.where(live, out, 0.0)
    for c in kept:
        c.wait()
    net.finish()


def call_one(plen, tlen, table, hid, enc, buckets, gains, mats, cot):
    T, D = hid.shape
    R = T // 4
    W = 3 * HD
    rows = mats[0].shape[0]
    F = mats[8].shape[1] // 4
    tok = -(-enc.shape[1] // 128) * 128
    S = jax.ShapeDtypeStruct
    blk = 4 * rows
    big = dict(
        FA=((2, 2, 2, 2, 2, blk, 2 * W), BF), FK=((2, 2, 2, 2, 2, blk, 2 * W), BF), FC=((2, 2, 2, 2, 2, blk, W), BF),
        GQ=((2, 2, 2, blk, 3 * W), BF),
        KP=((4, 4, tok, W + AUG), BF), VP=((4, 4, tok, W + AUG), BF), KT=((4, 4, W, tok), BF),
        ET=((4, D, tok), BF), PS=((3, T, T), F32),
        GF=((2, 2, 2, blk, 3 * F), BF),
    )
    outs = {n: big[n] for n in ("FA", "FK", "GQ", "KP", "VP", "KT", "ET", "PS")}
    outs.update(
        QA=((4, T, D), BF), QKV=((T, 3 * W), BF), AO=((T, W), BF), FIRST=((R, D), F32),
        G2=((R, D), F32), DO=((R, D + 2 * AUG), BF),
        GF=big["GF"], DG3=((8, D), F32), OUT=((R, D), F32), N2=((T, D), BF), ATO=((T, W), BF),
    )
    pack = [VMEM((4, rows, w), BF) for w in (3 * W, 2 * W, 2 * W, W, 3 * F)]
    scratch = pack + pack + [
        *[VMEM(*big[n]) for n in ("FA", "FK", "FC", "GQ")], VMEM((2, 2, 2, blk, 3 * F), BF),
        *[VMEM(*big[n]) for n in ("KP", "VP", "KT")], VMEM((4, 4, W, tok), BF),
        *[VMEM(*big[n]) for n in ("ET", "PS")], VMEM((4, R, W), BF), VMEM(*big["GF"]),
        VMEM((enc.shape[0], tok, D), BF), VMEM((4, T, W), BF), VMEM((3, T, T), F32),
        VMEM((4, 2, 2, W, T), BF), VMEM((4, 2, 2, 8, T), F32),
        VMEM((4, 2, W, T), BF), VMEM((4, 2, 8, T), F32),
        VMEM((4, W, T), BF), VMEM((4, 8, T), F32), VMEM((4, W, T), BF), VMEM((4, 8, T), F32),
        VMEM((3, W, T), BF), VMEM((3, 8, T), F32), VMEM((3, W, T), BF), VMEM((3, 8, T), F32),
        VMEM((4, W, T), F32), VMEM((4, 8, T), F32),
        VMEM((T, W + AUG), F32), VMEM((4, R, W + AUG), F32), VMEM((T, D), BF),
        VMEM((T, D), BF), VMEM((4, R, D), BF), VMEM((T, D), BF), VMEM((4, R, D), BF),
        VMEM((3 * T, W + AUG), BF),
        pltpu.SemaphoreType.DMA((160,)), pltpu.SemaphoreType.DMA((160,)), pltpu.SemaphoreType.DMA((12,)),
    ]
    smem = pl.BlockSpec(memory_space=pltpu.SMEM)
    vm = pl.BlockSpec(memory_space=pltpu.VMEM)
    anym = pl.BlockSpec(memory_space=pl.ANY)
    res = pl.pallas_call(
        kernel_one,
        out_shape=[S(*v) for v in outs.values()],
        in_specs=[smem] * 2 + [vm] * 2 + [anym] + [vm] * 14,
        out_specs=[anym if n in big else vm for n in outs],
        scratch_shapes=scratch,
        name="forward",
        compiler_params=pltpu.CompilerParams(collective_id=1, has_side_effects=True, vmem_limit_bytes=63 << 20),
    )(plen, tlen, table, hid, enc, buckets, gains, *mats, cot)
    return dict(zip(outs, res))


def kernel_two(
    buckets, gains, hid, ETH, FAH, FKH, GQH, QA, KPH, VPH, KTH, PSH, QKV, AOO, FIRST, G2, DO, GFH, DG3, OUTR, N2, ATO,
    DENC, DHID, OUT, SM, OF, OC, OK, OA, OL,
    DOB, KP, VP, KT, QAV, ET, FA, FK, GQ, PS,
    QU, DU, QX, DX, QM, DM, DS, PB, DQG, DKV, DQS, DQC, DXR, DOWN, DZS, DZR, DAS, DA, DSF, TBL, NS, NR, DEN,
    FSRC, F1, F2, F3, FTOT, CSRC, C1, C2, C3, CTOT,
    KSRC, K1, K2, K3, K4, K5, KTOT, ASRC, A1, A2, A3, ATOT,
    LSRC, L1, L2, L3, LTOT,
    SMR, DQL, DQO, G1A, G2A,
    ss, rs, ls, es,
):
    d, z, h = enter()
    net = Net(ss, rs)
    T, D = hid.shape
    R = T // 4
    W = 3 * HD
    hc, hx = h % 2, h // 2
    tok = ETH.shape[2]
    mine_rows = pl.ds(pl.multiple_of(R * h, R), R)

    def source(m):
        return lax.rem(z - m + 4, 4)

    def load(pairs, sem):
        cs = [pltpu.make_async_copy(a, b, sem(j)) for j, (a, b) in enumerate(pairs)]
        for c in cs:
            c.start()
        return cs

    def fetch(i):
        zz, slot = source(ORDER[i]), i % 2
        return load(
            [(a.at[zz], b.at[slot]) for a, b in ((KPH, KP), (VPH, VP), (KTH, KT), (QA, QAV))],
            lambda j: ls.at[j, slot],
        )

    DOB[z, mine_rows, :] = DO[...]
    gather = Gather(net, DOB, z, h, R)
    fetched = fetch(0)
    G2A[mine_rows, :] = G2[...].astype(BF)
    g2c = [net.send(G2A.at[mine_rows], G2A.at[mine_rows], head=h ^ m) for m in (2, 3, 1)]
    near = load([(GFH, FSRC)], lambda j: es.at[j])
    full, own = ("c", "x", "y", "a", "b"), ("y", "a", "b")
    sf = Halving(net, FSRC, own, ("y", "a", "b"), (F1, F2, F3), FTOT, OF)
    sc = Halving(net, CSRC, own, ("y", "a", "b"), (C1, C2, C3), CTOT, OC)
    sk = Halving(net, KSRC, full, ("c", "x", "y", "a", "b"), (K1, K2, K3, K4, K5), KTOT, OK)
    sa = Halving(net, ASRC, own, ("y", "a", "b"), (A1, A2, A3), ATOT, OA)
    sl = Halving(net, LSRC, own, ("y", "a", "b"), (L1, L2, L3), LTOT, OL)
    weights = load([(FAH, FA), (FKH, FK), (GQH, GQ), (PSH, PS)], lambda j: es.at[2 + j])
    gather.relay()
    OUT[mine_rows, :] = OUTR[...]
    for c in near:
        c.wait()

    lane = iota((T, W), 1)
    alane = iota((T, AUG), 1)
    zero = jnp.zeros((T, W), BF)
    azero = jnp.zeros((T, AUG), BF)
    one = jnp.ones((T, 1), F32)
    pad = jnp.zeros((T, AUG - 10), F32)

    def mine_of(a):
        return (lane >= HD * a) & (lane < HD * a + HD)

    def part(ref, g, i=None):
        blk = ref[g % 2, g // 2] if i is None else ref[g % 2, g // 2, :, :, :, :, W * i : W * i + W]
        return blk.reshape(D, blk.shape[-1])

    half = tok // 2

    def attend(i, zz):
        slot = i % 2
        ex = DOB[zz, :, D : D + 2 * AUG].astype(F32)
        for g in range(4):
            QU[g] = QAV[slot, :, W * g : W * g + W]
            DU[g] = DOB[zz, :, W * g : W * g + W]
            QX[g] = jnp.concatenate([ex[:, 9 * g : 9 * g + 9], one, pad], axis=1).astype(BF)
            DX[g] = jnp.concatenate([ex[:, AUG + 9 * g : AUG + 9 * g + 9], one * 0, pad], axis=1).astype(BF)

        def group(g, carry):
            for a in range(3):
                keep = (alane == 9) | ((alane >= 3 * a) & (alane < 3 * a + 3))
                QM[T * a : T * a + T] = jnp.concatenate([jnp.where(mine_of(a), QU[g], zero), jnp.where(keep, QX[g], azero)], axis=1)
                DM[T * a : T * a + T] = jnp.concatenate([jnp.where(mine_of(a), DU[g], zero), jnp.where(keep, DX[g], azero)], axis=1)
            for t in range(0, tok, half):
                kg, vg = KP[slot, g, t : t + half], VP[slot, g, t : t + half]
                for a in range(3):
                    p = jnp.exp(nt(kg, QM[T * a : T * a + T]))
                    ds = p * nt(vg, DM[T * a : T * a + T])
                    DS[t : t + half, T * a : T * a + T] = ds.astype(BF)
                    PB[t : t + half, T * a : T * a + T] = p.astype(BF)
            dk = nn(DS[...], QM[...])
            dv = nn(PB[...], DM[...])
            DKV[zz, g] = jnp.concatenate([dk[:, :W], dv[:, :W]], axis=1).astype(BF)
            dqs = [nn(KT[slot, g, HD * a : HD * a + HD, :], DS[:, T * a : T * a + T]) for a in range(3)]
            DQG[g] = jnp.concatenate(dqs, axis=0).T.astype(BF)
            return carry

        lax.fori_loop(0, 4, group, 0)
        dq = jnp.concatenate([DQG[g] for g in range(4)], axis=1)
        for j in range(4):
            DQS[i, j % 2, j // 2] = dq[R * j : R * j + R]

    q_core, q_x, q_z = {}, {}, {}

    def core_stage(i):
        q_core[i] = net.send(DQS.at[i, 1 - hc], DQC.at[i], head=h ^ 1)

    def x_stage(i):
        q_core[i].wait_recv()
        DQC[i, 1 - hx] = (DQS[i, hc, 1 - hx].astype(F32) + DQC[i, 1 - hx].astype(F32)).astype(BF)
        q_x[i] = net.send(DQC.at[i, 1 - hx], DXR.at[i], head=h ^ 2)
        DOWN[i] = DQS[i, hc, hx].astype(F32) + DQC[i, hx].astype(F32)

    def z_stage(i):
        q_x[i].wait_recv()
        o = DOWN[i] + DXR[i].astype(F32)
        if i < 3:
            DZS[i] = o.astype(BF)
            q_z[i] = net.send(DZS.at[i], DZR.at[i], psg=source(ORDER[i]))
        else:
            DOWN[i] = o

    for i, m in enumerate(ORDER):
        gather.ready(m)
        for c in fetched:
            c.wait()
        if i < 3:
            fetched = fetch(i + 1)
        attend(i, source(m))
        core_stage(i)
        if i >= 1:
            x_stage(i - 1)
        if i >= 2:
            z_stage(i - 2)
        if i == 0:
            for c in g2c:
                c.wait_recv()
            CSRC[...] = tn(G2A[...], ATO[...]).astype(BF).reshape(CSRC.shape)
            sf.push()
            sc.push()
    x_stage(3)
    z_stage(2)
    z_stage(3)
    sf.pull()
    sc.pull()

    def et_copy(n):
        return pltpu.make_async_copy(ETH.at[n % 4], ET.at[n % 2], ls.at[4, n % 2])

    et_copy(0).start()
    for c in weights:
        c.wait()
    dq = DOWN[3]
    for i in range(3):
        q_z[i].wait_recv()
        dq += DZR[i].astype(F32)
    dq_low = dq.astype(BF)

    first = FIRST[...]
    gain = gains[1:2].astype(F32)
    dn2 = jnp.zeros((R, D), F32)
    for g in range(4):
        dn2 += nt(dq_low[:, W * g : W * g + W], part(FA, g, 1))
    dv, dg2 = rms_back(dn2, first, gain)
    g1 = G2[...] + dv
    g1_low = g1.astype(BF)
    G1A[mine_rows, :] = g1_low
    for g in range(4):
        DQL[g] = dq_low[:, W * g : W * g + W]
    for g in range(4):
        DAS[g] = nn(g1_low, part(FA, g, 0)).astype(BF)
    das = [net.send(DAS.at[h ^ m], DA.at[h], head=h ^ m) for m in (2, 3, 1)]
    DA[h] = DAS[h]
    dql = [net.send(DQL.at[h ^ m], DQO.at[h], head=h ^ m) for m in (2, 3, 1)]
    DQO[h] = DQL[h]
    dql += [net.send(G1A.at[mine_rows], G1A.at[mine_rows], head=h ^ m) for m in (2, 3, 1)]

    def whole_grads(g, carry):
        acc = jnp.zeros((D, 2 * W), F32)
        for q in range(4):
            et_copy(4 * g + q).wait()

            @pl.when(4 * g + q < 15)
            def _():
                et_copy(4 * g + q + 1).start()

            acc += nn(ET[q % 2], DKV[q, g])
        gc, gx = g % 2, g // 2
        KSRC[gc, gx] = acc.astype(BF).reshape(2, 2, 2, D // 8, 2 * W)
        return carry

    lax.fori_loop(0, 4, whole_grads, 0)
    sk.push()
    for c in dql:
        c.wait_recv()
    rest = [tn(N2[...], DQO[...].reshape(T, W)), tn(G1A[...], AOO[...])]
    ASRC[...] = jnp.concatenate(rest, axis=1).astype(BF).reshape(ASRC.shape)
    sa.push()
    for c in das:
        c.wait_recv()

    da = DA[...].reshape(T, W)
    qs, ks, vs = QKV[:, 0:W], QKV[:, W : 2 * W], QKV[:, 2 * W : 3 * W]
    dq1 = jnp.zeros((T, W), F32)
    dk1 = jnp.zeros((T, W), F32)
    dv1 = jnp.zeros((T, W), F32)
    for a in range(3):
        mine = mine_of(a)
        dam = jnp.where(mine, da, zero)
        p = PS[a]
        dp = nt(dam, vs)
        ds = p * (dp - jnp.sum(p * dp, axis=-1, keepdims=True))
        DSF[a] = ds
        dsl = ds.astype(BF)
        dq1 += nn(dsl, jnp.where(mine, ks, zero))
        dk1 += tn(dsl, jnp.where(mine, qs, zero))
        dv1 += tn(p.astype(BF), dam)
    dqkv = jnp.concatenate([dq1, dk1, dv1], axis=1).astype(BF)
    wqkv = GQ[...].reshape(D, 3 * W)
    NS[...] = nt(dqkv, wqkv).astype(BF)
    nr = [net.send(NS.at[pl.ds(pl.multiple_of(R * (h ^ m), R), R)], NR.at[h], head=h ^ m) for m in (2, 3, 1)]
    NR[h] = NS[mine_rows, :]
    sk.pull()
    sa.pull()
    g0 = gains[0:1].astype(F32)
    n1 = rms_norm(hid[...].astype(F32), g0).astype(BF)
    LSRC[...] = tn(n1, dqkv).astype(BF).reshape(LSRC.shape)
    sl.push()

    step = DEN.shape[1]
    per = DENC.shape[1] // step

    def den_copy(n):
        rows = pl.ds(pl.multiple_of(lax.rem(n, per) * step, step), step)
        return pltpu.make_async_copy(DEN.at[lax.rem(n, 2)], DENC.at[n // per, rows], es.at[lax.rem(n, 2)])

    def denc(n, carry):
        rows = pl.ds(pl.multiple_of(lax.rem(n, per) * step, step), step)

        @pl.when(n >= 2)
        def _():
            den_copy(n - 2).wait()

        acc = nt(DKV[n // per, 0, rows, :], part(FK, 0))
        for g in range(1, 4):
            acc += nt(DKV[n // per, g, rows, :], part(FK, g))
        DEN[lax.rem(n, 2)] = acc
        den_copy(n).start()
        return carry

    def dencs(a, b):
        lax.fori_loop(a, b, denc, 0)

    dencs(0, 1)
    sf.pull()
    sc.pull()
    dencs(1, 2)
    for c in nr:
        c.wait_recv()
    dn1 = NR[0].astype(F32) + NR[1].astype(F32) + NR[2].astype(F32) + NR[3].astype(F32)
    dv, dg1 = rms_back(dn1, hid[mine_rows, :].astype(F32), g0)
    DHID[mine_rows, :] = g1 + dv
    dh = [net.send(DHID.at[mine_rows], DHID.at[mine_rows], head=h ^ m) for m in (2, 3, 1)]
    dh += [net.send(OUT.at[mine_rows], OUT.at[mine_rows], head=h ^ m) for m in (2, 3, 1)]

    sl.pull()
    sa.pull()
    sk.pull()

    bk = buckets[...]

    def table_step(i, carry):
        hit = bk == i
        for a in range(3):
            TBL[a, pl.ds(i, 1), :] = jnp.sum(jnp.where(hit, DSF[a], 0.0), axis=0, keepdims=True)
        return carry

    nb = TBL.shape[1]
    lax.fori_loop(0, nb, table_step, 0)
    tl = iota((nb, 128), 1)
    tab = jnp.zeros((nb, 128), F32)
    for a in range(3):
        tab = jnp.where(tl == a, jnp.sum(TBL[a], axis=1, keepdims=True), tab)
    tab = jnp.concatenate([tab, jnp.zeros((128 - nb, 128), F32)], axis=0).T[0:8]
    tab = jnp.concatenate([tab, jnp.zeros((8, D - 128), F32)], axis=1)
    dgs = jnp.concatenate([dg1, dg2, DG3[0:1], jnp.zeros((5, D), F32)], axis=0)
    SM[0] = jnp.concatenate([dgs, tab], axis=0)
    srow = iota((16, D), 0)

    def small(j, **dev):
        return net.send(SM.at[j], SMR.at[j], **dev)

    def small_end(j, c, shared):
        c.wait_recv()
        got = SMR[j]
        SM[j + 1] = SM[j] + (got if shared else jnp.where(srow < 8, got, 0.0))

    c = small(0, head=h ^ 1)
    sf.pull()
    sc.pull()
    small_end(0, c, False)
    c = small(1, head=h ^ 2)
    dencs(2, 4)
    sl.pull()
    sa.pull()
    sk.pull()
    small_end(1, c, False)
    c = small(2, dp=1 - d)
    dencs(4, 5)
    small_end(2, c, True)
    c = small(3, psg=z ^ 1)
    sl.pull()
    sk.pull()
    dencs(5, 6)
    small_end(3, c, True)
    c = small(4, psg=z ^ 2)
    sk.pull()
    dencs(6, 4 * per)
    small_end(4, c, True)
    for n in (4 * per - 2, 4 * per - 1):
        den_copy(n).wait()
    for s in (sf, sc, sk, sa, sl):
        s.done()
    for c in dh:
        c.wait_recv()
    net.finish()


def call_two(buckets, gains, hid, kept, rows, count):
    T, D = hid.shape
    R = T // 4
    W = 3 * HD
    k = kept
    tok = k["ET"].shape[2]
    F3 = k["GF"].shape[4]
    S = jax.ShapeDtypeStruct
    blk = D // 8
    outs = dict(
        DENC=((4, count, D), F32), DHID=((T, D), F32), OUT=((T, D), F32), SM=((6, 16, D), F32),
        OF=((4, rows, F3), F32), OC=((4, rows, W), F32), OK=((4, rows, 2 * W), F32), OA=((4, rows, 2 * W), F32),
        OL=((4, rows, 3 * W), F32),
    )

    def halving(n, w):
        return [VMEM((2,) * k + (blk, w), BF) for k in (n, *range(n - 1, -1, -1))] + [VMEM((blk, w), F32)]

    def like(n, *lead):
        return VMEM((*lead, *k[n].shape[1:]) if lead else k[n].shape, k[n].dtype)

    scratch = [
        VMEM((4, T, D + 2 * AUG), BF), like("KP", 2), like("VP", 2), like("KT", 2), like("QA", 2), like("ET", 2),
        like("FA"), like("FK"), like("GQ"), like("PS"),
        VMEM((4, T, W), BF), VMEM((4, T, W), BF), VMEM((4, T, AUG), BF), VMEM((4, T, AUG), BF),
        VMEM((3 * T, W + AUG), BF), VMEM((3 * T, W + AUG), BF), VMEM((tok, 3 * T), BF), VMEM((tok, 3 * T), BF),
        VMEM((4, T, W), BF), VMEM((4, 4, tok, 2 * W), BF),
        VMEM((4, 2, 2, R, D), BF), VMEM((4, 2, R, D), BF), VMEM((4, R, D), BF), VMEM((4, R, D), F32),
        VMEM((3, R, D), BF), VMEM((3, R, D), BF), VMEM((4, R, W), BF), VMEM((4, R, W), BF),
        VMEM((3, T, T), F32), VMEM((3, 32, T), F32), VMEM((T, D), BF), VMEM((4, R, D), BF), VMEM((2, count // 2, D), F32),
        *halving(3, F3), *halving(3, W), *halving(5, 2 * W), *halving(3, 2 * W), *halving(3, 3 * W),
        VMEM((5, 16, D), F32), VMEM((4, R, W), BF), VMEM((4, R, W), BF), VMEM((T, D), BF), VMEM((T, D), BF),
        pltpu.SemaphoreType.DMA((120,)), pltpu.SemaphoreType.DMA((120,)), pltpu.SemaphoreType.DMA((5, 2)), pltpu.SemaphoreType.DMA((6,)),
    ]
    vm = pl.BlockSpec(memory_space=pltpu.VMEM)
    anym = pl.BlockSpec(memory_space=pl.ANY)
    names = ("ET", "FA", "FK", "GQ", "QA", "KP", "VP", "KT", "PS", "QKV", "AO", "FIRST", "G2", "DO", "GF", "DG3", "OUT", "N2", "ATO")
    far = ("ET", "FA", "FK", "GQ", "QA", "KP", "VP", "KT", "PS", "GF")
    res = pl.pallas_call(
        kernel_two,
        out_shape=[S(*v) for v in outs.values()],
        in_specs=[vm] * 3 + [anym if n in far else vm for n in names],
        out_specs=[anym] + [vm] * (len(outs) - 1),
        scratch_shapes=scratch,
        name="backward",
        compiler_params=pltpu.CompilerParams(collective_id=2, has_side_effects=True, vmem_limit_bytes=63 << 20),
    )(buckets, gains, hid, *[k[n] for n in names])
    return dict(zip(outs, res))


def local_fast(
    hidden_in, encodings, passage_lengths, target_lengths, rel_buckets, gains, rel_table, *rest
):
    mats, cot = rest[:11], rest[11]
    span, passages, group, D = encodings.shape
    rows = mats[0].shape[0]
    W = 3 * HD
    F = mats[8].shape[1] // 4
    count = span * passages
    enc = jnp.transpose(encodings, (2, 1, 0, 3)).reshape(group, count, D)
    hid = hidden_in[0]
    kept = call_one(
        passage_lengths.T, target_lengths, rel_table.T, hid, enc, rel_buckets, gains, mats, cot[0]
    )
    r = call_two(rel_buckets, gains, hid, kept, rows, count)
    d_enc = jnp.transpose(r["DENC"].reshape(group, passages, span, D), (2, 1, 0, 3))

    last = call_three(r, W, F, rel_table.shape[0])
    return (last["OUT"][None], last["DHID"][None], d_enc, last["GAINS"], last["TABLE"].T) + tuple(
        last[n] for n in ("sq", "sk", "sv", "so", "cq", "ck", "cv", "co", "fg", "fu", "fd")
    )


def kernel_three(W, F, OUT, DHID, SM, OF, OC, OK, OA, OL, out, dhid, gains, table, sq, sk, sv, so, cq, ck, cv, co, fg, fu, fd):
    out[...] = OUT[...]
    dhid[...] = DHID[...]
    gains[...] = SM[5, 0:3, :]
    table[...] = SM[5, 8:11, 0 : table.shape[1]]
    for dst, src, i, w in (
        (sq, OL, 0, W), (sk, OL, 1, W), (sv, OL, 2, W), (so, OA, 1, W), (cq, OA, 0, W),
        (ck, OK, 0, W), (cv, OK, 1, W), (co, OC, 0, W), (fg, OF, 0, F), (fu, OF, 1, F), (fd, OF, 2, F),
    ):
        dst[...] = jnp.concatenate([src[j, :, w * i : w * i + w] for j in range(4)], axis=1)


def call_three(r, W, F, nb):
    S = jax.ShapeDtypeStruct
    names = ("OUT", "DHID", "SM", "OF", "OC", "OK", "OA", "OL")
    T, D = r["OUT"].shape
    rows = r["OF"].shape[1]
    outs = dict(OUT=(T, D), DHID=(T, D), GAINS=(3, D), TABLE=(3, nb))
    outs.update({n: (rows, 4 * W) for n in ("sq", "sk", "sv", "so", "cq", "ck", "cv", "co")})
    outs.update({n: (rows, 4 * F) for n in ("fg", "fu", "fd")})
    vm = pl.BlockSpec(memory_space=pltpu.VMEM)
    res = pl.pallas_call(
        functools.partial(kernel_three, W, F),
        out_shape=[S(v, F32) for v in outs.values()],
        in_specs=[vm] * len(names),
        out_specs=[vm] * len(outs),
        name="columns",
        compiler_params=pltpu.CompilerParams(vmem_limit_bytes=62 << 20),
    )(*[r[n] for n in names])
    return dict(zip(outs, res))


def merged(part, axis, combine):
    gathered = jax.tree.map(lambda a: lax.all_gather(a, axis), part)

    def take(source):
        return jax.tree.map(lambda a: lax.dynamic_index_in_dim(a, source, 0, False), gathered)

    return lax.fori_loop(
        1, lax.axis_size(axis), lambda source, state: combine(state, take(source)), take(0)
    )


def rms_plain(values, gain):
    return values * lax.rsqrt(jnp.mean(values * values, axis=-1, keepdims=True) + EPSILON) * gain


def gated(gate_in, up_in):
    return jax.nn.gelu(gate_in, approximate=True) * up_in


def over_heads(partial_value):
    return lax.psum(partial_value, "head")


def own_columns(matrix, index, width):
    return lax.dynamic_slice_in_dim(matrix, index * width, width, 1)


def left_mul(left, matrix):
    return jnp.einsum("qtd,dc->qtc", left, matrix, preferred_element_type=jnp.float32)


def right_mul(left, matrix):
    return jnp.einsum("qtc,dc->qtd", left, matrix, preferred_element_type=jnp.float32)


def row_outer(left, right):
    return jnp.einsum("qtd,qtc->dc", left, right, preferred_element_type=jnp.float32)


def local_plain(
    hidden_in,
    encodings,
    passage_lengths,
    target_lengths,
    rel_buckets,
    gains,
    rel_table,
    self_q,
    self_k,
    self_v,
    self_o,
    cross_q,
    cross_k,
    cross_v,
    cross_o,
    ff_gate,
    ff_up,
    ff_down,
    cotangent,
):
    gathered = (
        lax.all_gather(self_q, ("dp", "psg", "head"), axis=0, tiled=True),
        lax.all_gather(self_k, ("dp", "psg", "head"), axis=0, tiled=True),
        lax.all_gather(self_v, ("dp", "psg", "head"), axis=0, tiled=True),
        lax.all_gather(self_o, ("dp", "psg", "head"), axis=0, tiled=True),
        lax.all_gather(cross_q, ("dp", "psg", "head"), axis=0, tiled=True),
        lax.all_gather(cross_k, ("dp", "psg", "head"), axis=0, tiled=True),
        lax.all_gather(cross_v, ("dp", "psg", "head"), axis=0, tiled=True),
        lax.all_gather(cross_o, ("dp", "psg", "head"), axis=0, tiled=True),
        lax.all_gather(ff_gate, ("dp", "psg", "head"), axis=0, tiled=True),
        lax.all_gather(ff_up, ("dp", "psg", "head"), axis=0, tiled=True),
        lax.all_gather(ff_down, ("dp", "psg", "head"), axis=0, tiled=True),
    )
    (
        self_query,
        self_key,
        self_value,
        self_out,
        cross_query,
        cross_key,
        cross_value,
        cross_out,
        gate_full,
        up_full,
        down_full,
    ) = gathered
    head_index = lax.axis_index("head")
    heads_local = rel_table.shape[1]
    width = heads_local * HD
    total_width = self_query.shape[1]
    ff_total = gate_full.shape[1]
    ff_local = ff_total // lax.axis_size("head")
    query_rows = hidden_in.shape[0]
    target_span = hidden_in.shape[1]
    hidden = hidden_in.astype(jnp.float32)
    gain_all = gains.astype(jnp.float32)
    qkv_weight = jnp.concatenate(
        [
            own_columns(self_query, head_index, width),
            own_columns(self_key, head_index, width),
            own_columns(self_value, head_index, width),
        ],
        axis=1,
    )
    normed_one = rms_plain(hidden, gain_all[0]).astype(jnp.bfloat16)
    qkv_self = left_mul(normed_one, qkv_weight).astype(jnp.bfloat16)
    queries_self = qkv_self[..., :width].reshape(query_rows, target_span, heads_local, HD)
    keys_self = qkv_self[..., width : 2 * width].reshape(query_rows, target_span, heads_local, HD)
    values_self = qkv_self[..., 2 * width :].reshape(query_rows, target_span, heads_local, HD)
    positions = jnp.arange(target_span)
    causal = (positions[None, None, :] <= positions[None, :, None]) & (
        positions[None, None, :] < target_lengths[:, None, None]
    )
    buckets_hot = (rel_buckets[:, :, None] == jnp.arange(rel_table.shape[0])[None, None, :]).astype(
        jnp.float32
    )
    bias = jnp.einsum(
        "ijb,bh->hij", buckets_hot, rel_table.astype(jnp.float32), precision=lax.Precision.HIGHEST
    )
    scores_self = jnp.einsum(
        "qihd,qjhd->qhij", queries_self, keys_self, preferred_element_type=jnp.float32
    )
    scores_self = jnp.where(causal[:, None], scores_self + bias[None], NEGATIVE)
    probs_self = jax.nn.softmax(scores_self, axis=-1)
    probs_self_low = probs_self.astype(jnp.bfloat16)
    attn_one = jnp.einsum(
        "qhij,qjhd->qihd", probs_self_low, values_self, preferred_element_type=jnp.float32
    )
    attn_one = attn_one.reshape(query_rows, target_span, width).astype(jnp.bfloat16)
    self_out_own = own_columns(self_out, head_index, width)
    first = hidden + over_heads(right_mul(attn_one, self_out_own))
    normed_two = rms_plain(first, gain_all[1]).astype(jnp.bfloat16)
    cross_query_own = own_columns(cross_query, head_index, width)
    query_cross = left_mul(normed_two, cross_query_own).astype(jnp.bfloat16)
    query_group = lax.all_gather(query_cross, "psg", axis=0, tiled=True)
    group_count = query_group.shape[0]
    head_parts = lax.axis_size("head")
    kv_split = jnp.concatenate(
        [
            cross_key.reshape(cross_key.shape[0], head_parts, width),
            cross_value.reshape(cross_value.shape[0], head_parts, width),
        ],
        axis=2,
    )
    local_kv = jnp.einsum(
        "tpqd,dgc->qptgc", encodings, kv_split, preferred_element_type=jnp.float32
    ).astype(jnp.bfloat16)
    moved_kv = lax.all_to_all(local_kv, "head", split_axis=3, concat_axis=2, tiled=True)
    key_value = moved_kv.reshape(moved_kv.shape[0], moved_kv.shape[1], moved_kv.shape[2], 2 * width)
    passages_local = key_value.shape[1]
    passage_span = key_value.shape[2]
    key_count = passages_local * passage_span
    kv_flat = key_value.reshape(group_count, key_count, 2 * width)
    span = jnp.arange(passage_span)
    key_valid = (span[None, None, :] < jnp.transpose(passage_lengths)[:, :, None]).reshape(
        group_count, key_count
    )

    def masked_scores(query_block, kv_block, valid_block):
        query_heads = query_block.reshape(target_span, heads_local, HD)
        keys_part = kv_block[:, :width].reshape(key_count, heads_local, HD)
        raw = jnp.einsum("ihd,jhd->hij", query_heads, keys_part, preferred_element_type=jnp.float32)
        return jnp.where(valid_block[None, None, :], raw, NEGATIVE)

    def stats_one(item):
        masked = masked_scores(item[0], item[1], item[2])
        largest = jnp.max(masked, axis=-1)
        total = jnp.sum(jnp.exp(masked - largest[..., None]), axis=-1)
        return (largest, total)

    tops, totals = lax.map(stats_one, (query_group, kv_flat, key_valid))

    def combine(pair_one, pair_two):
        larger = jnp.maximum(pair_one[0], pair_two[0])
        return (
            larger,
            pair_one[1] * jnp.exp(pair_one[0] - larger)
            + pair_two[1] * jnp.exp(pair_two[0] - larger),
        )

    tops, totals = merged((tops, totals), "psg", combine)
    log_total = tops + jnp.log(totals)

    def values_one(item):
        masked = masked_scores(item[0], item[1], item[2])
        probs_low = jnp.exp(masked - item[3][..., None]).astype(jnp.bfloat16)
        values_part = item[1][:, width:].reshape(key_count, heads_local, HD)
        weighted = jnp.einsum(
            "hij,jhd->ihd", probs_low, values_part, preferred_element_type=jnp.float32
        )
        return weighted.reshape(target_span, width)

    partial_out = lax.map(values_one, (query_group, kv_flat, key_valid, log_total))
    attn_two = lax.psum_scatter(partial_out, "psg", scatter_dimension=0, tiled=True).astype(
        jnp.bfloat16
    )
    cross_out_own = own_columns(cross_out, head_index, width)
    second = first + over_heads(right_mul(attn_two, cross_out_own))
    normed_three = rms_plain(second, gain_all[2]).astype(jnp.bfloat16)
    ff_weight = jnp.concatenate(
        [own_columns(gate_full, head_index, ff_local), own_columns(up_full, head_index, ff_local)],
        axis=1,
    )
    gate_up = left_mul(normed_three, ff_weight)
    gate_part = gate_up[..., :ff_local]
    up_part = gate_up[..., ff_local:]
    activated = gated(gate_part, up_part).astype(jnp.bfloat16)
    down_own = own_columns(down_full, head_index, ff_local)
    output = second + over_heads(right_mul(activated, down_own))
    row_valid = (positions[None, :] < target_lengths[:, None])[:, :, None]
    out_hidden = jnp.where(row_valid, output, 0.0)
    grad_out = jnp.where(row_valid, cotangent.astype(jnp.float32), 0.0)
    grad_out_low = grad_out.astype(jnp.bfloat16)
    grad_down = row_outer(grad_out_low, activated)
    grad_act = left_mul(grad_out_low, down_own)
    gate_value, pull_gate = jax.vjp(gated, gate_part, up_part)
    grad_gate, grad_up = pull_gate(grad_act)
    grad_gate_up = jnp.concatenate([grad_gate, grad_up], axis=-1).astype(jnp.bfloat16)
    grad_ff_weight = row_outer(normed_three, grad_gate_up)
    grad_normed_three = over_heads(right_mul(grad_gate_up, ff_weight))
    norm_value, pull_three = jax.vjp(rms_plain, second, gain_all[2])
    grad_second_norm, grad_gain_three = pull_three(grad_normed_three)
    grad_two = grad_out + grad_second_norm
    grad_two_low = grad_two.astype(jnp.bfloat16)
    grad_cross_out = row_outer(grad_two_low, attn_two)
    grad_attn_two = left_mul(grad_two_low, cross_out_own).astype(jnp.bfloat16)
    grad_attn_group = lax.all_gather(grad_attn_two, "psg", axis=0, tiled=True)

    def prob_pieces(item):
        masked = masked_scores(item[0], item[1], item[2])
        probs = jnp.exp(masked - item[3][..., None])
        values_part = item[1][:, width:].reshape(key_count, heads_local, HD)
        grad_rows = item[4].reshape(target_span, heads_local, HD)
        grad_probs = jnp.einsum(
            "ihd,jhd->hij", grad_rows, values_part, preferred_element_type=jnp.float32
        )
        return (probs, grad_probs)

    def delta_one(item):
        probs, grad_probs = prob_pieces(item)
        return jnp.sum(probs * grad_probs, axis=-1)

    delta_part = lax.map(delta_one, (query_group, kv_flat, key_valid, log_total, grad_attn_group))
    delta = lax.psum(delta_part, "psg")

    def grads_one(item):
        probs, grad_probs = prob_pieces(item[:5])
        grad_scores = (probs * (grad_probs - item[5][..., None])).astype(jnp.bfloat16)
        probs_low = probs.astype(jnp.bfloat16)
        query_heads = item[0].reshape(target_span, heads_local, HD)
        keys_part = item[1][:, :width].reshape(key_count, heads_local, HD)
        grad_rows = item[4].reshape(target_span, heads_local, HD)
        grad_query = jnp.einsum(
            "hij,jhd->ihd", grad_scores, keys_part, preferred_element_type=jnp.float32
        )
        grad_keys = jnp.einsum(
            "hij,ihd->jhd", grad_scores, query_heads, preferred_element_type=jnp.float32
        )
        grad_values = jnp.einsum(
            "hij,ihd->jhd", probs_low, grad_rows, preferred_element_type=jnp.float32
        )
        grad_kv = jnp.concatenate(
            [grad_keys.reshape(key_count, width), grad_values.reshape(key_count, width)], axis=-1
        ).astype(jnp.bfloat16)
        return (grad_query.reshape(target_span, width), grad_kv)

    grad_query_group, grad_kv_flat = lax.map(
        grads_one, (query_group, kv_flat, key_valid, log_total, grad_attn_group, delta)
    )
    grad_query_cross = lax.psum_scatter(
        grad_query_group, "psg", scatter_dimension=0, tiled=True
    ).astype(jnp.bfloat16)
    grad_cross_query = row_outer(normed_two, grad_query_cross)
    grad_normed_two = over_heads(right_mul(grad_query_cross, cross_query_own))
    norm_value_two, pull_two = jax.vjp(rms_plain, first, gain_all[1])
    grad_first_norm, grad_gain_two = pull_two(grad_normed_two)
    grad_one = grad_two + grad_first_norm
    grad_kv = grad_kv_flat.reshape(group_count, passages_local, passage_span, 2 * width)
    grad_back = lax.all_to_all(
        grad_kv.reshape(group_count, passages_local, passage_span, 1, 2 * width),
        "head",
        split_axis=2,
        concat_axis=3,
        tiled=True,
    )
    d_encodings = jnp.einsum(
        "qptgc,dgc->tpqd", grad_back, kv_split, preferred_element_type=jnp.float32
    )
    grad_split = jnp.einsum(
        "tpqd,qptgc->dgc", encodings, grad_back, preferred_element_type=jnp.float32
    )
    grad_cross_key = grad_split[:, :, :width].reshape(grad_split.shape[0], total_width)
    grad_cross_value = grad_split[:, :, width:].reshape(grad_split.shape[0], total_width)
    grad_one_low = grad_one.astype(jnp.bfloat16)
    grad_self_out = row_outer(grad_one_low, attn_one)
    grad_attn_one = left_mul(grad_one_low, self_out_own).astype(jnp.bfloat16)
    grad_attn_one = grad_attn_one.reshape(query_rows, target_span, heads_local, HD)
    grad_probs_self = jnp.einsum(
        "qihd,qjhd->qhij", grad_attn_one, values_self, preferred_element_type=jnp.float32
    )
    grad_scores_self = probs_self * (
        grad_probs_self - jnp.sum(probs_self * grad_probs_self, axis=-1, keepdims=True)
    )
    grad_table = jnp.einsum(
        "ijb,hij->bh",
        buckets_hot,
        jnp.sum(grad_scores_self, axis=0),
        precision=lax.Precision.HIGHEST,
    )
    grad_scores_low = grad_scores_self.astype(jnp.bfloat16)
    grad_query_self = jnp.einsum(
        "qhij,qjhd->qihd", grad_scores_low, keys_self, preferred_element_type=jnp.float32
    )
    grad_key_self = jnp.einsum(
        "qhij,qihd->qjhd", grad_scores_low, queries_self, preferred_element_type=jnp.float32
    )
    grad_value_self = jnp.einsum(
        "qhij,qihd->qjhd", probs_self_low, grad_attn_one, preferred_element_type=jnp.float32
    )
    grad_qkv = jnp.concatenate(
        [
            grad_query_self.reshape(query_rows, target_span, width),
            grad_key_self.reshape(query_rows, target_span, width),
            grad_value_self.reshape(query_rows, target_span, width),
        ],
        axis=-1,
    ).astype(jnp.bfloat16)
    grad_qkv_weight = row_outer(normed_one, grad_qkv)
    grad_normed_one = over_heads(right_mul(grad_qkv, qkv_weight))
    norm_value_one, pull_one = jax.vjp(rms_plain, hidden, gain_all[0])
    grad_hidden_norm, grad_gain_one = pull_one(grad_normed_one)
    d_hidden = grad_one + grad_hidden_norm
    grad_gains = jnp.stack([grad_gain_one, grad_gain_two, grad_gain_three])
    d_gains, d_rel_table = lax.psum((grad_gains, grad_table), ("dp", "psg"))
    own_grads = [
        grad_qkv_weight[:, :width],
        grad_qkv_weight[:, width : 2 * width],
        grad_qkv_weight[:, 2 * width :],
        grad_self_out,
        grad_cross_query,
        grad_cross_out,
        grad_ff_weight[:, :ff_local],
        grad_ff_weight[:, ff_local:],
        grad_down,
    ]
    row_sums = lax.psum_scatter(tuple(own_grads), ("dp", "psg"), scatter_dimension=0, tiled=True)
    owned = (
        lax.all_to_all(row_sums[0], "head", split_axis=0, concat_axis=1, tiled=True),
        lax.all_to_all(row_sums[1], "head", split_axis=0, concat_axis=1, tiled=True),
        lax.all_to_all(row_sums[2], "head", split_axis=0, concat_axis=1, tiled=True),
        lax.all_to_all(row_sums[3], "head", split_axis=0, concat_axis=1, tiled=True),
        lax.all_to_all(row_sums[4], "head", split_axis=0, concat_axis=1, tiled=True),
        lax.all_to_all(row_sums[5], "head", split_axis=0, concat_axis=1, tiled=True),
        lax.all_to_all(row_sums[6], "head", split_axis=0, concat_axis=1, tiled=True),
        lax.all_to_all(row_sums[7], "head", split_axis=0, concat_axis=1, tiled=True),
        lax.all_to_all(row_sums[8], "head", split_axis=0, concat_axis=1, tiled=True),
    )
    key_done, value_done = (
        lax.psum_scatter(grad_cross_key, ("dp", "psg", "head"), scatter_dimension=0, tiled=True),
        lax.psum_scatter(grad_cross_value, ("dp", "psg", "head"), scatter_dimension=0, tiled=True),
    )
    return (
        out_hidden,
        d_hidden,
        d_encodings,
        d_gains,
        d_rel_table,
        owned[0],
        owned[1],
        owned[2],
        owned[3],
        owned[4],
        key_done,
        value_done,
        owned[5],
        owned[6],
        owned[7],
        owned[8],
    )


PLACED = (
    P(("dp", "psg"), None, None),
    P("head", "psg", "dp", None),
    P("psg", "dp"),
    P(("dp", "psg")),
    P(),
    P(),
    P(None, "head"),
    P(("dp", "psg", "head"), None),
    P(("dp", "psg", "head"), None),
    P(("dp", "psg", "head"), None),
    P(("dp", "psg", "head"), None),
    P(("dp", "psg", "head"), None),
    P(("dp", "psg", "head"), None),
    P(("dp", "psg", "head"), None),
    P(("dp", "psg", "head"), None),
    P(("dp", "psg", "head"), None),
    P(("dp", "psg", "head"), None),
    P(("dp", "psg", "head"), None),
    P(("dp", "psg"), None, None),
)

OUTS = (
    P(("dp", "psg"), None, None),
    P(("dp", "psg"), None, None),
    P("head", "psg", "dp", None),
    P(),
    P(None, "head"),
    P(("dp", "psg", "head"), None),
    P(("dp", "psg", "head"), None),
    P(("dp", "psg", "head"), None),
    P(("dp", "psg", "head"), None),
    P(("dp", "psg", "head"), None),
    P(("dp", "psg", "head"), None),
    P(("dp", "psg", "head"), None),
    P(("dp", "psg", "head"), None),
    P(("dp", "psg", "head"), None),
    P(("dp", "psg", "head"), None),
    P(("dp", "psg", "head"), None),
)


def solution(mesh):
    def local(*args):
        rows, span, heads = args[7].shape[0], args[1].shape[0], args[6].shape[1]
        fits = (mesh.shape["dp"], mesh.shape["psg"], mesh.shape["head"], heads) == (2, 4, 4, 3)
        fits = fits and (4 * rows) % 16 == 0 and rows % 8 == 0
        return (local_fast if fits else local_plain)(*args)

    placed = PLACED
    return jax.shard_map(local, mesh=mesh, in_specs=placed, out_specs=OUTS, check_vma=False)
```

```python
import functools

import jax
import jax.numpy as jnp
from jax import lax
from jax.experimental import pallas as pl
from jax.experimental.pallas import tpu as pltpu
from jax.sharding import PartitionSpec as P

HD = 64
EPSILON = 1e-06
NEGATIVE = -1e30
AUG = 64
BF = jnp.bfloat16
F32 = jnp.float32
MESH = pl.DeviceIdType.MESH
VMEM = pltpu.VMEM


def nn(a, b):
    return lax.dot_general(a, b, (((1,), (0,)), ((), ())), preferred_element_type=F32)


def nt(a, b):
    return lax.dot_general(a, b, (((1,), (1,)), ((), ())), preferred_element_type=F32)


def tn(a, b):
    return lax.dot_general(a, b, (((0,), (0,)), ((), ())), preferred_element_type=F32)


def rms_scale(v):
    return lax.rsqrt(jnp.mean(v * v, axis=-1, keepdims=True) + EPSILON)


def rms_norm(v, gain):
    return v * rms_scale(v) * gain


def rms_back(dn, v, gain):
    r = rms_scale(v)
    gd = gain * dn
    dv = r * gd - v * (r * r * r * jnp.mean(gd * v, axis=-1, keepdims=True))
    dg = jnp.sum(dn * v * r, axis=0, keepdims=True)
    return dv, dg


def iota(shape, axis):
    return lax.broadcasted_iota(jnp.int32, shape, axis)


class Net:
    def __init__(self, send_sems, recv_sems):
        self.send_sems, self.recv_sems, self.count, self.sent = send_sems, recv_sems, 0, []

    def send(self, src, dst, **device):
        at = self.count
        self.count += 1
        copy = pltpu.make_async_remote_copy(
            src, dst, self.send_sems.at[at], self.recv_sems.at[at],
            device_id=device, device_id_type=MESH,
        )
        copy.start()
        self.sent.append(copy)
        return copy

    def finish(self):
        for copy in self.sent:
            copy.wait_send()


def places():
    d, z, h = lax.axis_index("dp"), lax.axis_index("psg"), lax.axis_index("head")
    return dict(
        c=(h % 2, dict(head=h ^ 1)), x=(h // 2, dict(head=h ^ 2)), y=(d, dict(dp=1 - d)),
        a=(z // 2, dict(psg=z ^ 3)), b=(z % 2, dict(psg=z ^ 1)),
    )


class Doubling:
    def __init__(self, net, ref, names, order, late=()):
        self.net, self.ref, self.names, self.order, self.at = net, ref, names, order, places()
        self.late = [order.index(n) + 1 for n in late]
        self.sent = {s: [] if s in self.late else [self.go(0, s)] for s in range(1, len(order) + 1)}

    def region(self, j):
        idx = []
        for n in self.names:
            p, mine = self.order.index(n) + 1, self.at[n][0]
            idx.append(mine if p > j else (1 - mine if p == j else slice(None)))
        return self.ref.at[tuple(idx)]

    def go(self, j, s):
        block = self.region(j)
        return self.net.send(block, block, **self.at[self.order[s - 1]][1])

    def open(self, name, have):
        s = self.order.index(name) + 1
        self.late.remove(s)
        self.sent[s] = [self.go(i, s) for i in range(have + 1)]

    def step(self, name):
        j = self.order.index(name) + 1
        for c in self.sent[j]:
            c.wait_recv()
        for s in range(j + 1, len(self.order) + 1):
            if s not in self.late:
                self.sent[s].append(self.go(j, s))
            elif s == j + 1:
                self.sent[s] = [self.go(i, s) for i in range(s)]


class Halving:
    def __init__(self, net, src, names, order, bufs, total, shard):
        self.net, self.src, self.names, self.order, self.bufs = net, src, names, order, bufs
        self.total, self.shard, self.at, self.stage = total, shard, places(), 0

    def index(self, stage, last, free):
        idx, free = [], list(free)
        for n in self.names:
            p, mine = self.order.index(n), self.at[n][0]
            idx.append(mine if p < stage else (last(mine) if p == stage else free.pop(0)))
        return tuple(idx)

    def push(self):
        n = len(self.order) - self.stage - 1
        far = self.src.at[self.index(self.stage, lambda m: 1 - m, [slice(None)] * n)]
        self.copy = self.net.send(far, self.bufs[self.stage], **self.at[self.order[self.stage]][1])

    def pull(self):
        self.copy.wait_recv()
        n = len(self.order) - self.stage - 1
        buf = self.bufs[self.stage]
        if n == 0:
            idx = self.index(self.stage, lambda m: m, [])
            self.total[...] = self.src[idx].astype(F32) + buf[...].astype(F32)
        else:
            def add(i, carry):
                bits = [(i // 2**k) % 2 for k in range(n)]
                idx = self.index(self.stage, lambda m: m, bits)
                self.src[idx] = (self.src[idx].astype(F32) + buf[tuple(bits)].astype(F32)).astype(BF)
                return carry

            lax.fori_loop(0, 2**n, add, 0)
        self.stage += 1
        if n:
            self.push()
        else:
            self.trade()

    def trade(self):
        n, h = self.shard.shape[1], lax.axis_index("head")

        def rows(hh):
            return pl.ds(pl.multiple_of(n * hh, n), n)

        self.last = [self.net.send(self.total.at[rows(h ^ m)], self.shard.at[h], head=h ^ m) for m in (2, 3, 1)]
        self.shard[h] = self.total[rows(h), :]

    def done(self):
        for c in self.last:
            c.wait_recv()


def enter():
    barrier = pltpu.get_barrier_semaphore()
    d, z, h = lax.axis_index("dp"), lax.axis_index("psg"), lax.axis_index("head")
    peers = [dict(head=h ^ m) for m in (1, 2, 3)]
    peers += [dict(psg=lax.rem(z + m, 4)) for m in (1, 2, 3)]
    peers += [dict(dp=1 - d)]
    for peer in peers:
        pl.semaphore_signal(barrier, inc=1, device_id=peer, device_id_type=MESH)
    pl.semaphore_wait(barrier, len(peers))
    return d, z, h


ORDER = (1, 3, 2, 0)


class Gather:
    def __init__(self, net, buf, z, h, rows):
        self.net, self.buf, self.z, self.h, self.rows = net, buf, z, h, rows
        mine = self.at(z, h)
        self.ring = {m: net.send(mine, mine, psg=lax.rem(z + m, 4)) for m in (1, 3, 2)}
        self.hops = {0: self.on(z)}
        self.last = {}

    def at(self, zz, hh):
        return self.buf.at[zz, pl.ds(pl.multiple_of(self.rows * hh, self.rows), self.rows)]

    def on(self, zz):
        block = self.at(zz, self.h)
        return [self.net.send(block, block, head=self.h ^ 2), self.net.send(block, block, head=self.h ^ 1)]

    def source(self, m):
        return lax.rem(self.z - m + 4, 4)

    def relay(self):
        for m in (1, 3, 2):
            self.ring[m].wait_recv()
            self.hops[m] = self.on(self.source(m))
        for m in ORDER:
            self.hops[m][0].wait_recv()
            block = self.at(self.source(m), self.h ^ 2)
            self.last[m] = self.net.send(block, block, head=self.h ^ 1)

    def ready(self, m):
        self.hops[m][1].wait_recv()
        self.last[m].wait_recv()


def kernel_one(
    plen, tlen,
    table, hid, ench, buckets, gains, sq, sk, sv, so, cq, ck, cv, co, fg, fu, fd, cot,
    FAH, FKH, GQH, KPH, VPH, KTH, ETH, PSH, QA, QKV, AOS, FIRST, G2, DO, GFH, DG3, OUT, N2, ATO,
    PQ, PA, PK, PC, PG, AQ, AA, AK, AC, AG,
    FA, FK, FC, GQ, GG, KP, VP, KT, VT, ET, PS, AO, GF,
    enc, QU, BIAS, OS, ST, OC, SC, OXS, SXS, OX, SX, OZS, SZS, OZ, SZ,
    OWN, SOWN, ATS, AT, N3, R3S, R3, R1S, R1, QM,
    ss, rs, ls,
):
    d, z, h = enter()
    net = Net(ss, rs)
    T, D = hid.shape
    R = T // 4
    W = 3 * HD
    hc, hx = h % 2, h // 2
    e = 1 - d
    zp, zm, zo = lax.rem(z + 1, 4), lax.rem(z + 3, 4), lax.rem(z + 2, 4)
    kept = []

    def keep_out(src, dst):
        c = pltpu.make_async_copy(src, dst, ls.at[len(kept)])
        c.start()
        kept.append(c)

    count = ench.shape[1]
    e_load = pltpu.make_async_copy(ench, enc.at[:, pl.ds(0, count)], ls.at[11])
    e_load.start()

    F = fg.shape[1] // 4

    def pack(dst, names):
        for g in range(4):
            s = slice(W * g, W * g + W)
            parts = [r[...].astype(F32)[:, s] for r in names]
            dst[g] = (jnp.concatenate(parts, axis=1) if len(parts) > 1 else parts[0]).astype(BF)

    def trade(src, dst):
        cs = [net.send(src.at[h ^ m], dst.at[h], head=h ^ m) for m in (2, 3, 1)]
        dst[h] = src[h]
        return cs

    pack(PQ, (sq, sk, sv))
    tq = trade(PQ, AQ)
    pack(PA, (so, cq))
    ta = trade(PA, AA)
    pack(PK, (ck, cv))
    tk = trade(PK, AK)
    pack(PC, (co,))
    for g in range(4):
        for i, ref in enumerate((fg, fu, fd)):
            PG[g, :, F * i : F * i + F] = ref[:, F * g : F * g + F]
    tc = trade(PC, AC)
    tg = trade(PG, AG)

    def assemble(cs, src, dst):
        for c in cs:
            c.wait_recv()
        dst[...] = jnp.concatenate([src[j].astype(F32) for j in range(4)], axis=0).astype(BF)

    full, own = tuple("cxyab"), tuple("yab")
    za, zb = z // 2, z % 2
    assemble(tq, AQ, GQ.at[d, za, zb])
    wq = Doubling(net, GQ, own, tuple("bay"))
    assemble(ta, AA, FA.at[hc, hx, d, za, zb])
    wa = Doubling(net, FA, full, tuple("baxyc"))
    assemble(tk, AK, FK.at[hc, hx, d, za, zb])
    wk = Doubling(net, FK, full, tuple("bayxc"))
    g0 = gains[0:1].astype(F32)
    hidden = hid[...].astype(F32)
    n1 = rms_norm(hidden, g0).astype(BF)

    def flip(q, carry):
        ET[q] = enc[q].astype(F32).T.astype(BF)
        return carry

    assemble(tc, AC, FC.at[hc, hx, d, za, zb])
    assemble(tg, AG, GG.at[d, za, zb])
    for w in (wq, wk, wa):
        w.step("b")
    e_load.wait()
    enc[:, count:, :] = jnp.zeros((enc.shape[0], enc.shape[1] - count, D), BF)
    lax.fori_loop(0, 2, flip, 0)
    for w in (wq, wa, wk):
        w.step("a")
    wc = Doubling(net, FC, full, tuple("bayxc"), ("x", "c"))
    wg = Doubling(net, GG, own, tuple("bay"), ("y",))
    lax.fori_loop(2, 4, flip, 0)
    bk = buckets[...]
    tab = table[...].astype(F32)
    for a in range(3):
        acc = jnp.zeros((T, T), F32)
        for i in range(tab.shape[1]):
            acc = jnp.where(bk == i, tab[a : a + 1, i : i + 1], acc)
        BIAS[a] = acc
    wa.step("x")
    wk.step("y")
    wg.open("y", 0)
    wq.step("y")

    wqkv = GQ[...].reshape(D, 3 * W)
    QKV[...] = nn(n1, wqkv).astype(BF)
    keep_out(GQ, GQH)
    wk.step("x")
    wc.step("b")
    wg.step("b")
    qs, ks, vs = QKV[:, 0:W], QKV[:, W : 2 * W], QKV[:, 2 * W : 3 * W]
    lane = iota((T, W), 1)
    row, col = iota((T, T), 0), iota((T, T), 1)
    keep = (col <= row) & (col < tlen[0])
    acc = jnp.zeros((T, W), F32)
    zero = jnp.zeros((T, W), BF)
    for a in range(3):
        mine = (lane >= HD * a) & (lane < HD * a + HD)
        s = nt(jnp.where(mine, qs, zero), ks) + BIAS[a]
        s = jnp.where(keep, s, NEGATIVE)
        ex = jnp.exp(s - jnp.max(s, axis=-1, keepdims=True))
        p = ex / jnp.sum(ex, axis=-1, keepdims=True)
        PS[a] = p
        acc += nn(p.astype(BF), jnp.where(mine, vs, zero))
    AOS[...] = acc.astype(BF)
    ao = [net.send(AOS.at[pl.ds(pl.multiple_of(R * (h ^ m), R), R)], AO.at[h], head=h ^ m) for m in (2, 3, 1)]
    AO[h] = AOS[pl.ds(pl.multiple_of(R * h, R), R), :]
    keep_out(PS, PSH)
    wa.step("y")
    wa.step("c")
    for c in ao:
        c.wait_recv()

    def part(ref, g, i=None):
        blk = ref[g % 2, g // 2] if i is None else ref[g % 2, g // 2, :, :, :, :, W * i : W * i + W]
        return blk.reshape(D, blk.shape[-1])

    mine_rows = pl.ds(pl.multiple_of(R * h, R), R)
    first = hid[mine_rows, :].astype(F32)
    for g in range(4):
        first += nt(AO[g], part(FA, g, 0))
    FIRST[...] = first
    n2 = rms_norm(first, gains[1:2].astype(F32)).astype(BF)
    N2[mine_rows, :] = n2
    QA[z, mine_rows, :] = jnp.concatenate([nn(n2, part(FA, g, 1)) for g in range(4)], axis=1).astype(BF)
    spreadq = Gather(net, QA, z, h, R)
    n2c = [net.send(N2.at[mine_rows], N2.at[mine_rows], head=h ^ m) for m in (2, 3, 1)]
    keep_out(FA, FAH)
    wk.step("c")
    keep_out(FK, FKH)

    tok = enc.shape[1]
    krow, klane = iota((tok, AUG), 0), iota((tok, AUG), 1)
    per = 96
    npass = plen.shape[1]
    vaug = jnp.where(klane < 9, -1.0, 0.0).astype(F32)

    def project(q, carry):
        dead = krow >= per * npass
        for p in range(npass):
            inside = (krow >= per * p) & (krow < per * p + per)
            dead = dead | (inside & (krow - per * p + per * h >= plen[q, p]))
        kaug = jnp.where(klane == 9, jnp.where(dead, NEGATIVE, 0.0), vaug)

        def group(g, c2):
            kv = nn(enc[q], FK[g % 2, g // 2].reshape(D, 2 * W))
            k, v = kv[:, :W], kv[:, W:]
            KP[q, g] = jnp.concatenate([k, kaug], axis=1).astype(BF)
            VP[q, g] = jnp.concatenate([v, vaug], axis=1).astype(BF)
            KT[q, g] = k.T.astype(BF)
            VT[q, g] = v.T.astype(BF)
            return c2

        lax.fori_loop(0, 4, group, 0)
        return carry

    lax.fori_loop(0, 2, project, 0)
    spreadq.relay()
    wc.step("a")
    wg.step("a")
    lax.fori_loop(2, 4, project, 0)
    for src, dst in ((KP, KPH), (VP, VPH), (KT, KTH), (ET, ETH)):
        keep_out(src, dst)

    qaug = jnp.where(iota((T, AUG), 1) == 9, 1.0, 0.0).astype(BF)

    def weights(m1, l1, m2, l2):
        top = jnp.maximum(m1, m2)
        w1, w2 = l1 * jnp.exp(m1 - top), l2 * jnp.exp(m2 - top)
        return top, w1 + w2, w1, w2

    def spread(x):
        return jnp.concatenate([jnp.broadcast_to(x[a : a + 1], (HD, T)) for a in range(3)], axis=0)

    def join(o1, s1, o2, s2):
        top, tot, w1, w2 = weights(s1[0:3], s1[3:6], s2[0:3], s2[3:6])
        o = o1 * spread(w1 / tot) + o2 * spread(w2 / tot)
        return o, jnp.concatenate([top, tot, jnp.zeros((2, T), F32)], axis=0)

    def attend(i, zz):
        for g in range(4):
            QU[g] = QA[zz, :, W * g : W * g + W]

        def group(g, carry):
            qg, kg = QU[g], KP[zz, g]
            outs, tops, tots = [], [], []
            for a in range(3):
                mine = (lane >= HD * a) & (lane < HD * a + HD)
                qm = jnp.concatenate([jnp.where(mine, qg, zero), qaug], axis=1)
                s = nt(kg, qm)
                m = jnp.max(s, axis=0, keepdims=True)
                ex = jnp.exp(s - m)
                l = jnp.sum(ex, axis=0, keepdims=True)
                o = nn(VT[zz, g, HD * a : HD * a + HD, :], ex.astype(BF))
                outs.append(o / l)
                tops.append(m)
                tots.append(l)
            gc, gx = g % 2, g // 2
            OS[i, gc, gx] = jnp.concatenate(outs, axis=0).astype(BF)
            ST[i, gc, gx] = jnp.concatenate(tops + tots + [jnp.zeros((2, T), F32)], axis=0)
            return carry

        lax.fori_loop(0, 4, group, 0)

    q_core, q_x, q_z = {}, {}, {}

    def core_stage(i):
        q_core[i] = (net.send(OS.at[i, 1 - hc], OC.at[i], head=h ^ 1), net.send(ST.at[i, 1 - hc], SC.at[i], head=h ^ 1))

    def x_stage(i):
        for c in q_core[i]:
            c.wait_recv()
        o, s = join(OS[i, hc, 1 - hx].astype(F32), ST[i, hc, 1 - hx], OC[i, 1 - hx].astype(F32), SC[i, 1 - hx])
        OXS[i] = o.astype(BF)
        SXS[i] = s
        q_x[i] = (net.send(OXS.at[i], OX.at[i], head=h ^ 2), net.send(SXS.at[i], SX.at[i], head=h ^ 2))
        o, s = join(OS[i, hc, hx].astype(F32), ST[i, hc, hx], OC[i, hx].astype(F32), SC[i, hx])
        OWN[i] = o
        SOWN[i] = s

    def z_stage(i):
        for c in q_x[i]:
            c.wait_recv()
        o, s = join(OWN[i], SOWN[i], OX[i].astype(F32), SX[i])
        if i < 3:
            m = ORDER[i]
            OZS[i] = o.astype(BF)
            SZS[i] = s
            to = lax.rem(z - m + 4, 4)
            q_z[i] = (net.send(OZS.at[i], OZ.at[i], psg=to), net.send(SZS.at[i], SZ.at[i], psg=to))
        else:
            OWN[i] = o
            SOWN[i] = s

    for i, m in enumerate(ORDER):
        zz = lax.rem(z - m + 4, 4)
        spreadq.ready(m)
        attend(i, zz)
        if i < 2:
            wc.step(("y", "x")[i])
        core_stage(i)
        if i >= 1:
            x_stage(i - 1)
        if i >= 2:
            z_stage(i - 2)
    x_stage(3)
    z_stage(2)
    z_stage(3)
    o, s = OWN[3], SOWN[3]
    for i in range(3):
        for c in q_z[i]:
            c.wait_recv()
        o, s = join(o, s, OZ[i].astype(F32), SZ[i])
    lse = s[0:3] + jnp.log(s[3:6])
    full = jnp.concatenate([o, lse, jnp.zeros((AUG - 3, T), F32)], axis=0)
    ATS[...] = full.T
    ATO[...] = ATS[:, 0:W].astype(BF)
    for c in n2c:
        c.wait_recv()
    at = [net.send(ATS.at[pl.ds(pl.multiple_of(R * (h ^ m), R), R)], AT.at[h], head=h ^ m) for m in (1, 2, 3)]
    AT[h] = ATS[mine_rows, :]
    wc.step("c")
    for c in at:
        c.wait_recv()
    second = FIRST[...]
    for g in range(4):
        low = AT[g, :, 0:W].astype(BF)
        second += nt(low, part(FC, g))
    g2gain = gains[2:3].astype(F32)
    N3[mine_rows, :] = rms_norm(second, g2gain).astype(BF)
    n3c = [net.send(N3.at[mine_rows], N3.at[mine_rows], head=h ^ m) for m in (2, 3, 1)]
    rowid = iota((T, 1), 0)
    go_low = jnp.where(rowid < tlen[0], cot[...], jnp.zeros((T, D), BF))
    wg.step("y")
    for c in n3c:
        c.wait_recv()
    wdown = GG[:, :, :, :, 2 * F : 3 * F].reshape(D, F)
    wgu = GG[:, :, :, :, 0 : 2 * F].reshape(D, 2 * F)
    d_act = nn(go_low, wdown)
    n3 = N3[...]
    gate_up = nn(n3, wgu)
    gate, up = gate_up[:, :F], gate_up[:, F:]
    c0 = 0.7978845608028654
    inner = c0 * (gate + 0.044715 * gate * gate * gate)
    th = jnp.tanh(inner)
    gel = 0.5 * gate * (1.0 + th)
    act = (gel * up).astype(BF)
    dgel = 0.5 * (1.0 + th) + 0.5 * gate * (1.0 - th * th) * (c0 * (1.0 + 3 * 0.044715 * gate * gate))
    dgu = jnp.concatenate([d_act * up * dgel, d_act * gel], axis=1).astype(BF)
    R3S[...] = nt(dgu, wgu).astype(BF)
    r3 = [net.send(R3S.at[pl.ds(pl.multiple_of(R * (h ^ m), R), R)], R3.at[h], head=h ^ m) for m in (2, 3, 1)]
    R1S[...] = nt(act, wdown).astype(BF)
    r1 = [net.send(R1S.at[pl.ds(pl.multiple_of(R * (h ^ m), R), R)], R1.at[h], head=h ^ m) for m in (2, 3, 1)]
    R3[h] = R3S[mine_rows, :]
    R1[h] = R1S[mine_rows, :]
    GF[:, :, :, :, 2 * F : 3 * F] = tn(go_low, act).astype(BF).reshape(2, 2, 2, D // 8, F)
    GF[:, :, :, :, 0 : 2 * F] = tn(n3, dgu).astype(BF).reshape(2, 2, 2, D // 8, 2 * F)
    keep_out(GF, GFH)
    for c in r3:
        c.wait_recv()
    dn3 = R3[0].astype(F32) + R3[1].astype(F32) + R3[2].astype(F32) + R3[3].astype(F32)
    live = (iota((R, 1), 0) + R * h) < tlen[0]
    go = jnp.where(live, cot[mine_rows, :].astype(F32), 0.0)
    dv, dg = rms_back(dn3, second, g2gain)
    DG3[...] = jnp.concatenate([dg, jnp.zeros((7, D), F32)], axis=0)
    g2 = go + dv
    G2[...] = g2
    g2_low = g2.astype(BF)
    alane = iota((R, 2 * AUG), 1)
    wl = iota((R, W), 1)
    aug = jnp.zeros((R, 2 * AUG), F32)
    dos = []

    def parts(x):
        hi_ = x.astype(BF).astype(F32)
        mid = (x - hi_).astype(BF).astype(F32)
        return hi_, mid, x - hi_ - mid

    for g in range(4):
        do = nn(g2_low, part(FC, g)).astype(BF)
        dos.append(do.astype(F32))
        prod = do.astype(F32) * AT[g, :, 0:W]
        for a in range(3):
            delta = jnp.sum(jnp.where((wl >= HD * a) & (wl < HD * a + HD), prod, 0.0), axis=1, keepdims=True)
            for off, val in ((0, AT[g, :, W + a : W + a + 1]), (AUG, delta)):
                for j, piece in enumerate(parts(val)):
                    aug = jnp.where(alane == off + 9 * g + 3 * a + j, piece, aug)
    DO[...] = jnp.concatenate(dos + [aug], axis=1).astype(BF)
    for c in r1:
        c.wait_recv()
    out = second + R1[0].astype(F32) + R1[1].astype(F32) + R1[2].astype(F32) + R1[3].astype(F32)
    OUT[...] = jnp.where(live, out, 0.0)
    for c in kept:
        c.wait()
    net.finish()


def call_one(plen, tlen, table, hid, enc, buckets, gains, mats, cot):
    T, D = hid.shape
    R = T // 4
    W = 3 * HD
    rows = mats[0].shape[0]
    F = mats[8].shape[1] // 4
    tok = -(-enc.shape[1] // 128) * 128
    S = jax.ShapeDtypeStruct
    blk = 4 * rows
    big = dict(
        FA=((2, 2, 2, 2, 2, blk, 2 * W), BF), FK=((2, 2, 2, 2, 2, blk, 2 * W), BF), FC=((2, 2, 2, 2, 2, blk, W), BF),
        GQ=((2, 2, 2, blk, 3 * W), BF),
        KP=((4, 4, tok, W + AUG), BF), VP=((4, 4, tok, W + AUG), BF), KT=((4, 4, W, tok), BF),
        ET=((4, D, tok), BF), PS=((3, T, T), F32),
        GF=((2, 2, 2, blk, 3 * F), BF),
    )
    order = list(big)
    outs = {n: big[n] for n in order[:2] + order[3:9]}
    outs.update(
        QA=((4, T, D), BF), QKV=((T, 3 * W), BF), AO=((T, W), BF), FIRST=((R, D), F32),
        G2=((R, D), F32), DO=((R, D + 2 * AUG), BF),
        GF=big["GF"], DG3=((8, D), F32), OUT=((R, D), F32), N2=((T, D), BF), ATO=((T, W), BF),
    )
    pack = [VMEM((4, rows, w), BF) for w in (3 * W, 2 * W, 2 * W, W, 3 * F)]
    scratch = pack + pack + [
        *[VMEM(*big[n]) for n in order[:4]], VMEM((2, 2, 2, blk, 3 * F), BF),
        *[VMEM(*big[n]) for n in order[4:7]], VMEM((4, 4, W, tok), BF),
        *[VMEM(*big[n]) for n in order[7:9]], VMEM((4, R, W), BF), VMEM(*big["GF"]),
        VMEM((enc.shape[0], tok, D), BF), VMEM((4, T, W), BF), VMEM((3, T, T), F32),
        VMEM((4, 2, 2, W, T), BF), VMEM((4, 2, 2, 8, T), F32),
        VMEM((4, 2, W, T), BF), VMEM((4, 2, 8, T), F32),
        VMEM((4, W, T), BF), VMEM((4, 8, T), F32), VMEM((4, W, T), BF), VMEM((4, 8, T), F32),
        VMEM((3, W, T), BF), VMEM((3, 8, T), F32), VMEM((3, W, T), BF), VMEM((3, 8, T), F32),
        VMEM((4, W, T), F32), VMEM((4, 8, T), F32),
        VMEM((T, W + AUG), F32), VMEM((4, R, W + AUG), F32), VMEM((T, D), BF),
        VMEM((T, D), BF), VMEM((4, R, D), BF), VMEM((T, D), BF), VMEM((4, R, D), BF),
        VMEM((3 * T, W + AUG), BF),
        pltpu.SemaphoreType.DMA((160,)), pltpu.SemaphoreType.DMA((160,)), pltpu.SemaphoreType.DMA((12,)),
    ]
    smem = pl.BlockSpec(memory_space=pltpu.SMEM)
    vm = pl.BlockSpec(memory_space=pltpu.VMEM)
    anym = pl.BlockSpec(memory_space=pl.ANY)
    res = pl.pallas_call(
        kernel_one,
        out_shape=[S(*v) for v in outs.values()],
        in_specs=[smem] * 2 + [vm] * 2 + [anym] + [vm] * 14,
        out_specs=[anym if n in big else vm for n in outs],
        scratch_shapes=scratch,
        name="forward",
        compiler_params=pltpu.CompilerParams(collective_id=1, has_side_effects=True, vmem_limit_bytes=63 << 20),
    )(plen, tlen, table, hid, enc, buckets, gains, *mats, cot)
    return dict(zip(outs, res)), big


def kernel_two(
    buckets, gains, hid, ETH, FAH, FKH, GQH, QA, KPH, VPH, KTH, PSH, QKV, AOO, FIRST, G2, DO, GFH, DG3, OUTR, N2, ATO,
    DENC, DHID, OUT, SM, OF, OC, OK, OA, OL,
    DOB, KP, VP, KT, QAV, ET, FA, FK, GQ, PS,
    QU, DU, QX, DX, QM, DM, DS, PB, DQG, DKV, DQS, DQC, DXR, DOWN, DZS, DZR, DAS, DA, DSF, TBL, NS, NR, DEN,
    FSRC, F1, F2, F3, FTOT, CSRC, C1, C2, C3, CTOT,
    KSRC, K1, K2, K3, K4, K5, KTOT, ASRC, A1, A2, A3, ATOT,
    LSRC, L1, L2, L3, LTOT,
    SMR, DQL, DQO, G1A, G2A,
    ss, rs, ls, es,
):
    d, z, h = enter()
    net = Net(ss, rs)
    T, D = hid.shape
    R = T // 4
    W = 3 * HD
    hc, hx = h % 2, h // 2
    tok = ETH.shape[2]
    mine_rows = pl.ds(pl.multiple_of(R * h, R), R)

    def source(m):
        return lax.rem(z - m + 4, 4)

    def load(pairs, sem):
        cs = [pltpu.make_async_copy(a, b, sem(j)) for j, (a, b) in enumerate(pairs)]
        for c in cs:
            c.start()
        return cs

    def fetch(i):
        zz, slot = source(ORDER[i]), i % 2
        return load(
            [(a.at[zz], b.at[slot]) for a, b in ((KPH, KP), (VPH, VP), (KTH, KT), (QA, QAV))],
            lambda j: ls.at[j, slot],
        )

    DOB[z, mine_rows, :] = DO[...]
    gather = Gather(net, DOB, z, h, R)
    fetched = fetch(0)
    G2A[mine_rows, :] = G2[...].astype(BF)
    g2c = [net.send(G2A.at[mine_rows], G2A.at[mine_rows], head=h ^ m) for m in (2, 3, 1)]
    near = load([(GFH, FSRC)], lambda j: es.at[j])
    full, own = tuple("cxyab"), tuple("yab")
    sf = Halving(net, FSRC, own, tuple("yab"), (F1, F2, F3), FTOT, OF)
    sc = Halving(net, CSRC, own, tuple("yab"), (C1, C2, C3), CTOT, OC)
    sk = Halving(net, KSRC, full, tuple("cxyab"), (K1, K2, K3, K4, K5), KTOT, OK)
    sa = Halving(net, ASRC, own, tuple("yab"), (A1, A2, A3), ATOT, OA)
    sl = Halving(net, LSRC, own, tuple("yab"), (L1, L2, L3), LTOT, OL)
    weights = load([(FAH, FA), (FKH, FK), (GQH, GQ), (PSH, PS)], lambda j: es.at[2 + j])
    gather.relay()
    OUT[mine_rows, :] = OUTR[...]
    for c in near:
        c.wait()

    lane = iota((T, W), 1)
    alane = iota((T, AUG), 1)
    zero = jnp.zeros((T, W), BF)
    azero = jnp.zeros((T, AUG), BF)
    one = jnp.ones((T, 1), F32)
    pad = jnp.zeros((T, AUG - 10), F32)

    def mine_of(a):
        return (lane >= HD * a) & (lane < HD * a + HD)

    def part(ref, g, i=None):
        blk = ref[g % 2, g // 2] if i is None else ref[g % 2, g // 2, :, :, :, :, W * i : W * i + W]
        return blk.reshape(D, blk.shape[-1])

    half = tok // 2

    def attend(i, zz):
        slot = i % 2
        ex = DOB[zz, :, D : D + 2 * AUG].astype(F32)
        for g in range(4):
            QU[g] = QAV[slot, :, W * g : W * g + W]
            DU[g] = DOB[zz, :, W * g : W * g + W]
            QX[g] = jnp.concatenate([ex[:, 9 * g : 9 * g + 9], one, pad], axis=1).astype(BF)
            DX[g] = jnp.concatenate([ex[:, AUG + 9 * g : AUG + 9 * g + 9], one * 0, pad], axis=1).astype(BF)

        def group(g, carry):
            for a in range(3):
                keep = (alane == 9) | ((alane >= 3 * a) & (alane < 3 * a + 3))
                QM[T * a : T * a + T] = jnp.concatenate([jnp.where(mine_of(a), QU[g], zero), jnp.where(keep, QX[g], azero)], axis=1)
                DM[T * a : T * a + T] = jnp.concatenate([jnp.where(mine_of(a), DU[g], zero), jnp.where(keep, DX[g], azero)], axis=1)
            for t in range(0, tok, half):
                kg, vg = KP[slot, g, t : t + half], VP[slot, g, t : t + half]
                for a in range(3):
                    p = jnp.exp(nt(kg, QM[T * a : T * a + T]))
                    ds = p * nt(vg, DM[T * a : T * a + T])
                    DS[t : t + half, T * a : T * a + T] = ds.astype(BF)
                    PB[t : t + half, T * a : T * a + T] = p.astype(BF)
            dk = nn(DS[...], QM[...])
            dv = nn(PB[...], DM[...])
            DKV[zz, g] = jnp.concatenate([dk[:, :W], dv[:, :W]], axis=1).astype(BF)
            dqs = [nn(KT[slot, g, HD * a : HD * a + HD, :], DS[:, T * a : T * a + T]) for a in range(3)]
            DQG[g] = jnp.concatenate(dqs, axis=0).T.astype(BF)
            return carry

        lax.fori_loop(0, 4, group, 0)
        dq = jnp.concatenate([DQG[g] for g in range(4)], axis=1)
        for j in range(4):
            DQS[i, j % 2, j // 2] = dq[R * j : R * j + R]

    q_core, q_x, q_z = {}, {}, {}

    def core_stage(i):
        q_core[i] = net.send(DQS.at[i, 1 - hc], DQC.at[i], head=h ^ 1)

    def x_stage(i):
        q_core[i].wait_recv()
        DQC[i, 1 - hx] = (DQS[i, hc, 1 - hx].astype(F32) + DQC[i, 1 - hx].astype(F32)).astype(BF)
        q_x[i] = net.send(DQC.at[i, 1 - hx], DXR.at[i], head=h ^ 2)
        DOWN[i] = DQS[i, hc, hx].astype(F32) + DQC[i, hx].astype(F32)

    def z_stage(i):
        q_x[i].wait_recv()
        o = DOWN[i] + DXR[i].astype(F32)
        if i < 3:
            DZS[i] = o.astype(BF)
            q_z[i] = net.send(DZS.at[i], DZR.at[i], psg=source(ORDER[i]))
        else:
            DOWN[i] = o

    for i, m in enumerate(ORDER):
        gather.ready(m)
        for c in fetched:
            c.wait()
        if i < 3:
            fetched = fetch(i + 1)
        attend(i, source(m))
        core_stage(i)
        if i >= 1:
            x_stage(i - 1)
        if i >= 2:
            z_stage(i - 2)
        if i == 0:
            for c in g2c:
                c.wait_recv()
            CSRC[...] = tn(G2A[...], ATO[...]).astype(BF).reshape(CSRC.shape)
            sf.push()
            sc.push()
    x_stage(3)
    z_stage(2)
    z_stage(3)
    sf.pull()
    sc.pull()

    def et_copy(n):
        return pltpu.make_async_copy(ETH.at[n % 4], ET.at[n % 2], ls.at[4, n % 2])

    et_copy(0).start()
    for c in weights:
        c.wait()
    dq = DOWN[3]
    for i in range(3):
        q_z[i].wait_recv()
        dq += DZR[i].astype(F32)
    dq_low = dq.astype(BF)

    first = FIRST[...]
    gain = gains[1:2].astype(F32)
    dn2 = jnp.zeros((R, D), F32)
    for g in range(4):
        dn2 += nt(dq_low[:, W * g : W * g + W], part(FA, g, 1))
    dv, dg2 = rms_back(dn2, first, gain)
    g1 = G2[...] + dv
    g1_low = g1.astype(BF)
    G1A[mine_rows, :] = g1_low
    for g in range(4):
        DQL[g] = dq_low[:, W * g : W * g + W]
    for g in range(4):
        DAS[g] = nn(g1_low, part(FA, g, 0)).astype(BF)
    das = [net.send(DAS.at[h ^ m], DA.at[h], head=h ^ m) for m in (2, 3, 1)]
    DA[h] = DAS[h]
    dql = [net.send(DQL.at[h ^ m], DQO.at[h], head=h ^ m) for m in (2, 3, 1)]
    DQO[h] = DQL[h]
    dql += [net.send(G1A.at[mine_rows], G1A.at[mine_rows], head=h ^ m) for m in (2, 3, 1)]

    def whole_grads(g, carry):
        acc = jnp.zeros((D, 2 * W), F32)
        for q in range(4):
            et_copy(4 * g + q).wait()

            @pl.when(4 * g + q < 15)
            def _():
                et_copy(4 * g + q + 1).start()

            acc += nn(ET[q % 2], DKV[q, g])
        gc, gx = g % 2, g // 2
        KSRC[gc, gx] = acc.astype(BF).reshape(2, 2, 2, D // 8, 2 * W)
        return carry

    lax.fori_loop(0, 4, whole_grads, 0)
    sk.push()
    for c in dql:
        c.wait_recv()
    rest = [tn(N2[...], DQO[...].reshape(T, W)), tn(G1A[...], AOO[...])]
    ASRC[...] = jnp.concatenate(rest, axis=1).astype(BF).reshape(ASRC.shape)
    sa.push()
    for c in das:
        c.wait_recv()

    da = DA[...].reshape(T, W)
    qs, ks, vs = QKV[:, 0:W], QKV[:, W : 2 * W], QKV[:, 2 * W : 3 * W]
    dq1 = jnp.zeros((T, W), F32)
    dk1 = jnp.zeros((T, W), F32)
    dv1 = jnp.zeros((T, W), F32)
    for a in range(3):
        mine = mine_of(a)
        dam = jnp.where(mine, da, zero)
        p = PS[a]
        dp = nt(dam, vs)
        ds = p * (dp - jnp.sum(p * dp, axis=-1, keepdims=True))
        DSF[a] = ds
        dsl = ds.astype(BF)
        dq1 += nn(dsl, jnp.where(mine, ks, zero))
        dk1 += tn(dsl, jnp.where(mine, qs, zero))
        dv1 += tn(p.astype(BF), dam)
    dqkv = jnp.concatenate([dq1, dk1, dv1], axis=1).astype(BF)
    wqkv = GQ[...].reshape(D, 3 * W)
    NS[...] = nt(dqkv, wqkv).astype(BF)
    nr = [net.send(NS.at[pl.ds(pl.multiple_of(R * (h ^ m), R), R)], NR.at[h], head=h ^ m) for m in (2, 3, 1)]
    NR[h] = NS[mine_rows, :]
    sk.pull()
    sa.pull()
    g0 = gains[0:1].astype(F32)
    n1 = rms_norm(hid[...].astype(F32), g0).astype(BF)
    LSRC[...] = tn(n1, dqkv).astype(BF).reshape(LSRC.shape)
    sl.push()

    step = DEN.shape[1]
    per = DENC.shape[1] // step

    def den_copy(n):
        rows = pl.ds(pl.multiple_of(lax.rem(n, per) * step, step), step)
        return pltpu.make_async_copy(DEN.at[lax.rem(n, 2)], DENC.at[n // per, rows], es.at[lax.rem(n, 2)])

    def denc(n, carry):
        rows = pl.ds(pl.multiple_of(lax.rem(n, per) * step, step), step)

        @pl.when(n >= 2)
        def _():
            den_copy(n - 2).wait()

        acc = nt(DKV[n // per, 0, rows, :], part(FK, 0))
        for g in range(1, 4):
            acc += nt(DKV[n // per, g, rows, :], part(FK, g))
        DEN[lax.rem(n, 2)] = acc
        den_copy(n).start()
        return carry

    def dencs(a, b):
        lax.fori_loop(a, b, denc, 0)

    dencs(0, 1)
    sf.pull()
    sc.pull()
    dencs(1, 2)
    for c in nr:
        c.wait_recv()
    dn1 = NR[0].astype(F32) + NR[1].astype(F32) + NR[2].astype(F32) + NR[3].astype(F32)
    dv, dg1 = rms_back(dn1, hid[mine_rows, :].astype(F32), g0)
    DHID[mine_rows, :] = g1 + dv
    dh = [net.send(DHID.at[mine_rows], DHID.at[mine_rows], head=h ^ m) for m in (2, 3, 1)]
    dh += [net.send(OUT.at[mine_rows], OUT.at[mine_rows], head=h ^ m) for m in (2, 3, 1)]

    sl.pull()
    sa.pull()
    sk.pull()

    bk = buckets[...]

    def table_step(i, carry):
        hit = bk == i
        for a in range(3):
            TBL[a, pl.ds(i, 1), :] = jnp.sum(jnp.where(hit, DSF[a], 0.0), axis=0, keepdims=True)
        return carry

    nb = TBL.shape[1]
    lax.fori_loop(0, nb, table_step, 0)
    tl = iota((nb, 128), 1)
    tab = jnp.zeros((nb, 128), F32)
    for a in range(3):
        tab = jnp.where(tl == a, jnp.sum(TBL[a], axis=1, keepdims=True), tab)
    tab = jnp.concatenate([tab, jnp.zeros((128 - nb, 128), F32)], axis=0).T[0:8]
    tab = jnp.concatenate([tab, jnp.zeros((8, D - 128), F32)], axis=1)
    dgs = jnp.concatenate([dg1, dg2, DG3[0:1], jnp.zeros((5, D), F32)], axis=0)
    SM[0] = jnp.concatenate([dgs, tab], axis=0)
    srow = iota((16, D), 0)

    def small(j, **dev):
        return net.send(SM.at[j], SMR.at[j], **dev)

    def small_end(j, c, shared):
        c.wait_recv()
        got = SMR[j]
        SM[j + 1] = SM[j] + (got if shared else jnp.where(srow < 8, got, 0.0))

    c = small(0, head=h ^ 1)
    sf.pull()
    sc.pull()
    small_end(0, c, False)
    c = small(1, head=h ^ 2)
    dencs(2, 4)
    sl.pull()
    sa.pull()
    sk.pull()
    small_end(1, c, False)
    c = small(2, dp=1 - d)
    dencs(4, 5)
    small_end(2, c, True)
    c = small(3, psg=z ^ 1)
    sl.pull()
    sk.pull()
    dencs(5, 6)
    small_end(3, c, True)
    c = small(4, psg=z ^ 2)
    sk.pull()
    dencs(6, 4 * per)
    small_end(4, c, True)
    for n in (4 * per - 2, 4 * per - 1):
        den_copy(n).wait()
    for s in (sf, sc, sk, sa, sl):
        s.done()
    for c in dh:
        c.wait_recv()
    net.finish()


def call_two(buckets, gains, hid, kept, big, rows, count):
    T, D = hid.shape
    R = T // 4
    W = 3 * HD
    k = kept
    tok = k["ET"].shape[2]
    F3 = k["GF"].shape[4]
    S = jax.ShapeDtypeStruct
    blk = D // 8
    outs = dict(
        DENC=((4, count, D), F32), DHID=((T, D), F32), OUT=((T, D), F32), SM=((6, 16, D), F32),
        OF=((4, rows, F3), F32), OC=((4, rows, W), F32), OK=((4, rows, 2 * W), F32), OA=((4, rows, 2 * W), F32),
        OL=((4, rows, 3 * W), F32),
    )

    def halving(n, w):
        return [VMEM((2,) * k + (blk, w), BF) for k in (n, *range(n - 1, -1, -1))] + [VMEM((blk, w), F32)]

    def like(n, *lead):
        return VMEM((*lead, *k[n].shape[1:]) if lead else k[n].shape, k[n].dtype)

    scratch = [
        VMEM((4, T, D + 2 * AUG), BF), like("KP", 2), like("VP", 2), like("KT", 2), like("QA", 2), like("ET", 2),
        like("FA"), like("FK"), like("GQ"), like("PS"),
        VMEM((4, T, W), BF), VMEM((4, T, W), BF), VMEM((4, T, AUG), BF), VMEM((4, T, AUG), BF),
        VMEM((3 * T, W + AUG), BF), VMEM((3 * T, W + AUG), BF), VMEM((tok, 3 * T), BF), VMEM((tok, 3 * T), BF),
        VMEM((4, T, W), BF), VMEM((4, 4, tok, 2 * W), BF),
        VMEM((4, 2, 2, R, D), BF), VMEM((4, 2, R, D), BF), VMEM((4, R, D), BF), VMEM((4, R, D), F32),
        VMEM((3, R, D), BF), VMEM((3, R, D), BF), VMEM((4, R, W), BF), VMEM((4, R, W), BF),
        VMEM((3, T, T), F32), VMEM((3, 32, T), F32), VMEM((T, D), BF), VMEM((4, R, D), BF), VMEM((2, count // 2, D), F32),
        *halving(3, F3), *halving(3, W), *halving(5, 2 * W), *halving(3, 2 * W), *halving(3, 3 * W),
        VMEM((5, 16, D), F32), VMEM((4, R, W), BF), VMEM((4, R, W), BF), VMEM((T, D), BF), VMEM((T, D), BF),
        pltpu.SemaphoreType.DMA((120,)), pltpu.SemaphoreType.DMA((120,)), pltpu.SemaphoreType.DMA((5, 2)), pltpu.SemaphoreType.DMA((6,)),
    ]
    vm = pl.BlockSpec(memory_space=pltpu.VMEM)
    anym = pl.BlockSpec(memory_space=pl.ANY)
    far = set(big) | {"QA"}
    ordered = dict(ET=0, FA=0, FK=0, GQ=0, QA=0, KP=0, VP=0, KT=0, PS=0)
    names = [*ordered, *[n for n in k if n not in ordered]]
    res = pl.pallas_call(
        kernel_two,
        out_shape=[S(*v) for v in outs.values()],
        in_specs=[vm] * 3 + [anym if n in far else vm for n in names],
        out_specs=[anym] + [vm] * (len(outs) - 1),
        scratch_shapes=scratch,
        name="backward",
        compiler_params=pltpu.CompilerParams(collective_id=2, has_side_effects=True, vmem_limit_bytes=63 << 20),
    )(buckets, gains, hid, *[k[n] for n in names])
    return dict(zip(outs, res))


def local_fast(
    hidden_in, encodings, passage_lengths, target_lengths, rel_buckets, gains, rel_table, *rest
):
    mats, cot = rest[:11], rest[11]
    span, passages, group, D = encodings.shape
    rows = mats[0].shape[0]
    W = 3 * HD
    F = mats[8].shape[1] // 4
    count = span * passages
    enc = jnp.transpose(encodings, (2, 1, 0, 3)).reshape(group, count, D)
    hid = hidden_in[0]
    kept, big = call_one(
        passage_lengths.T, target_lengths, rel_table.T, hid, enc, rel_buckets, gains, mats, cot[0]
    )
    r = call_two(rel_buckets, gains, hid, kept, big, rows, count)
    d_enc = jnp.transpose(r["DENC"].reshape(group, passages, span, D), (2, 1, 0, 3))

    last = call_three(r, W, F, rel_table.shape[0])
    out, dhid, d_gains, d_table, *grads = last
    return (out[None], dhid[None], d_enc, d_gains, d_table.T, *grads)


def kernel_three(W, F, OUT, DHID, SM, OF, OC, OK, OA, OL, out, dhid, gains, table, sq, sk, sv, so, cq, ck, cv, co, fg, fu, fd):
    out[...] = OUT[...]
    dhid[...] = DHID[...]
    gains[...] = SM[5, 0:3, :]
    table[...] = SM[5, 8:11, 0 : table.shape[1]]
    for dst, src, i, w in (
        (sq, OL, 0, W), (sk, OL, 1, W), (sv, OL, 2, W), (so, OA, 1, W), (cq, OA, 0, W),
        (ck, OK, 0, W), (cv, OK, 1, W), (co, OC, 0, W), (fg, OF, 0, F), (fu, OF, 1, F), (fd, OF, 2, F),
    ):
        dst[...] = jnp.concatenate([src[j, :, w * i : w * i + w] for j in range(4)], axis=1)


def call_three(r, W, F, nb):
    S = jax.ShapeDtypeStruct
    DENC, DHID, OUT, SM, OF, OC, OK, OA, OL = r.values()
    T, D = OUT.shape
    rows = OF.shape[1]
    outs = [(T, D), (T, D), (3, D), (3, nb)] + [(rows, 4 * W)] * 8 + [(rows, 4 * F)] * 3
    vm = pl.BlockSpec(memory_space=pltpu.VMEM)
    res = pl.pallas_call(
        functools.partial(kernel_three, W, F),
        out_shape=[S(v, F32) for v in outs],
        in_specs=[vm] * 8,
        out_specs=[vm] * len(outs),
        name="columns",
        compiler_params=pltpu.CompilerParams(vmem_limit_bytes=62 << 20),
    )(OUT, DHID, SM, OF, OC, OK, OA, OL)
    return res


def merged(part, axis, combine):
    gathered = jax.tree.map(lambda a: lax.all_gather(a, axis), part)

    def take(source):
        return jax.tree.map(lambda a: lax.dynamic_index_in_dim(a, source, 0, False), gathered)

    return lax.fori_loop(
        1, lax.axis_size(axis), lambda source, state: combine(state, take(source)), take(0)
    )


def rms_plain(values, gain):
    return values * lax.rsqrt(jnp.mean(values * values, axis=-1, keepdims=True) + EPSILON) * gain


def gated(gate_in, up_in):
    return jax.nn.gelu(gate_in, approximate=True) * up_in


def over_heads(partial_value):
    return lax.psum(partial_value, "head")


def own_columns(matrix, index, width):
    return lax.dynamic_slice_in_dim(matrix, index * width, width, 1)


def left_mul(left, matrix):
    return jnp.einsum("qtd,dc->qtc", left, matrix, preferred_element_type=jnp.float32)


def right_mul(left, matrix):
    return jnp.einsum("qtc,dc->qtd", left, matrix, preferred_element_type=jnp.float32)


def row_outer(left, right):
    return jnp.einsum("qtd,qtc->dc", left, right, preferred_element_type=jnp.float32)


def local_plain(
    hidden_in,
    encodings,
    passage_lengths,
    target_lengths,
    rel_buckets,
    gains,
    rel_table,
    self_q,
    self_k,
    self_v,
    self_o,
    cross_q,
    cross_k,
    cross_v,
    cross_o,
    ff_gate,
    ff_up,
    ff_down,
    cotangent,
):
    gathered = (
        lax.all_gather(self_q, ("dp", "psg", "head"), axis=0, tiled=True),
        lax.all_gather(self_k, ("dp", "psg", "head"), axis=0, tiled=True),
        lax.all_gather(self_v, ("dp", "psg", "head"), axis=0, tiled=True),
        lax.all_gather(self_o, ("dp", "psg", "head"), axis=0, tiled=True),
        lax.all_gather(cross_q, ("dp", "psg", "head"), axis=0, tiled=True),
        lax.all_gather(cross_k, ("dp", "psg", "head"), axis=0, tiled=True),
        lax.all_gather(cross_v, ("dp", "psg", "head"), axis=0, tiled=True),
        lax.all_gather(cross_o, ("dp", "psg", "head"), axis=0, tiled=True),
        lax.all_gather(ff_gate, ("dp", "psg", "head"), axis=0, tiled=True),
        lax.all_gather(ff_up, ("dp", "psg", "head"), axis=0, tiled=True),
        lax.all_gather(ff_down, ("dp", "psg", "head"), axis=0, tiled=True),
    )
    (
        self_query,
        self_key,
        self_value,
        self_out,
        cross_query,
        cross_key,
        cross_value,
        cross_out,
        gate_full,
        up_full,
        down_full,
    ) = gathered
    head_index = lax.axis_index("head")
    heads_local = rel_table.shape[1]
    width = heads_local * HD
    total_width = self_query.shape[1]
    ff_total = gate_full.shape[1]
    ff_local = ff_total // lax.axis_size("head")
    query_rows = hidden_in.shape[0]
    target_span = hidden_in.shape[1]
    hidden = hidden_in.astype(jnp.float32)
    gain_all = gains.astype(jnp.float32)
    qkv_weight = jnp.concatenate(
        [
            own_columns(self_query, head_index, width),
            own_columns(self_key, head_index, width),
            own_columns(self_value, head_index, width),
        ],
        axis=1,
    )
    normed_one = rms_plain(hidden, gain_all[0]).astype(jnp.bfloat16)
    qkv_self = left_mul(normed_one, qkv_weight).astype(jnp.bfloat16)
    queries_self = qkv_self[..., :width].reshape(query_rows, target_span, heads_local, HD)
    keys_self = qkv_self[..., width : 2 * width].reshape(query_rows, target_span, heads_local, HD)
    values_self = qkv_self[..., 2 * width :].reshape(query_rows, target_span, heads_local, HD)
    positions = jnp.arange(target_span)
    causal = (positions[None, None, :] <= positions[None, :, None]) & (
        positions[None, None, :] < target_lengths[:, None, None]
    )
    buckets_hot = (rel_buckets[:, :, None] == jnp.arange(rel_table.shape[0])[None, None, :]).astype(
        jnp.float32
    )
    bias = jnp.einsum(
        "ijb,bh->hij", buckets_hot, rel_table.astype(jnp.float32), precision=lax.Precision.HIGHEST
    )
    scores_self = jnp.einsum(
        "qihd,qjhd->qhij", queries_self, keys_self, preferred_element_type=jnp.float32
    )
    scores_self = jnp.where(causal[:, None], scores_self + bias[None], NEGATIVE)
    probs_self = jax.nn.softmax(scores_self, axis=-1)
    probs_self_low = probs_self.astype(jnp.bfloat16)
    attn_one = jnp.einsum(
        "qhij,qjhd->qihd", probs_self_low, values_self, preferred_element_type=jnp.float32
    )
    attn_one = attn_one.reshape(query_rows, target_span, width).astype(jnp.bfloat16)
    self_out_own = own_columns(self_out, head_index, width)
    first = hidden + over_heads(right_mul(attn_one, self_out_own))
    normed_two = rms_plain(first, gain_all[1]).astype(jnp.bfloat16)
    cross_query_own = own_columns(cross_query, head_index, width)
    query_cross = left_mul(normed_two, cross_query_own).astype(jnp.bfloat16)
    query_group = lax.all_gather(query_cross, "psg", axis=0, tiled=True)
    group_count = query_group.shape[0]
    head_parts = lax.axis_size("head")
    kv_split = jnp.concatenate(
        [
            cross_key.reshape(cross_key.shape[0], head_parts, width),
            cross_value.reshape(cross_value.shape[0], head_parts, width),
        ],
        axis=2,
    )
    local_kv = jnp.einsum(
        "tpqd,dgc->qptgc", encodings, kv_split, preferred_element_type=jnp.float32
    ).astype(jnp.bfloat16)
    moved_kv = lax.all_to_all(local_kv, "head", split_axis=3, concat_axis=2, tiled=True)
    key_value = moved_kv.reshape(moved_kv.shape[0], moved_kv.shape[1], moved_kv.shape[2], 2 * width)
    passages_local = key_value.shape[1]
    passage_span = key_value.shape[2]
    key_count = passages_local * passage_span
    kv_flat = key_value.reshape(group_count, key_count, 2 * width)
    span = jnp.arange(passage_span)
    key_valid = (span[None, None, :] < jnp.transpose(passage_lengths)[:, :, None]).reshape(
        group_count, key_count
    )

    def masked_scores(query_block, kv_block, valid_block):
        query_heads = query_block.reshape(target_span, heads_local, HD)
        keys_part = kv_block[:, :width].reshape(key_count, heads_local, HD)
        raw = jnp.einsum("ihd,jhd->hij", query_heads, keys_part, preferred_element_type=jnp.float32)
        return jnp.where(valid_block[None, None, :], raw, NEGATIVE)

    def stats_one(item):
        masked = masked_scores(item[0], item[1], item[2])
        largest = jnp.max(masked, axis=-1)
        total = jnp.sum(jnp.exp(masked - largest[..., None]), axis=-1)
        return (largest, total)

    tops, totals = lax.map(stats_one, (query_group, kv_flat, key_valid))

    def combine(pair_one, pair_two):
        larger = jnp.maximum(pair_one[0], pair_two[0])
        return (
            larger,
            pair_one[1] * jnp.exp(pair_one[0] - larger)
            + pair_two[1] * jnp.exp(pair_two[0] - larger),
        )

    tops, totals = merged((tops, totals), "psg", combine)
    log_total = tops + jnp.log(totals)

    def values_one(item):
        masked = masked_scores(item[0], item[1], item[2])
        probs_low = jnp.exp(masked - item[3][..., None]).astype(jnp.bfloat16)
        values_part = item[1][:, width:].reshape(key_count, heads_local, HD)
        weighted = jnp.einsum(
            "hij,jhd->ihd", probs_low, values_part, preferred_element_type=jnp.float32
        )
        return weighted.reshape(target_span, width)

    partial_out = lax.map(values_one, (query_group, kv_flat, key_valid, log_total))
    attn_two = lax.psum_scatter(partial_out, "psg", scatter_dimension=0, tiled=True).astype(
        jnp.bfloat16
    )
    cross_out_own = own_columns(cross_out, head_index, width)
    second = first + over_heads(right_mul(attn_two, cross_out_own))
    normed_three = rms_plain(second, gain_all[2]).astype(jnp.bfloat16)
    ff_weight = jnp.concatenate(
        [own_columns(gate_full, head_index, ff_local), own_columns(up_full, head_index, ff_local)],
        axis=1,
    )
    gate_up = left_mul(normed_three, ff_weight)
    gate_part = gate_up[..., :ff_local]
    up_part = gate_up[..., ff_local:]
    activated = gated(gate_part, up_part).astype(jnp.bfloat16)
    down_own = own_columns(down_full, head_index, ff_local)
    output = second + over_heads(right_mul(activated, down_own))
    row_valid = (positions[None, :] < target_lengths[:, None])[:, :, None]
    out_hidden = jnp.where(row_valid, output, 0.0)
    grad_out = jnp.where(row_valid, cotangent.astype(jnp.float32), 0.0)
    grad_out_low = grad_out.astype(jnp.bfloat16)
    grad_down = row_outer(grad_out_low, activated)
    grad_act = left_mul(grad_out_low, down_own)
    gate_value, pull_gate = jax.vjp(gated, gate_part, up_part)
    grad_gate, grad_up = pull_gate(grad_act)
    grad_gate_up = jnp.concatenate([grad_gate, grad_up], axis=-1).astype(jnp.bfloat16)
    grad_ff_weight = row_outer(normed_three, grad_gate_up)
    grad_normed_three = over_heads(right_mul(grad_gate_up, ff_weight))
    norm_value, pull_three = jax.vjp(rms_plain, second, gain_all[2])
    grad_second_norm, grad_gain_three = pull_three(grad_normed_three)
    grad_two = grad_out + grad_second_norm
    grad_two_low = grad_two.astype(jnp.bfloat16)
    grad_cross_out = row_outer(grad_two_low, attn_two)
    grad_attn_two = left_mul(grad_two_low, cross_out_own).astype(jnp.bfloat16)
    grad_attn_group = lax.all_gather(grad_attn_two, "psg", axis=0, tiled=True)

    def prob_pieces(item):
        masked = masked_scores(item[0], item[1], item[2])
        probs = jnp.exp(masked - item[3][..., None])
        values_part = item[1][:, width:].reshape(key_count, heads_local, HD)
        grad_rows = item[4].reshape(target_span, heads_local, HD)
        grad_probs = jnp.einsum(
            "ihd,jhd->hij", grad_rows, values_part, preferred_element_type=jnp.float32
        )
        return (probs, grad_probs)

    def delta_one(item):
        probs, grad_probs = prob_pieces(item)
        return jnp.sum(probs * grad_probs, axis=-1)

    delta_part = lax.map(delta_one, (query_group, kv_flat, key_valid, log_total, grad_attn_group))
    delta = lax.psum(delta_part, "psg")

    def grads_one(item):
        probs, grad_probs = prob_pieces(item[:5])
        grad_scores = (probs * (grad_probs - item[5][..., None])).astype(jnp.bfloat16)
        probs_low = probs.astype(jnp.bfloat16)
        query_heads = item[0].reshape(target_span, heads_local, HD)
        keys_part = item[1][:, :width].reshape(key_count, heads_local, HD)
        grad_rows = item[4].reshape(target_span, heads_local, HD)
        grad_query = jnp.einsum(
            "hij,jhd->ihd", grad_scores, keys_part, preferred_element_type=jnp.float32
        )
        grad_keys = jnp.einsum(
            "hij,ihd->jhd", grad_scores, query_heads, preferred_element_type=jnp.float32
        )
        grad_values = jnp.einsum(
            "hij,ihd->jhd", probs_low, grad_rows, preferred_element_type=jnp.float32
        )
        grad_kv = jnp.concatenate(
            [grad_keys.reshape(key_count, width), grad_values.reshape(key_count, width)], axis=-1
        ).astype(jnp.bfloat16)
        return (grad_query.reshape(target_span, width), grad_kv)

    grad_query_group, grad_kv_flat = lax.map(
        grads_one, (query_group, kv_flat, key_valid, log_total, grad_attn_group, delta)
    )
    grad_query_cross = lax.psum_scatter(
        grad_query_group, "psg", scatter_dimension=0, tiled=True
    ).astype(jnp.bfloat16)
    grad_cross_query = row_outer(normed_two, grad_query_cross)
    grad_normed_two = over_heads(right_mul(grad_query_cross, cross_query_own))
    norm_value_two, pull_two = jax.vjp(rms_plain, first, gain_all[1])
    grad_first_norm, grad_gain_two = pull_two(grad_normed_two)
    grad_one = grad_two + grad_first_norm
    grad_kv = grad_kv_flat.reshape(group_count, passages_local, passage_span, 2 * width)
    grad_back = lax.all_to_all(
        grad_kv.reshape(group_count, passages_local, passage_span, 1, 2 * width),
        "head",
        split_axis=2,
        concat_axis=3,
        tiled=True,
    )
    d_encodings = jnp.einsum(
        "qptgc,dgc->tpqd", grad_back, kv_split, preferred_element_type=jnp.float32
    )
    grad_split = jnp.einsum(
        "tpqd,qptgc->dgc", encodings, grad_back, preferred_element_type=jnp.float32
    )
    grad_cross_key = grad_split[:, :, :width].reshape(grad_split.shape[0], total_width)
    grad_cross_value = grad_split[:, :, width:].reshape(grad_split.shape[0], total_width)
    grad_one_low = grad_one.astype(jnp.bfloat16)
    grad_self_out = row_outer(grad_one_low, attn_one)
    grad_attn_one = left_mul(grad_one_low, self_out_own).astype(jnp.bfloat16)
    grad_attn_one = grad_attn_one.reshape(query_rows, target_span, heads_local, HD)
    grad_probs_self = jnp.einsum(
        "qihd,qjhd->qhij", grad_attn_one, values_self, preferred_element_type=jnp.float32
    )
    grad_scores_self = probs_self * (
        grad_probs_self - jnp.sum(probs_self * grad_probs_self, axis=-1, keepdims=True)
    )
    grad_table = jnp.einsum(
        "ijb,hij->bh",
        buckets_hot,
        jnp.sum(grad_scores_self, axis=0),
        precision=lax.Precision.HIGHEST,
    )
    grad_scores_low = grad_scores_self.astype(jnp.bfloat16)
    grad_query_self = jnp.einsum(
        "qhij,qjhd->qihd", grad_scores_low, keys_self, preferred_element_type=jnp.float32
    )
    grad_key_self = jnp.einsum(
        "qhij,qihd->qjhd", grad_scores_low, queries_self, preferred_element_type=jnp.float32
    )
    grad_value_self = jnp.einsum(
        "qhij,qihd->qjhd", probs_self_low, grad_attn_one, preferred_element_type=jnp.float32
    )
    grad_qkv = jnp.concatenate(
        [
            grad_query_self.reshape(query_rows, target_span, width),
            grad_key_self.reshape(query_rows, target_span, width),
            grad_value_self.reshape(query_rows, target_span, width),
        ],
        axis=-1,
    ).astype(jnp.bfloat16)
    grad_qkv_weight = row_outer(normed_one, grad_qkv)
    grad_normed_one = over_heads(right_mul(grad_qkv, qkv_weight))
    norm_value_one, pull_one = jax.vjp(rms_plain, hidden, gain_all[0])
    grad_hidden_norm, grad_gain_one = pull_one(grad_normed_one)
    d_hidden = grad_one + grad_hidden_norm
    grad_gains = jnp.stack([grad_gain_one, grad_gain_two, grad_gain_three])
    d_gains, d_rel_table = lax.psum((grad_gains, grad_table), ("dp", "psg"))
    own_grads = [
        grad_qkv_weight[:, :width],
        grad_qkv_weight[:, width : 2 * width],
        grad_qkv_weight[:, 2 * width :],
        grad_self_out,
        grad_cross_query,
        grad_cross_out,
        grad_ff_weight[:, :ff_local],
        grad_ff_weight[:, ff_local:],
        grad_down,
    ]
    row_sums = lax.psum_scatter(tuple(own_grads), ("dp", "psg"), scatter_dimension=0, tiled=True)
    owned = (
        lax.all_to_all(row_sums[0], "head", split_axis=0, concat_axis=1, tiled=True),
        lax.all_to_all(row_sums[1], "head", split_axis=0, concat_axis=1, tiled=True),
        lax.all_to_all(row_sums[2], "head", split_axis=0, concat_axis=1, tiled=True),
        lax.all_to_all(row_sums[3], "head", split_axis=0, concat_axis=1, tiled=True),
        lax.all_to_all(row_sums[4], "head", split_axis=0, concat_axis=1, tiled=True),
        lax.all_to_all(row_sums[5], "head", split_axis=0, concat_axis=1, tiled=True),
        lax.all_to_all(row_sums[6], "head", split_axis=0, concat_axis=1, tiled=True),
        lax.all_to_all(row_sums[7], "head", split_axis=0, concat_axis=1, tiled=True),
        lax.all_to_all(row_sums[8], "head", split_axis=0, concat_axis=1, tiled=True),
    )
    key_done, value_done = (
        lax.psum_scatter(grad_cross_key, ("dp", "psg", "head"), scatter_dimension=0, tiled=True),
        lax.psum_scatter(grad_cross_value, ("dp", "psg", "head"), scatter_dimension=0, tiled=True),
    )
    return (
        out_hidden,
        d_hidden,
        d_encodings,
        d_gains,
        d_rel_table,
        owned[0],
        owned[1],
        owned[2],
        owned[3],
        owned[4],
        key_done,
        value_done,
        owned[5],
        owned[6],
        owned[7],
        owned[8],
    )


PLACED = (
    P(("dp", "psg"), None, None),
    P("head", "psg", "dp", None),
    P("psg", "dp"),
    P(("dp", "psg")),
    P(),
    P(),
    P(None, "head"),
    P(("dp", "psg", "head"), None),
    P(("dp", "psg", "head"), None),
    P(("dp", "psg", "head"), None),
    P(("dp", "psg", "head"), None),
    P(("dp", "psg", "head"), None),
    P(("dp", "psg", "head"), None),
    P(("dp", "psg", "head"), None),
    P(("dp", "psg", "head"), None),
    P(("dp", "psg", "head"), None),
    P(("dp", "psg", "head"), None),
    P(("dp", "psg", "head"), None),
    P(("dp", "psg"), None, None),
)

OUTS = (
    P(("dp", "psg"), None, None),
    P(("dp", "psg"), None, None),
    P("head", "psg", "dp", None),
    P(),
    P(None, "head"),
    P(("dp", "psg", "head"), None),
    P(("dp", "psg", "head"), None),
    P(("dp", "psg", "head"), None),
    P(("dp", "psg", "head"), None),
    P(("dp", "psg", "head"), None),
    P(("dp", "psg", "head"), None),
    P(("dp", "psg", "head"), None),
    P(("dp", "psg", "head"), None),
    P(("dp", "psg", "head"), None),
    P(("dp", "psg", "head"), None),
    P(("dp", "psg", "head"), None),
)


def solution(mesh):
    def local(*args):
        rows, span, heads = args[7].shape[0], args[1].shape[0], args[6].shape[1]
        fits = (mesh.shape["dp"], mesh.shape["psg"], mesh.shape["head"], heads) == (2, 4, 4, 3)
        fits = fits and (4 * rows) % 16 == 0 and rows % 8 == 0
        return (local_fast if fits else local_plain)(*args)

    placed = PLACED
    return jax.shard_map(local, mesh=mesh, in_specs=placed, out_specs=OUTS, check_vma=False)
```

```python
import functools

import jax
import jax.numpy as jnp
from jax import lax
from jax.experimental import pallas as pl
from jax.experimental.pallas import tpu as pltpu
from jax.sharding import PartitionSpec as P

HD = 64
EPSILON = 1e-06
NEGATIVE = -1e30
AUG = 64
BF = jnp.bfloat16
F32 = jnp.float32
MESH = pl.DeviceIdType.MESH
VMEM = pltpu.VMEM


def nn(a, b):
    return lax.dot_general(a, b, (((1,), (0,)), ((), ())), preferred_element_type=F32)


def nt(a, b):
    return lax.dot_general(a, b, (((1,), (1,)), ((), ())), preferred_element_type=F32)


def tn(a, b):
    return lax.dot_general(a, b, (((0,), (0,)), ((), ())), preferred_element_type=F32)


def rms_scale(v):
    return lax.rsqrt(jnp.mean(v * v, axis=-1, keepdims=True) + EPSILON)


def rms_norm(v, gain):
    return v * rms_scale(v) * gain


def rms_back(dn, v, gain):
    r = rms_scale(v)
    gd = gain * dn
    dv = r * gd - v * (r * r * r * jnp.mean(gd * v, axis=-1, keepdims=True))
    dg = jnp.sum(dn * v * r, axis=0, keepdims=True)
    return dv, dg


def iota(shape, axis):
    return lax.broadcasted_iota(jnp.int32, shape, axis)


class Net:
    def __init__(self, send_sems, recv_sems):
        self.send_sems, self.recv_sems, self.count, self.sent = send_sems, recv_sems, 0, []

    def send(self, src, dst, **device):
        at = self.count
        self.count += 1
        copy = pltpu.make_async_remote_copy(
            src, dst, self.send_sems.at[at], self.recv_sems.at[at],
            device_id=device, device_id_type=MESH,
        )
        copy.start()
        self.sent.append(copy)
        return copy

    def finish(self):
        for copy in self.sent:
            copy.wait_send()


def places():
    d, z, h = lax.axis_index("dp"), lax.axis_index("psg"), lax.axis_index("head")
    return dict(
        c=(h % 2, dict(head=h ^ 1)), x=(h // 2, dict(head=h ^ 2)), y=(d, dict(dp=1 - d)),
        a=(z // 2, dict(psg=z ^ 3)), b=(z % 2, dict(psg=z ^ 1)),
    )


class Doubling:
    def __init__(self, net, ref, names, order, late=()):
        self.net, self.ref, self.names, self.order, self.at = net, ref, names, order, places()
        self.late = [order.index(n) + 1 for n in late]
        self.sent = {s: [] if s in self.late else [self.go(0, s)] for s in range(1, len(order) + 1)}

    def region(self, j):
        idx = []
        for n in self.names:
            p, mine = self.order.index(n) + 1, self.at[n][0]
            idx.append(mine if p > j else (1 - mine if p == j else slice(None)))
        return self.ref.at[tuple(idx)]

    def go(self, j, s):
        block = self.region(j)
        return self.net.send(block, block, **self.at[self.order[s - 1]][1])

    def open(self, name, have):
        s = self.order.index(name) + 1
        self.late.remove(s)
        self.sent[s] = [self.go(i, s) for i in range(have + 1)]

    def step(self, name):
        j = self.order.index(name) + 1
        for c in self.sent[j]:
            c.wait_recv()
        for s in range(j + 1, len(self.order) + 1):
            if s not in self.late:
                self.sent[s].append(self.go(j, s))
            elif s == j + 1:
                self.sent[s] = [self.go(i, s) for i in range(s)]


class Halving:
    def __init__(self, net, src, names, order, bufs, total, shard):
        self.net, self.src, self.names, self.order, self.bufs = net, src, names, order, bufs
        self.total, self.shard, self.at, self.stage = total, shard, places(), 0

    def index(self, stage, last, free):
        idx, free = [], list(free)
        for n in self.names:
            p, mine = self.order.index(n), self.at[n][0]
            idx.append(mine if p < stage else (last(mine) if p == stage else free.pop(0)))
        return tuple(idx)

    def push(self):
        n = len(self.order) - self.stage - 1
        far = self.src.at[self.index(self.stage, lambda m: 1 - m, [slice(None)] * n)]
        self.copy = self.net.send(far, self.bufs[self.stage], **self.at[self.order[self.stage]][1])

    def pull(self):
        self.copy.wait_recv()
        n = len(self.order) - self.stage - 1
        buf = self.bufs[self.stage]
        if n == 0:
            idx = self.index(self.stage, lambda m: m, [])
            self.total[...] = self.src[idx].astype(F32) + buf[...].astype(F32)
        else:
            def add(i, carry):
                bits = [(i // 2**k) % 2 for k in range(n)]
                idx = self.index(self.stage, lambda m: m, bits)
                self.src[idx] = (self.src[idx].astype(F32) + buf[tuple(bits)].astype(F32)).astype(BF)
                return carry

            lax.fori_loop(0, 2**n, add, 0)
        self.stage += 1
        if n:
            self.push()
        else:
            self.trade()

    def trade(self):
        n, h = self.shard.shape[1], lax.axis_index("head")

        def rows(hh):
            return pl.ds(pl.multiple_of(n * hh, n), n)

        self.last = [self.net.send(self.total.at[rows(h ^ m)], self.shard.at[h], head=h ^ m) for m in (2, 3, 1)]
        self.shard[h] = self.total[rows(h), :]

    def done(self):
        for c in self.last:
            c.wait_recv()


def enter():
    barrier = pltpu.get_barrier_semaphore()
    d, z, h = lax.axis_index("dp"), lax.axis_index("psg"), lax.axis_index("head")
    peers = [dict(head=h ^ m) for m in (1, 2, 3)]
    peers += [dict(psg=lax.rem(z + m, 4)) for m in (1, 2, 3)]
    peers += [dict(dp=1 - d)]
    for peer in peers:
        pl.semaphore_signal(barrier, inc=1, device_id=peer, device_id_type=MESH)
    pl.semaphore_wait(barrier, len(peers))
    return d, z, h


ORDER = (1, 3, 2, 0)


class Gather:
    def __init__(self, net, buf, z, h, rows):
        self.net, self.buf, self.z, self.h, self.rows = net, buf, z, h, rows
        mine = self.at(z, h)
        self.ring = {m: net.send(mine, mine, psg=lax.rem(z + m, 4)) for m in (1, 3, 2)}
        self.hops = {0: self.on(z)}
        self.last = {}

    def at(self, zz, hh):
        return self.buf.at[zz, pl.ds(pl.multiple_of(self.rows * hh, self.rows), self.rows)]

    def on(self, zz):
        block = self.at(zz, self.h)
        return [self.net.send(block, block, head=self.h ^ 2), self.net.send(block, block, head=self.h ^ 1)]

    def source(self, m):
        return lax.rem(self.z - m + 4, 4)

    def relay(self):
        for m in (1, 3, 2):
            self.ring[m].wait_recv()
            self.hops[m] = self.on(self.source(m))
        for m in ORDER:
            self.hops[m][0].wait_recv()
            block = self.at(self.source(m), self.h ^ 2)
            self.last[m] = self.net.send(block, block, head=self.h ^ 1)

    def ready(self, m):
        self.hops[m][1].wait_recv()
        self.last[m].wait_recv()


def kernel_one(
    plen, tlen,
    table, hid, ench, buckets, gains, sq, sk, sv, so, cq, ck, cv, co, fg, fu, fd, cot,
    FAH, FKH, GQH, KPH, VPH, KTH, ETH, PSH, QA, QKV, AOS, FIRST, G2, DO, GFH, DG3, OUT, N2, ATO,
    PQ, PA, PK, PC, PG, AQ, AA, AK, AC, AG,
    FA, FK, FC, GQ, GG, KP, VP, KT, VT, ET, PS, AO, GF,
    enc, QU, BIAS, OS, ST, OC, SC, OXS, SXS, OX, SX, OZS, SZS, OZ, SZ,
    OWN, SOWN, ATS, AT, N3, R3S, R3, R1S, R1, QM,
    ss, rs, ls,
):
    d, z, h = enter()
    net = Net(ss, rs)
    T, D = hid.shape
    R = T // 4
    W = 3 * HD
    hc, hx = h % 2, h // 2
    e = 1 - d
    zp, zm, zo = lax.rem(z + 1, 4), lax.rem(z + 3, 4), lax.rem(z + 2, 4)
    kept = []

    def keep_out(src, dst):
        c = pltpu.make_async_copy(src, dst, ls.at[len(kept)])
        c.start()
        kept.append(c)

    count = ench.shape[1]
    e_load = pltpu.make_async_copy(ench, enc.at[:, pl.ds(0, count)], ls.at[11])
    e_load.start()

    F = fg.shape[1] // 4

    def pack(dst, names):
        for g in range(4):
            s = slice(W * g, W * g + W)
            parts = [r[...].astype(F32)[:, s] for r in names]
            dst[g] = (jnp.concatenate(parts, axis=1) if len(parts) > 1 else parts[0]).astype(BF)

    def trade(src, dst):
        cs = [net.send(src.at[h ^ m], dst.at[h], head=h ^ m) for m in (2, 3, 1)]
        dst[h] = src[h]
        return cs

    pack(PQ, (sq, sk, sv))
    tq = trade(PQ, AQ)
    pack(PA, (so, cq))
    ta = trade(PA, AA)
    pack(PK, (ck, cv))
    tk = trade(PK, AK)
    pack(PC, (co,))
    for g in range(4):
        for i, ref in enumerate((fg, fu, fd)):
            PG[g, :, F * i : F * i + F] = ref[:, F * g : F * g + F]
    tc = trade(PC, AC)
    tg = trade(PG, AG)

    def assemble(cs, src, dst):
        for c in cs:
            c.wait_recv()
        dst[...] = jnp.concatenate([src[j].astype(F32) for j in range(4)], axis=0).astype(BF)

    full, own = tuple("cxyab"), tuple("yab")
    za, zb = z // 2, z % 2
    assemble(tq, AQ, GQ.at[d, za, zb])
    wq = Doubling(net, GQ, own, tuple("bay"))
    assemble(ta, AA, FA.at[hc, hx, d, za, zb])
    wa = Doubling(net, FA, full, tuple("baxyc"))
    assemble(tk, AK, FK.at[hc, hx, d, za, zb])
    wk = Doubling(net, FK, full, tuple("bayxc"))
    g0 = gains[0:1].astype(F32)
    hidden = hid[...].astype(F32)
    n1 = rms_norm(hidden, g0).astype(BF)

    def flip(q, carry):
        ET[q] = enc[q].astype(F32).T.astype(BF)
        return carry

    assemble(tc, AC, FC.at[hc, hx, d, za, zb])
    assemble(tg, AG, GG.at[d, za, zb])
    for w in (wq, wk, wa):
        w.step("b")
    e_load.wait()
    enc[:, count:, :] = jnp.zeros((enc.shape[0], enc.shape[1] - count, D), BF)
    lax.fori_loop(0, 2, flip, 0)
    for w in (wq, wa, wk):
        w.step("a")
    wc = Doubling(net, FC, full, tuple("bayxc"), ("x", "c"))
    wg = Doubling(net, GG, own, tuple("bay"), ("y",))
    lax.fori_loop(2, 4, flip, 0)
    bk = buckets[...]
    tab = table[...].astype(F32)
    for a in range(3):
        acc = jnp.zeros((T, T), F32)
        for i in range(tab.shape[1]):
            acc = jnp.where(bk == i, tab[a : a + 1, i : i + 1], acc)
        BIAS[a] = acc
    wa.step("x")
    wk.step("y")
    wg.open("y", 0)
    wq.step("y")

    wqkv = GQ[...].reshape(D, 3 * W)
    QKV[...] = nn(n1, wqkv).astype(BF)
    keep_out(GQ, GQH)
    wk.step("x")
    wc.step("b")
    wg.step("b")
    qs, ks, vs = QKV[:, 0:W], QKV[:, W : 2 * W], QKV[:, 2 * W : 3 * W]
    lane = iota((T, W), 1)
    row, col = iota((T, T), 0), iota((T, T), 1)
    keep = (col <= row) & (col < tlen[0])
    acc = jnp.zeros((T, W), F32)
    zero = jnp.zeros((T, W), BF)
    for a in range(3):
        mine = (lane >= HD * a) & (lane < HD * a + HD)
        s = nt(jnp.where(mine, qs, zero), ks) + BIAS[a]
        s = jnp.where(keep, s, NEGATIVE)
        ex = jnp.exp(s - jnp.max(s, axis=-1, keepdims=True))
        p = ex / jnp.sum(ex, axis=-1, keepdims=True)
        PS[a] = p
        acc += nn(p.astype(BF), jnp.where(mine, vs, zero))
    AOS[...] = acc.astype(BF)
    ao = [net.send(AOS.at[pl.ds(pl.multiple_of(R * (h ^ m), R), R)], AO.at[h], head=h ^ m) for m in (2, 3, 1)]
    AO[h] = AOS[pl.ds(pl.multiple_of(R * h, R), R), :]
    keep_out(PS, PSH)
    wa.step("y")
    wa.step("c")
    for c in ao:
        c.wait_recv()

    def part(ref, g, i=None):
        blk = ref[g % 2, g // 2] if i is None else ref[g % 2, g // 2, :, :, :, :, W * i : W * i + W]
        return blk.reshape(D, blk.shape[-1])

    mine_rows = pl.ds(pl.multiple_of(R * h, R), R)
    first = hid[mine_rows, :].astype(F32)
    for g in range(4):
        first += nt(AO[g], part(FA, g, 0))
    FIRST[...] = first
    n2 = rms_norm(first, gains[1:2].astype(F32)).astype(BF)
    N2[mine_rows, :] = n2
    QA[z, mine_rows, :] = jnp.concatenate([nn(n2, part(FA, g, 1)) for g in range(4)], axis=1).astype(BF)
    spreadq = Gather(net, QA, z, h, R)
    n2c = [net.send(N2.at[mine_rows], N2.at[mine_rows], head=h ^ m) for m in (2, 3, 1)]
    keep_out(FA, FAH)
    wk.step("c")
    keep_out(FK, FKH)

    tok = enc.shape[1]
    krow, klane = iota((tok, AUG), 0), iota((tok, AUG), 1)
    per = 96
    npass = plen.shape[1]
    vaug = jnp.where(klane < 9, -1.0, 0.0).astype(F32)

    def project(q, carry):
        dead = krow >= per * npass
        for p in range(npass):
            inside = (krow >= per * p) & (krow < per * p + per)
            dead = dead | (inside & (krow - per * p + per * h >= plen[q, p]))
        kaug = jnp.where(klane == 9, jnp.where(dead, NEGATIVE, 0.0), vaug)

        def group(g, c2):
            kv = nn(enc[q], FK[g % 2, g // 2].reshape(D, 2 * W))
            k, v = kv[:, :W], kv[:, W:]
            KP[q, g] = jnp.concatenate([k, kaug], axis=1).astype(BF)
            VP[q, g] = jnp.concatenate([v, vaug], axis=1).astype(BF)
            KT[q, g] = k.T.astype(BF)
            VT[q, g] = v.T.astype(BF)
            return c2

        lax.fori_loop(0, 4, group, 0)
        return carry

    lax.fori_loop(0, 2, project, 0)
    spreadq.relay()
    wc.step("a")
    wg.step("a")
    lax.fori_loop(2, 4, project, 0)
    for src, dst in ((KP, KPH), (VP, VPH), (KT, KTH), (ET, ETH)):
        keep_out(src, dst)

    qaug = jnp.where(iota((T, AUG), 1) == 9, 1.0, 0.0).astype(BF)

    def weights(m1, l1, m2, l2):
        top = jnp.maximum(m1, m2)
        w1, w2 = l1 * jnp.exp(m1 - top), l2 * jnp.exp(m2 - top)
        return top, w1 + w2, w1, w2

    def spread(x):
        return jnp.concatenate([jnp.broadcast_to(x[a : a + 1], (HD, T)) for a in range(3)], axis=0)

    def join(o1, s1, o2, s2):
        top, tot, w1, w2 = weights(s1[0:3], s1[3:6], s2[0:3], s2[3:6])
        o = o1 * spread(w1 / tot) + o2 * spread(w2 / tot)
        return o, jnp.concatenate([top, tot, jnp.zeros((2, T), F32)], axis=0)

    def attend(i, zz):
        for g in range(4):
            QU[g] = QA[zz, :, W * g : W * g + W]

        def group(g, carry):
            qg, kg = QU[g], KP[zz, g]
            outs, tops, tots = [], [], []
            for a in range(3):
                mine = (lane >= HD * a) & (lane < HD * a + HD)
                qm = jnp.concatenate([jnp.where(mine, qg, zero), qaug], axis=1)
                s = nt(kg, qm)
                m = jnp.max(s, axis=0, keepdims=True)
                ex = jnp.exp(s - m)
                l = jnp.sum(ex, axis=0, keepdims=True)
                o = nn(VT[zz, g, HD * a : HD * a + HD, :], ex.astype(BF))
                outs.append(o / l)
                tops.append(m)
                tots.append(l)
            gc, gx = g % 2, g // 2
            OS[i, gc, gx] = jnp.concatenate(outs, axis=0).astype(BF)
            ST[i, gc, gx] = jnp.concatenate(tops + tots + [jnp.zeros((2, T), F32)], axis=0)
            return carry

        lax.fori_loop(0, 4, group, 0)

    q_core, q_x, q_z = {}, {}, {}

    def core_stage(i):
        q_core[i] = (net.send(OS.at[i, 1 - hc], OC.at[i], head=h ^ 1), net.send(ST.at[i, 1 - hc], SC.at[i], head=h ^ 1))

    def x_stage(i):
        for c in q_core[i]:
            c.wait_recv()
        o, s = join(OS[i, hc, 1 - hx].astype(F32), ST[i, hc, 1 - hx], OC[i, 1 - hx].astype(F32), SC[i, 1 - hx])
        OXS[i] = o.astype(BF)
        SXS[i] = s
        q_x[i] = (net.send(OXS.at[i], OX.at[i], head=h ^ 2), net.send(SXS.at[i], SX.at[i], head=h ^ 2))
        o, s = join(OS[i, hc, hx].astype(F32), ST[i, hc, hx], OC[i, hx].astype(F32), SC[i, hx])
        OWN[i] = o
        SOWN[i] = s

    def z_stage(i):
        for c in q_x[i]:
            c.wait_recv()
        o, s = join(OWN[i], SOWN[i], OX[i].astype(F32), SX[i])
        if i < 3:
            m = ORDER[i]
            OZS[i] = o.astype(BF)
            SZS[i] = s
            to = lax.rem(z - m + 4, 4)
            q_z[i] = (net.send(OZS.at[i], OZ.at[i], psg=to), net.send(SZS.at[i], SZ.at[i], psg=to))
        else:
            OWN[i] = o
            SOWN[i] = s

    for i, m in enumerate(ORDER):
        zz = lax.rem(z - m + 4, 4)
        spreadq.ready(m)
        attend(i, zz)
        if i < 2:
            wc.step(("y", "x")[i])
        core_stage(i)
        if i >= 1:
            x_stage(i - 1)
        if i >= 2:
            z_stage(i - 2)
    x_stage(3)
    z_stage(2)
    z_stage(3)
    o, s = OWN[3], SOWN[3]
    for i in range(3):
        for c in q_z[i]:
            c.wait_recv()
        o, s = join(o, s, OZ[i].astype(F32), SZ[i])
    lse = s[0:3] + jnp.log(s[3:6])
    full = jnp.concatenate([o, lse, jnp.zeros((AUG - 3, T), F32)], axis=0)
    ATS[...] = full.T
    ATO[...] = ATS[:, 0:W].astype(BF)
    for c in n2c:
        c.wait_recv()
    at = [net.send(ATS.at[pl.ds(pl.multiple_of(R * (h ^ m), R), R)], AT.at[h], head=h ^ m) for m in (1, 2, 3)]
    AT[h] = ATS[mine_rows, :]
    wc.step("c")
    for c in at:
        c.wait_recv()
    second = FIRST[...]
    for g in range(4):
        low = AT[g, :, 0:W].astype(BF)
        second += nt(low, part(FC, g))
    g2gain = gains[2:3].astype(F32)
    N3[mine_rows, :] = rms_norm(second, g2gain).astype(BF)
    n3c = [net.send(N3.at[mine_rows], N3.at[mine_rows], head=h ^ m) for m in (2, 3, 1)]
    rowid = iota((T, 1), 0)
    go_low = jnp.where(rowid < tlen[0], cot[...], jnp.zeros((T, D), BF))
    wg.step("y")
    for c in n3c:
        c.wait_recv()
    wdown = GG[:, :, :, :, 2 * F : 3 * F].reshape(D, F)
    wgu = GG[:, :, :, :, 0 : 2 * F].reshape(D, 2 * F)
    d_act = nn(go_low, wdown)
    n3 = N3[...]
    gate_up = nn(n3, wgu)
    gate, up = gate_up[:, :F], gate_up[:, F:]
    c0 = 0.7978845608028654
    inner = c0 * (gate + 0.044715 * gate * gate * gate)
    th = jnp.tanh(inner)
    gel = 0.5 * gate * (1.0 + th)
    act = (gel * up).astype(BF)
    dgel = 0.5 * (1.0 + th) + 0.5 * gate * (1.0 - th * th) * (c0 * (1.0 + 3 * 0.044715 * gate * gate))
    dgu = jnp.concatenate([d_act * up * dgel, d_act * gel], axis=1).astype(BF)
    R3S[...] = nt(dgu, wgu).astype(BF)
    r3 = [net.send(R3S.at[pl.ds(pl.multiple_of(R * (h ^ m), R), R)], R3.at[h], head=h ^ m) for m in (2, 3, 1)]
    R1S[...] = nt(act, wdown).astype(BF)
    r1 = [net.send(R1S.at[pl.ds(pl.multiple_of(R * (h ^ m), R), R)], R1.at[h], head=h ^ m) for m in (2, 3, 1)]
    R3[h] = R3S[mine_rows, :]
    R1[h] = R1S[mine_rows, :]
    GF[:, :, :, :, 2 * F : 3 * F] = tn(go_low, act).astype(BF).reshape(2, 2, 2, D // 8, F)
    GF[:, :, :, :, 0 : 2 * F] = tn(n3, dgu).astype(BF).reshape(2, 2, 2, D // 8, 2 * F)
    keep_out(GF, GFH)
    for c in r3:
        c.wait_recv()
    dn3 = R3[0].astype(F32) + R3[1].astype(F32) + R3[2].astype(F32) + R3[3].astype(F32)
    live = (iota((R, 1), 0) + R * h) < tlen[0]
    go = jnp.where(live, cot[mine_rows, :].astype(F32), 0.0)
    dv, dg = rms_back(dn3, second, g2gain)
    DG3[...] = jnp.concatenate([dg, jnp.zeros((7, D), F32)], axis=0)
    g2 = go + dv
    G2[...] = g2
    g2_low = g2.astype(BF)
    alane = iota((R, 2 * AUG), 1)
    wl = iota((R, W), 1)
    aug = jnp.zeros((R, 2 * AUG), F32)
    dos = []

    def parts(x):
        hi_ = x.astype(BF).astype(F32)
        mid = (x - hi_).astype(BF).astype(F32)
        return hi_, mid, x - hi_ - mid

    for g in range(4):
        do = nn(g2_low, part(FC, g)).astype(BF)
        dos.append(do.astype(F32))
        prod = do.astype(F32) * AT[g, :, 0:W]
        for a in range(3):
            delta = jnp.sum(jnp.where((wl >= HD * a) & (wl < HD * a + HD), prod, 0.0), axis=1, keepdims=True)
            for off, val in ((0, AT[g, :, W + a : W + a + 1]), (AUG, delta)):
                for j, piece in enumerate(parts(val)):
                    aug = jnp.where(alane == off + 9 * g + 3 * a + j, piece, aug)
    DO[...] = jnp.concatenate(dos + [aug], axis=1).astype(BF)
    for c in r1:
        c.wait_recv()
    out = second + R1[0].astype(F32) + R1[1].astype(F32) + R1[2].astype(F32) + R1[3].astype(F32)
    OUT[...] = jnp.where(live, out, 0.0)
    for c in kept:
        c.wait()
    net.finish()


def call_one(plen, tlen, table, hid, enc, buckets, gains, mats, cot):
    T, D = hid.shape
    R = T // 4
    W = 3 * HD
    rows = mats[0].shape[0]
    F = mats[8].shape[1] // 4
    tok = -(-enc.shape[1] // 128) * 128
    S = jax.ShapeDtypeStruct
    blk = 4 * rows
    big = dict(
        FA=((2, 2, 2, 2, 2, blk, 2 * W), BF), FK=((2, 2, 2, 2, 2, blk, 2 * W), BF), FC=((2, 2, 2, 2, 2, blk, W), BF),
        GQ=((2, 2, 2, blk, 3 * W), BF),
        KP=((4, 4, tok, W + AUG), BF), VP=((4, 4, tok, W + AUG), BF), KT=((4, 4, W, tok), BF),
        ET=((4, D, tok), BF), PS=((3, T, T), F32),
        GF=((2, 2, 2, blk, 3 * F), BF),
    )
    order = list(big)
    outs = {n: big[n] for n in order[:2] + order[3:9]}
    outs.update(
        QA=((4, T, D), BF), QKV=((T, 3 * W), BF), AO=((T, W), BF), FIRST=((R, D), F32),
        G2=((R, D), F32), DO=((R, D + 2 * AUG), BF),
        GF=big["GF"], DG3=((8, D), F32), OUT=((R, D), F32), N2=((T, D), BF), ATO=((T, W), BF),
    )
    pack = [VMEM((4, rows, w), BF) for w in (3 * W, 2 * W, 2 * W, W, 3 * F)]
    scratch = pack + pack + [
        *[VMEM(*big[n]) for n in order[:4]], VMEM((2, 2, 2, blk, 3 * F), BF),
        *[VMEM(*big[n]) for n in order[4:7]], VMEM((4, 4, W, tok), BF),
        *[VMEM(*big[n]) for n in order[7:9]], VMEM((4, R, W), BF), VMEM(*big["GF"]),
        VMEM((enc.shape[0], tok, D), BF), VMEM((4, T, W), BF), VMEM((3, T, T), F32),
        VMEM((4, 2, 2, W, T), BF), VMEM((4, 2, 2, 8, T), F32),
        VMEM((4, 2, W, T), BF), VMEM((4, 2, 8, T), F32),
        VMEM((4, W, T), BF), VMEM((4, 8, T), F32), VMEM((4, W, T), BF), VMEM((4, 8, T), F32),
        VMEM((3, W, T), BF), VMEM((3, 8, T), F32), VMEM((3, W, T), BF), VMEM((3, 8, T), F32),
        VMEM((4, W, T), F32), VMEM((4, 8, T), F32),
        VMEM((T, W + AUG), F32), VMEM((4, R, W + AUG), F32), VMEM((T, D), BF),
        VMEM((T, D), BF), VMEM((4, R, D), BF), VMEM((T, D), BF), VMEM((4, R, D), BF),
        VMEM((3 * T, W + AUG), BF),
        pltpu.SemaphoreType.DMA((160,)), pltpu.SemaphoreType.DMA((160,)), pltpu.SemaphoreType.DMA((12,)),
    ]
    smem = pl.BlockSpec(memory_space=pltpu.SMEM)
    vm = pl.BlockSpec(memory_space=pltpu.VMEM)
    anym = pl.BlockSpec(memory_space=pl.ANY)
    res = pl.pallas_call(
        kernel_one,
        out_shape=[S(*v) for v in outs.values()],
        in_specs=[smem] * 2 + [vm] * 2 + [anym] + [vm] * 14,
        out_specs=[anym if n in big else vm for n in outs],
        scratch_shapes=scratch,
        name="forward",
        compiler_params=pltpu.CompilerParams(collective_id=1, has_side_effects=True, vmem_limit_bytes=63 << 20),
    )(plen, tlen, table, hid, enc, buckets, gains, *mats, cot)
    return dict(zip(outs, res)), big


def kernel_two(
    buckets, gains, hid, ETH, FAH, FKH, GQH, QA, KPH, VPH, KTH, PSH, QKV, AOO, FIRST, G2, DO, GFH, DG3, OUTR, N2, ATO,
    DENC, DHID, OUT, SM, OF, OC, OK, OA, OL,
    DOB, KP, VP, KT, QAV, ET, FA, FK, GQ, PS,
    QU, DU, QX, DX, QM, DM, DS, PB, DQG, DKV, DQS, DQC, DXR, DOWN, DZS, DZR, DAS, DA, DSF, TBL, NS, NR, DEN,
    FSRC, F1, F2, F3, FTOT, CSRC, C1, C2, C3, CTOT,
    KSRC, K1, K2, K3, K4, K5, KTOT, ASRC, A1, A2, A3, ATOT,
    LSRC, L1, L2, L3, LTOT,
    SMR, DQL, DQO, G1A, G2A,
    ss, rs, ls, es,
):
    d, z, h = enter()
    net = Net(ss, rs)
    T, D = hid.shape
    R = T // 4
    W = 3 * HD
    hc, hx = h % 2, h // 2
    tok = ETH.shape[2]
    mine_rows = pl.ds(pl.multiple_of(R * h, R), R)

    def source(m):
        return lax.rem(z - m + 4, 4)

    def load(pairs, sem):
        cs = [pltpu.make_async_copy(a, b, sem(j)) for j, (a, b) in enumerate(pairs)]
        for c in cs:
            c.start()
        return cs

    def fetch(i):
        zz, slot = source(ORDER[i]), i % 2
        return load(
            [(a.at[zz], b.at[slot]) for a, b in ((KPH, KP), (VPH, VP), (KTH, KT), (QA, QAV))],
            lambda j: ls.at[j, slot],
        )

    DOB[z, mine_rows, :] = DO[...]
    gather = Gather(net, DOB, z, h, R)
    fetched = fetch(0)
    G2A[mine_rows, :] = G2[...].astype(BF)
    near = load([(GFH, FSRC)], lambda j: es.at[j])
    full, own = tuple("cxyab"), tuple("yab")
    sf = Halving(net, FSRC, own, tuple("yab"), (F1, F2, F3), FTOT, OF)
    sc = Halving(net, CSRC, own, tuple("yab"), (C1, C2, C3), CTOT, OC)
    sk = Halving(net, KSRC, full, tuple("cxyab"), (K1, K2, K3, K4, K5), KTOT, OK)
    sa = Halving(net, ASRC, own, tuple("yab"), (A1, A2, A3), ATOT, OA)
    sl = Halving(net, LSRC, own, tuple("yab"), (L1, L2, L3), LTOT, OL)
    weights = load([(FAH, FA), (FKH, FK), (GQH, GQ), (PSH, PS)], lambda j: es.at[2 + j])
    gather.relay()
    g2c = [net.send(G2A.at[mine_rows], G2A.at[mine_rows], head=h ^ m) for m in (2, 3, 1)]
    OUT[mine_rows, :] = OUTR[...]
    for c in near:
        c.wait()

    lane = iota((T, W), 1)
    alane = iota((T, AUG), 1)
    zero = jnp.zeros((T, W), BF)
    azero = jnp.zeros((T, AUG), BF)
    one = jnp.ones((T, 1), F32)
    pad = jnp.zeros((T, AUG - 10), F32)

    def mine_of(a):
        return (lane >= HD * a) & (lane < HD * a + HD)

    def part(ref, g, i=None):
        blk = ref[g % 2, g // 2] if i is None else ref[g % 2, g // 2, :, :, :, :, W * i : W * i + W]
        return blk.reshape(D, blk.shape[-1])

    half = tok // 2

    def attend(i, zz):
        slot = i % 2
        ex = DOB[zz, :, D : D + 2 * AUG].astype(F32)
        for g in range(4):
            QU[g] = QAV[slot, :, W * g : W * g + W]
            DU[g] = DOB[zz, :, W * g : W * g + W]
            QX[g] = jnp.concatenate([ex[:, 9 * g : 9 * g + 9], one, pad], axis=1).astype(BF)
            DX[g] = jnp.concatenate([ex[:, AUG + 9 * g : AUG + 9 * g + 9], one * 0, pad], axis=1).astype(BF)

        def group(g, carry):
            for a in range(3):
                keep = (alane == 9) | ((alane >= 3 * a) & (alane < 3 * a + 3))
                QM[T * a : T * a + T] = jnp.concatenate([jnp.where(mine_of(a), QU[g], zero), jnp.where(keep, QX[g], azero)], axis=1)
                DM[T * a : T * a + T] = jnp.concatenate([jnp.where(mine_of(a), DU[g], zero), jnp.where(keep, DX[g], azero)], axis=1)
            for t in range(0, tok, half):
                kg, vg = KP[slot, g, t : t + half], VP[slot, g, t : t + half]
                for a in range(3):
                    p = jnp.exp(nt(kg, QM[T * a : T * a + T]))
                    ds = p * nt(vg, DM[T * a : T * a + T])
                    DS[t : t + half, T * a : T * a + T] = ds.astype(BF)
                    PB[t : t + half, T * a : T * a + T] = p.astype(BF)
            dk = nn(DS[...], QM[...])
            dv = nn(PB[...], DM[...])
            DKV[zz, g] = jnp.concatenate([dk[:, :W], dv[:, :W]], axis=1).astype(BF)
            dqs = [nn(KT[slot, g, HD * a : HD * a + HD, :], DS[:, T * a : T * a + T]) for a in range(3)]
            DQG[g] = jnp.concatenate(dqs, axis=0).T.astype(BF)
            return carry

        lax.fori_loop(0, 4, group, 0)
        dq = jnp.concatenate([DQG[g] for g in range(4)], axis=1)
        for j in range(4):
            DQS[i, j % 2, j // 2] = dq[R * j : R * j + R]

    q_core, q_x, q_z = {}, {}, {}

    def core_stage(i):
        q_core[i] = net.send(DQS.at[i, 1 - hc], DQC.at[i], head=h ^ 1)

    def x_stage(i):
        q_core[i].wait_recv()
        DQC[i, 1 - hx] = (DQS[i, hc, 1 - hx].astype(F32) + DQC[i, 1 - hx].astype(F32)).astype(BF)
        q_x[i] = net.send(DQC.at[i, 1 - hx], DXR.at[i], head=h ^ 2)
        DOWN[i] = DQS[i, hc, hx].astype(F32) + DQC[i, hx].astype(F32)

    def z_stage(i):
        q_x[i].wait_recv()
        o = DOWN[i] + DXR[i].astype(F32)
        if i < 3:
            DZS[i] = o.astype(BF)
            q_z[i] = net.send(DZS.at[i], DZR.at[i], psg=source(ORDER[i]))
        else:
            DOWN[i] = o

    for i, m in enumerate(ORDER):
        gather.ready(m)
        for c in fetched:
            c.wait()
        if i < 3:
            fetched = fetch(i + 1)
        attend(i, source(m))
        core_stage(i)
        if i >= 1:
            x_stage(i - 1)
        if i >= 2:
            z_stage(i - 2)
        if i == 0:
            for c in g2c:
                c.wait_recv()
            CSRC[...] = tn(G2A[...], ATO[...]).astype(BF).reshape(CSRC.shape)
            sf.push()
            sc.push()
    x_stage(3)
    z_stage(2)
    z_stage(3)
    sf.pull()
    sc.pull()

    def et_copy(n):
        return pltpu.make_async_copy(ETH.at[n % 4], ET.at[n % 2], ls.at[4, n % 2])

    et_copy(0).start()
    for c in weights:
        c.wait()
    dq = DOWN[3]
    for i in range(3):
        q_z[i].wait_recv()
        dq += DZR[i].astype(F32)
    dq_low = dq.astype(BF)

    first = FIRST[...]
    gain = gains[1:2].astype(F32)
    dn2 = jnp.zeros((R, D), F32)
    for g in range(4):
        dn2 += nt(dq_low[:, W * g : W * g + W], part(FA, g, 1))
    dv, dg2 = rms_back(dn2, first, gain)
    g1 = G2[...] + dv
    g1_low = g1.astype(BF)
    G1A[mine_rows, :] = g1_low
    for g in range(4):
        DQL[g] = dq_low[:, W * g : W * g + W]
    for g in range(4):
        DAS[g] = nn(g1_low, part(FA, g, 0)).astype(BF)
    das = [net.send(DAS.at[h ^ m], DA.at[h], head=h ^ m) for m in (2, 3, 1)]
    DA[h] = DAS[h]
    dql = [net.send(DQL.at[h ^ m], DQO.at[h], head=h ^ m) for m in (2, 3, 1)]
    DQO[h] = DQL[h]
    dql += [net.send(G1A.at[mine_rows], G1A.at[mine_rows], head=h ^ m) for m in (2, 3, 1)]

    def whole_grads(g, carry):
        acc = jnp.zeros((D, 2 * W), F32)
        for q in range(4):
            et_copy(4 * g + q).wait()

            @pl.when(4 * g + q < 15)
            def _():
                et_copy(4 * g + q + 1).start()

            acc += nn(ET[q % 2], DKV[q, g])
        gc, gx = g % 2, g // 2
        KSRC[gc, gx] = acc.astype(BF).reshape(2, 2, 2, D // 8, 2 * W)
        return carry

    lax.fori_loop(0, 4, whole_grads, 0)
    sk.push()
    for c in dql:
        c.wait_recv()
    rest = [tn(N2[...], DQO[...].reshape(T, W)), tn(G1A[...], AOO[...])]
    ASRC[...] = jnp.concatenate(rest, axis=1).astype(BF).reshape(ASRC.shape)
    sa.push()
    for c in das:
        c.wait_recv()

    da = DA[...].reshape(T, W)
    qs, ks, vs = QKV[:, 0:W], QKV[:, W : 2 * W], QKV[:, 2 * W : 3 * W]
    dq1 = jnp.zeros((T, W), F32)
    dk1 = jnp.zeros((T, W), F32)
    dv1 = jnp.zeros((T, W), F32)
    for a in range(3):
        mine = mine_of(a)
        dam = jnp.where(mine, da, zero)
        p = PS[a]
        dp = nt(dam, vs)
        ds = p * (dp - jnp.sum(p * dp, axis=-1, keepdims=True))
        DSF[a] = ds
        dsl = ds.astype(BF)
        dq1 += nn(dsl, jnp.where(mine, ks, zero))
        dk1 += tn(dsl, jnp.where(mine, qs, zero))
        dv1 += tn(p.astype(BF), dam)
    dqkv = jnp.concatenate([dq1, dk1, dv1], axis=1).astype(BF)
    wqkv = GQ[...].reshape(D, 3 * W)
    NS[...] = nt(dqkv, wqkv).astype(BF)
    nr = [net.send(NS.at[pl.ds(pl.multiple_of(R * (h ^ m), R), R)], NR.at[h], head=h ^ m) for m in (2, 3, 1)]
    NR[h] = NS[mine_rows, :]
    sk.pull()
    sa.pull()
    g0 = gains[0:1].astype(F32)
    n1 = rms_norm(hid[...].astype(F32), g0).astype(BF)
    LSRC[...] = tn(n1, dqkv).astype(BF).reshape(LSRC.shape)
    sl.push()

    step = DEN.shape[1]
    per = DENC.shape[1] // step

    def den_copy(n):
        rows = pl.ds(pl.multiple_of(lax.rem(n, per) * step, step), step)
        return pltpu.make_async_copy(DEN.at[lax.rem(n, 2)], DENC.at[n // per, rows], es.at[lax.rem(n, 2)])

    def denc(n, carry):
        rows = pl.ds(pl.multiple_of(lax.rem(n, per) * step, step), step)

        @pl.when(n >= 2)
        def _():
            den_copy(n - 2).wait()

        acc = nt(DKV[n // per, 0, rows, :], part(FK, 0))
        for g in range(1, 4):
            acc += nt(DKV[n // per, g, rows, :], part(FK, g))
        DEN[lax.rem(n, 2)] = acc
        den_copy(n).start()
        return carry

    def dencs(a, b):
        lax.fori_loop(a, b, denc, 0)

    dencs(0, 1)
    sf.pull()
    sc.pull()
    dencs(1, 2)
    for c in nr:
        c.wait_recv()
    dn1 = NR[0].astype(F32) + NR[1].astype(F32) + NR[2].astype(F32) + NR[3].astype(F32)
    dv, dg1 = rms_back(dn1, hid[mine_rows, :].astype(F32), g0)
    DHID[mine_rows, :] = g1 + dv
    dh = [net.send(DHID.at[mine_rows], DHID.at[mine_rows], head=h ^ m) for m in (2, 3, 1)]
    dh += [net.send(OUT.at[mine_rows], OUT.at[mine_rows], head=h ^ m) for m in (2, 3, 1)]

    sl.pull()
    sa.pull()
    sk.pull()

    bk = buckets[...]

    def table_step(i, carry):
        hit = bk == i
        for a in range(3):
            TBL[a, pl.ds(i, 1), :] = jnp.sum(jnp.where(hit, DSF[a], 0.0), axis=0, keepdims=True)
        return carry

    nb = TBL.shape[1]
    lax.fori_loop(0, nb, table_step, 0)
    tl = iota((nb, 128), 1)
    tab = jnp.zeros((nb, 128), F32)
    for a in range(3):
        tab = jnp.where(tl == a, jnp.sum(TBL[a], axis=1, keepdims=True), tab)
    tab = jnp.concatenate([tab, jnp.zeros((128 - nb, 128), F32)], axis=0).T[0:8]
    tab = jnp.concatenate([tab, jnp.zeros((8, D - 128), F32)], axis=1)
    dgs = jnp.concatenate([dg1, dg2, DG3[0:1], jnp.zeros((5, D), F32)], axis=0)
    SM[0] = jnp.concatenate([dgs, tab], axis=0)
    srow = iota((16, D), 0)

    def small(j, **dev):
        return net.send(SM.at[j], SMR.at[j], **dev)

    def small_end(j, c, shared):
        c.wait_recv()
        got = SMR[j]
        SM[j + 1] = SM[j] + (got if shared else jnp.where(srow < 8, got, 0.0))

    c = small(0, head=h ^ 1)
    sf.pull()
    sc.pull()
    small_end(0, c, False)
    c = small(1, head=h ^ 2)
    dencs(2, 4)
    sl.pull()
    sa.pull()
    sk.pull()
    small_end(1, c, False)
    c = small(2, dp=1 - d)
    dencs(4, 5)
    small_end(2, c, True)
    c = small(3, psg=z ^ 1)
    sl.pull()
    sk.pull()
    dencs(5, 6)
    small_end(3, c, True)
    c = small(4, psg=z ^ 2)
    sk.pull()
    dencs(6, 4 * per)
    small_end(4, c, True)
    for n in (4 * per - 2, 4 * per - 1):
        den_copy(n).wait()
    for s in (sf, sc, sk, sa, sl):
        s.done()
    for c in dh:
        c.wait_recv()
    net.finish()


def call_two(buckets, gains, hid, kept, big, rows, count):
    T, D = hid.shape
    R = T // 4
    W = 3 * HD
    k = kept
    tok = k["ET"].shape[2]
    F3 = k["GF"].shape[4]
    S = jax.ShapeDtypeStruct
    blk = D // 8
    outs = dict(
        DENC=((4, count, D), F32), DHID=((T, D), F32), OUT=((T, D), F32), SM=((6, 16, D), F32),
        OF=((4, rows, F3), F32), OC=((4, rows, W), F32), OK=((4, rows, 2 * W), F32), OA=((4, rows, 2 * W), F32),
        OL=((4, rows, 3 * W), F32),
    )

    def halving(n, w):
        return [VMEM((2,) * k + (blk, w), BF) for k in (n, *range(n - 1, -1, -1))] + [VMEM((blk, w), F32)]

    def like(n, *lead):
        return VMEM((*lead, *k[n].shape[1:]) if lead else k[n].shape, k[n].dtype)

    scratch = [
        VMEM((4, T, D + 2 * AUG), BF), like("KP", 2), like("VP", 2), like("KT", 2), like("QA", 2), like("ET", 2),
        like("FA"), like("FK"), like("GQ"), like("PS"),
        VMEM((4, T, W), BF), VMEM((4, T, W), BF), VMEM((4, T, AUG), BF), VMEM((4, T, AUG), BF),
        VMEM((3 * T, W + AUG), BF), VMEM((3 * T, W + AUG), BF), VMEM((tok, 3 * T), BF), VMEM((tok, 3 * T), BF),
        VMEM((4, T, W), BF), VMEM((4, 4, tok, 2 * W), BF),
        VMEM((4, 2, 2, R, D), BF), VMEM((4, 2, R, D), BF), VMEM((4, R, D), BF), VMEM((4, R, D), F32),
        VMEM((3, R, D), BF), VMEM((3, R, D), BF), VMEM((4, R, W), BF), VMEM((4, R, W), BF),
        VMEM((3, T, T), F32), VMEM((3, 32, T), F32), VMEM((T, D), BF), VMEM((4, R, D), BF), VMEM((2, count // 2, D), F32),
        *halving(3, F3), *halving(3, W), *halving(5, 2 * W), *halving(3, 2 * W), *halving(3, 3 * W),
        VMEM((5, 16, D), F32), VMEM((4, R, W), BF), VMEM((4, R, W), BF), VMEM((T, D), BF), VMEM((T, D), BF),
        pltpu.SemaphoreType.DMA((120,)), pltpu.SemaphoreType.DMA((120,)), pltpu.SemaphoreType.DMA((5, 2)), pltpu.SemaphoreType.DMA((6,)),
    ]
    vm = pl.BlockSpec(memory_space=pltpu.VMEM)
    anym = pl.BlockSpec(memory_space=pl.ANY)
    far = set(big) | {"QA"}
    ordered = dict(ET=0, FA=0, FK=0, GQ=0, QA=0, KP=0, VP=0, KT=0, PS=0)
    names = [*ordered, *[n for n in k if n not in ordered]]
    res = pl.pallas_call(
        kernel_two,
        out_shape=[S(*v) for v in outs.values()],
        in_specs=[vm] * 3 + [anym if n in far else vm for n in names],
        out_specs=[anym] + [vm] * (len(outs) - 1),
        scratch_shapes=scratch,
        name="backward",
        compiler_params=pltpu.CompilerParams(collective_id=2, has_side_effects=True, vmem_limit_bytes=63 << 20),
    )(buckets, gains, hid, *[k[n] for n in names])
    return dict(zip(outs, res))


def local_fast(
    hidden_in, encodings, passage_lengths, target_lengths, rel_buckets, gains, rel_table, *rest
):
    mats, cot = rest[:11], rest[11]
    span, passages, group, D = encodings.shape
    rows = mats[0].shape[0]
    W = 3 * HD
    F = mats[8].shape[1] // 4
    count = span * passages
    enc = jnp.transpose(encodings, (2, 1, 0, 3)).reshape(group, count, D)
    hid = hidden_in[0]
    kept, big = call_one(
        passage_lengths.T, target_lengths, rel_table.T, hid, enc, rel_buckets, gains, mats, cot[0]
    )
    r = call_two(rel_buckets, gains, hid, kept, big, rows, count)
    d_enc = jnp.transpose(r["DENC"].reshape(group, passages, span, D), (2, 1, 0, 3))

    last = call_three(r, W, F, rel_table.shape[0])
    out, dhid, d_gains, d_table, *grads = last
    return (out[None], dhid[None], d_enc, d_gains, d_table.T, *grads)


def kernel_three(W, F, OUT, DHID, SM, OF, OC, OK, OA, OL, out, dhid, gains, table, sq, sk, sv, so, cq, ck, cv, co, fg, fu, fd):
    out[...] = OUT[...]
    dhid[...] = DHID[...]
    gains[...] = SM[5, 0:3, :]
    table[...] = SM[5, 8:11, 0 : table.shape[1]]
    for dst, src, i, w in (
        (sq, OL, 0, W), (sk, OL, 1, W), (sv, OL, 2, W), (so, OA, 1, W), (cq, OA, 0, W),
        (ck, OK, 0, W), (cv, OK, 1, W), (co, OC, 0, W), (fg, OF, 0, F), (fu, OF, 1, F), (fd, OF, 2, F),
    ):
        dst[...] = jnp.concatenate([src[j, :, w * i : w * i + w] for j in range(4)], axis=1)


def call_three(r, W, F, nb):
    S = jax.ShapeDtypeStruct
    DENC, DHID, OUT, SM, OF, OC, OK, OA, OL = r.values()
    T, D = OUT.shape
    rows = OF.shape[1]
    outs = [(T, D), (T, D), (3, D), (3, nb)] + [(rows, 4 * W)] * 8 + [(rows, 4 * F)] * 3
    vm = pl.BlockSpec(memory_space=pltpu.VMEM)
    res = pl.pallas_call(
        functools.partial(kernel_three, W, F),
        out_shape=[S(v, F32) for v in outs],
        in_specs=[vm] * 8,
        out_specs=[vm] * len(outs),
        name="columns",
        compiler_params=pltpu.CompilerParams(vmem_limit_bytes=62 << 20),
    )(OUT, DHID, SM, OF, OC, OK, OA, OL)
    return res


def merged(part, axis, combine):
    gathered = jax.tree.map(lambda a: lax.all_gather(a, axis), part)

    def take(source):
        return jax.tree.map(lambda a: lax.dynamic_index_in_dim(a, source, 0, False), gathered)

    return lax.fori_loop(
        1, lax.axis_size(axis), lambda source, state: combine(state, take(source)), take(0)
    )


def rms_plain(values, gain):
    return values * lax.rsqrt(jnp.mean(values * values, axis=-1, keepdims=True) + EPSILON) * gain


def gated(gate_in, up_in):
    return jax.nn.gelu(gate_in, approximate=True) * up_in


def over_heads(partial_value):
    return lax.psum(partial_value, "head")


def own_columns(matrix, index, width):
    return lax.dynamic_slice_in_dim(matrix, index * width, width, 1)


def left_mul(left, matrix):
    return jnp.einsum("qtd,dc->qtc", left, matrix, preferred_element_type=jnp.float32)


def right_mul(left, matrix):
    return jnp.einsum("qtc,dc->qtd", left, matrix, preferred_element_type=jnp.float32)


def row_outer(left, right):
    return jnp.einsum("qtd,qtc->dc", left, right, preferred_element_type=jnp.float32)


def local_plain(
    hidden_in,
    encodings,
    passage_lengths,
    target_lengths,
    rel_buckets,
    gains,
    rel_table,
    self_q,
    self_k,
    self_v,
    self_o,
    cross_q,
    cross_k,
    cross_v,
    cross_o,
    ff_gate,
    ff_up,
    ff_down,
    cotangent,
):
    gathered = (
        lax.all_gather(self_q, ("dp", "psg", "head"), axis=0, tiled=True),
        lax.all_gather(self_k, ("dp", "psg", "head"), axis=0, tiled=True),
        lax.all_gather(self_v, ("dp", "psg", "head"), axis=0, tiled=True),
        lax.all_gather(self_o, ("dp", "psg", "head"), axis=0, tiled=True),
        lax.all_gather(cross_q, ("dp", "psg", "head"), axis=0, tiled=True),
        lax.all_gather(cross_k, ("dp", "psg", "head"), axis=0, tiled=True),
        lax.all_gather(cross_v, ("dp", "psg", "head"), axis=0, tiled=True),
        lax.all_gather(cross_o, ("dp", "psg", "head"), axis=0, tiled=True),
        lax.all_gather(ff_gate, ("dp", "psg", "head"), axis=0, tiled=True),
        lax.all_gather(ff_up, ("dp", "psg", "head"), axis=0, tiled=True),
        lax.all_gather(ff_down, ("dp", "psg", "head"), axis=0, tiled=True),
    )
    (
        self_query,
        self_key,
        self_value,
        self_out,
        cross_query,
        cross_key,
        cross_value,
        cross_out,
        gate_full,
        up_full,
        down_full,
    ) = gathered
    head_index = lax.axis_index("head")
    heads_local = rel_table.shape[1]
    width = heads_local * HD
    total_width = self_query.shape[1]
    ff_total = gate_full.shape[1]
    ff_local = ff_total // lax.axis_size("head")
    query_rows = hidden_in.shape[0]
    target_span = hidden_in.shape[1]
    hidden = hidden_in.astype(jnp.float32)
    gain_all = gains.astype(jnp.float32)
    qkv_weight = jnp.concatenate(
        [
            own_columns(self_query, head_index, width),
            own_columns(self_key, head_index, width),
            own_columns(self_value, head_index, width),
        ],
        axis=1,
    )
    normed_one = rms_plain(hidden, gain_all[0]).astype(jnp.bfloat16)
    qkv_self = left_mul(normed_one, qkv_weight).astype(jnp.bfloat16)
    queries_self = qkv_self[..., :width].reshape(query_rows, target_span, heads_local, HD)
    keys_self = qkv_self[..., width : 2 * width].reshape(query_rows, target_span, heads_local, HD)
    values_self = qkv_self[..., 2 * width :].reshape(query_rows, target_span, heads_local, HD)
    positions = jnp.arange(target_span)
    causal = (positions[None, None, :] <= positions[None, :, None]) & (
        positions[None, None, :] < target_lengths[:, None, None]
    )
    buckets_hot = (rel_buckets[:, :, None] == jnp.arange(rel_table.shape[0])[None, None, :]).astype(
        jnp.float32
    )
    bias = jnp.einsum(
        "ijb,bh->hij", buckets_hot, rel_table.astype(jnp.float32), precision=lax.Precision.HIGHEST
    )
    scores_self = jnp.einsum(
        "qihd,qjhd->qhij", queries_self, keys_self, preferred_element_type=jnp.float32
    )
    scores_self = jnp.where(causal[:, None], scores_self + bias[None], NEGATIVE)
    probs_self = jax.nn.softmax(scores_self, axis=-1)
    probs_self_low = probs_self.astype(jnp.bfloat16)
    attn_one = jnp.einsum(
        "qhij,qjhd->qihd", probs_self_low, values_self, preferred_element_type=jnp.float32
    )
    attn_one = attn_one.reshape(query_rows, target_span, width).astype(jnp.bfloat16)
    self_out_own = own_columns(self_out, head_index, width)
    first = hidden + over_heads(right_mul(attn_one, self_out_own))
    normed_two = rms_plain(first, gain_all[1]).astype(jnp.bfloat16)
    cross_query_own = own_columns(cross_query, head_index, width)
    query_cross = left_mul(normed_two, cross_query_own).astype(jnp.bfloat16)
    query_group = lax.all_gather(query_cross, "psg", axis=0, tiled=True)
    group_count = query_group.shape[0]
    head_parts = lax.axis_size("head")
    kv_split = jnp.concatenate(
        [
            cross_key.reshape(cross_key.shape[0], head_parts, width),
            cross_value.reshape(cross_value.shape[0], head_parts, width),
        ],
        axis=2,
    )
    local_kv = jnp.einsum(
        "tpqd,dgc->qptgc", encodings, kv_split, preferred_element_type=jnp.float32
    ).astype(jnp.bfloat16)
    moved_kv = lax.all_to_all(local_kv, "head", split_axis=3, concat_axis=2, tiled=True)
    key_value = moved_kv.reshape(moved_kv.shape[0], moved_kv.shape[1], moved_kv.shape[2], 2 * width)
    passages_local = key_value.shape[1]
    passage_span = key_value.shape[2]
    key_count = passages_local * passage_span
    kv_flat = key_value.reshape(group_count, key_count, 2 * width)
    span = jnp.arange(passage_span)
    key_valid = (span[None, None, :] < jnp.transpose(passage_lengths)[:, :, None]).reshape(
        group_count, key_count
    )

    def masked_scores(query_block, kv_block, valid_block):
        query_heads = query_block.reshape(target_span, heads_local, HD)
        keys_part = kv_block[:, :width].reshape(key_count, heads_local, HD)
        raw = jnp.einsum("ihd,jhd->hij", query_heads, keys_part, preferred_element_type=jnp.float32)
        return jnp.where(valid_block[None, None, :], raw, NEGATIVE)

    def stats_one(item):
        masked = masked_scores(item[0], item[1], item[2])
        largest = jnp.max(masked, axis=-1)
        total = jnp.sum(jnp.exp(masked - largest[..., None]), axis=-1)
        return (largest, total)

    tops, totals = lax.map(stats_one, (query_group, kv_flat, key_valid))

    def combine(pair_one, pair_two):
        larger = jnp.maximum(pair_one[0], pair_two[0])
        return (
            larger,
            pair_one[1] * jnp.exp(pair_one[0] - larger)
            + pair_two[1] * jnp.exp(pair_two[0] - larger),
        )

    tops, totals = merged((tops, totals), "psg", combine)
    log_total = tops + jnp.log(totals)

    def values_one(item):
        masked = masked_scores(item[0], item[1], item[2])
        probs_low = jnp.exp(masked - item[3][..., None]).astype(jnp.bfloat16)
        values_part = item[1][:, width:].reshape(key_count, heads_local, HD)
        weighted = jnp.einsum(
            "hij,jhd->ihd", probs_low, values_part, preferred_element_type=jnp.float32
        )
        return weighted.reshape(target_span, width)

    partial_out = lax.map(values_one, (query_group, kv_flat, key_valid, log_total))
    attn_two = lax.psum_scatter(partial_out, "psg", scatter_dimension=0, tiled=True).astype(
        jnp.bfloat16
    )
    cross_out_own = own_columns(cross_out, head_index, width)
    second = first + over_heads(right_mul(attn_two, cross_out_own))
    normed_three = rms_plain(second, gain_all[2]).astype(jnp.bfloat16)
    ff_weight = jnp.concatenate(
        [own_columns(gate_full, head_index, ff_local), own_columns(up_full, head_index, ff_local)],
        axis=1,
    )
    gate_up = left_mul(normed_three, ff_weight)
    gate_part = gate_up[..., :ff_local]
    up_part = gate_up[..., ff_local:]
    activated = gated(gate_part, up_part).astype(jnp.bfloat16)
    down_own = own_columns(down_full, head_index, ff_local)
    output = second + over_heads(right_mul(activated, down_own))
    row_valid = (positions[None, :] < target_lengths[:, None])[:, :, None]
    out_hidden = jnp.where(row_valid, output, 0.0)
    grad_out = jnp.where(row_valid, cotangent.astype(jnp.float32), 0.0)
    grad_out_low = grad_out.astype(jnp.bfloat16)
    grad_down = row_outer(grad_out_low, activated)
    grad_act = left_mul(grad_out_low, down_own)
    gate_value, pull_gate = jax.vjp(gated, gate_part, up_part)
    grad_gate, grad_up = pull_gate(grad_act)
    grad_gate_up = jnp.concatenate([grad_gate, grad_up], axis=-1).astype(jnp.bfloat16)
    grad_ff_weight = row_outer(normed_three, grad_gate_up)
    grad_normed_three = over_heads(right_mul(grad_gate_up, ff_weight))
    norm_value, pull_three = jax.vjp(rms_plain, second, gain_all[2])
    grad_second_norm, grad_gain_three = pull_three(grad_normed_three)
    grad_two = grad_out + grad_second_norm
    grad_two_low = grad_two.astype(jnp.bfloat16)
    grad_cross_out = row_outer(grad_two_low, attn_two)
    grad_attn_two = left_mul(grad_two_low, cross_out_own).astype(jnp.bfloat16)
    grad_attn_group = lax.all_gather(grad_attn_two, "psg", axis=0, tiled=True)

    def prob_pieces(item):
        masked = masked_scores(item[0], item[1], item[2])
        probs = jnp.exp(masked - item[3][..., None])
        values_part = item[1][:, width:].reshape(key_count, heads_local, HD)
        grad_rows = item[4].reshape(target_span, heads_local, HD)
        grad_probs = jnp.einsum(
            "ihd,jhd->hij", grad_rows, values_part, preferred_element_type=jnp.float32
        )
        return (probs, grad_probs)

    def delta_one(item):
        probs, grad_probs = prob_pieces(item)
        return jnp.sum(probs * grad_probs, axis=-1)

    delta_part = lax.map(delta_one, (query_group, kv_flat, key_valid, log_total, grad_attn_group))
    delta = lax.psum(delta_part, "psg")

    def grads_one(item):
        probs, grad_probs = prob_pieces(item[:5])
        grad_scores = (probs * (grad_probs - item[5][..., None])).astype(jnp.bfloat16)
        probs_low = probs.astype(jnp.bfloat16)
        query_heads = item[0].reshape(target_span, heads_local, HD)
        keys_part = item[1][:, :width].reshape(key_count, heads_local, HD)
        grad_rows = item[4].reshape(target_span, heads_local, HD)
        grad_query = jnp.einsum(
            "hij,jhd->ihd", grad_scores, keys_part, preferred_element_type=jnp.float32
        )
        grad_keys = jnp.einsum(
            "hij,ihd->jhd", grad_scores, query_heads, preferred_element_type=jnp.float32
        )
        grad_values = jnp.einsum(
            "hij,ihd->jhd", probs_low, grad_rows, preferred_element_type=jnp.float32
        )
        grad_kv = jnp.concatenate(
            [grad_keys.reshape(key_count, width), grad_values.reshape(key_count, width)], axis=-1
        ).astype(jnp.bfloat16)
        return (grad_query.reshape(target_span, width), grad_kv)

    grad_query_group, grad_kv_flat = lax.map(
        grads_one, (query_group, kv_flat, key_valid, log_total, grad_attn_group, delta)
    )
    grad_query_cross = lax.psum_scatter(
        grad_query_group, "psg", scatter_dimension=0, tiled=True
    ).astype(jnp.bfloat16)
    grad_cross_query = row_outer(normed_two, grad_query_cross)
    grad_normed_two = over_heads(right_mul(grad_query_cross, cross_query_own))
    norm_value_two, pull_two = jax.vjp(rms_plain, first, gain_all[1])
    grad_first_norm, grad_gain_two = pull_two(grad_normed_two)
    grad_one = grad_two + grad_first_norm
    grad_kv = grad_kv_flat.reshape(group_count, passages_local, passage_span, 2 * width)
    grad_back = lax.all_to_all(
        grad_kv.reshape(group_count, passages_local, passage_span, 1, 2 * width),
        "head",
        split_axis=2,
        concat_axis=3,
        tiled=True,
    )
    d_encodings = jnp.einsum(
        "qptgc,dgc->tpqd", grad_back, kv_split, preferred_element_type=jnp.float32
    )
    grad_split = jnp.einsum(
        "tpqd,qptgc->dgc", encodings, grad_back, preferred_element_type=jnp.float32
    )
    grad_cross_key = grad_split[:, :, :width].reshape(grad_split.shape[0], total_width)
    grad_cross_value = grad_split[:, :, width:].reshape(grad_split.shape[0], total_width)
    grad_one_low = grad_one.astype(jnp.bfloat16)
    grad_self_out = row_outer(grad_one_low, attn_one)
    grad_attn_one = left_mul(grad_one_low, self_out_own).astype(jnp.bfloat16)
    grad_attn_one = grad_attn_one.reshape(query_rows, target_span, heads_local, HD)
    grad_probs_self = jnp.einsum(
        "qihd,qjhd->qhij", grad_attn_one, values_self, preferred_element_type=jnp.float32
    )
    grad_scores_self = probs_self * (
        grad_probs_self - jnp.sum(probs_self * grad_probs_self, axis=-1, keepdims=True)
    )
    grad_table = jnp.einsum(
        "ijb,hij->bh",
        buckets_hot,
        jnp.sum(grad_scores_self, axis=0),
        precision=lax.Precision.HIGHEST,
    )
    grad_scores_low = grad_scores_self.astype(jnp.bfloat16)
    grad_query_self = jnp.einsum(
        "qhij,qjhd->qihd", grad_scores_low, keys_self, preferred_element_type=jnp.float32
    )
    grad_key_self = jnp.einsum(
        "qhij,qihd->qjhd", grad_scores_low, queries_self, preferred_element_type=jnp.float32
    )
    grad_value_self = jnp.einsum(
        "qhij,qihd->qjhd", probs_self_low, grad_attn_one, preferred_element_type=jnp.float32
    )
    grad_qkv = jnp.concatenate(
        [
            grad_query_self.reshape(query_rows, target_span, width),
            grad_key_self.reshape(query_rows, target_span, width),
            grad_value_self.reshape(query_rows, target_span, width),
        ],
        axis=-1,
    ).astype(jnp.bfloat16)
    grad_qkv_weight = row_outer(normed_one, grad_qkv)
    grad_normed_one = over_heads(right_mul(grad_qkv, qkv_weight))
    norm_value_one, pull_one = jax.vjp(rms_plain, hidden, gain_all[0])
    grad_hidden_norm, grad_gain_one = pull_one(grad_normed_one)
    d_hidden = grad_one + grad_hidden_norm
    grad_gains = jnp.stack([grad_gain_one, grad_gain_two, grad_gain_three])
    d_gains, d_rel_table = lax.psum((grad_gains, grad_table), ("dp", "psg"))
    own_grads = [
        grad_qkv_weight[:, :width],
        grad_qkv_weight[:, width : 2 * width],
        grad_qkv_weight[:, 2 * width :],
        grad_self_out,
        grad_cross_query,
        grad_cross_out,
        grad_ff_weight[:, :ff_local],
        grad_ff_weight[:, ff_local:],
        grad_down,
    ]
    row_sums = lax.psum_scatter(tuple(own_grads), ("dp", "psg"), scatter_dimension=0, tiled=True)
    owned = (
        lax.all_to_all(row_sums[0], "head", split_axis=0, concat_axis=1, tiled=True),
        lax.all_to_all(row_sums[1], "head", split_axis=0, concat_axis=1, tiled=True),
        lax.all_to_all(row_sums[2], "head", split_axis=0, concat_axis=1, tiled=True),
        lax.all_to_all(row_sums[3], "head", split_axis=0, concat_axis=1, tiled=True),
        lax.all_to_all(row_sums[4], "head", split_axis=0, concat_axis=1, tiled=True),
        lax.all_to_all(row_sums[5], "head", split_axis=0, concat_axis=1, tiled=True),
        lax.all_to_all(row_sums[6], "head", split_axis=0, concat_axis=1, tiled=True),
        lax.all_to_all(row_sums[7], "head", split_axis=0, concat_axis=1, tiled=True),
        lax.all_to_all(row_sums[8], "head", split_axis=0, concat_axis=1, tiled=True),
    )
    key_done, value_done = (
        lax.psum_scatter(grad_cross_key, ("dp", "psg", "head"), scatter_dimension=0, tiled=True),
        lax.psum_scatter(grad_cross_value, ("dp", "psg", "head"), scatter_dimension=0, tiled=True),
    )
    return (
        out_hidden,
        d_hidden,
        d_encodings,
        d_gains,
        d_rel_table,
        owned[0],
        owned[1],
        owned[2],
        owned[3],
        owned[4],
        key_done,
        value_done,
        owned[5],
        owned[6],
        owned[7],
        owned[8],
    )


PLACED = (
    P(("dp", "psg"), None, None),
    P("head", "psg", "dp", None),
    P("psg", "dp"),
    P(("dp", "psg")),
    P(),
    P(),
    P(None, "head"),
    P(("dp", "psg", "head"), None),
    P(("dp", "psg", "head"), None),
    P(("dp", "psg", "head"), None),
    P(("dp", "psg", "head"), None),
    P(("dp", "psg", "head"), None),
    P(("dp", "psg", "head"), None),
    P(("dp", "psg", "head"), None),
    P(("dp", "psg", "head"), None),
    P(("dp", "psg", "head"), None),
    P(("dp", "psg", "head"), None),
    P(("dp", "psg", "head"), None),
    P(("dp", "psg"), None, None),
)

OUTS = (
    P(("dp", "psg"), None, None),
    P(("dp", "psg"), None, None),
    P("head", "psg", "dp", None),
    P(),
    P(None, "head"),
    P(("dp", "psg", "head"), None),
    P(("dp", "psg", "head"), None),
    P(("dp", "psg", "head"), None),
    P(("dp", "psg", "head"), None),
    P(("dp", "psg", "head"), None),
    P(("dp", "psg", "head"), None),
    P(("dp", "psg", "head"), None),
    P(("dp", "psg", "head"), None),
    P(("dp", "psg", "head"), None),
    P(("dp", "psg", "head"), None),
    P(("dp", "psg", "head"), None),
)


def solution(mesh):
    def local(*args):
        rows, span, heads = args[7].shape[0], args[1].shape[0], args[6].shape[1]
        fits = (mesh.shape["dp"], mesh.shape["psg"], mesh.shape["head"], heads) == (2, 4, 4, 3)
        fits = fits and (4 * rows) % 16 == 0 and rows % 8 == 0
        return (local_fast if fits else local_plain)(*args)

    placed = PLACED
    return jax.shard_map(local, mesh=mesh, in_specs=placed, out_specs=OUTS, check_vma=False)
```
